32 devices in a mesh: dp: 8 (over z, x), seq: 4 (over y, core).
Axes of the slice: x: 2, y: 2, z: 4, core: 2. Of those that a mesh axis runs over, the one named last changes fastest.
Arguments:
- queries: bfloat16 [8, 512, 1024], P('dp', 'seq'), may hold values from -6 to 6
- key_vecs: bfloat16 [8, 512, 1024], P('dp', 'seq'), may hold values from -6 to 6
- value_vecs: bfloat16 [8, 512, 1024], P('dp', 'seq'), may hold values from -6 to 6
- residual_in: bfloat16 [8, 512, 1024], P('dp', 'seq'), may hold values from -8 to 8
- point_weight: bfloat16 [1024, 2048], P('seq'), may hold values from -0.5 to 0.5
- context_grad: bfloat16 [8, 512, 1024], P('dp', 'seq'), may hold values from -6 to 6
- depth_kernel: float32 [31, 1024], replicated, may hold values from -1 to 1
- norm_gain: float32 [1024], replicated, may hold values from 0.5 to 1.5
- norm_bias: float32 [1024], replicated, may hold values from -3 to 3
- conv_grad: bfloat16 [8, 512, 1024], P('dp', 'seq'), may hold values from -1.5 to 1.5
Outputs:
- context: bfloat16 [8, 512, 1024], P('dp', 'seq')
- conv_output: bfloat16 [8, 512, 1024], P('dp', 'seq')
- query_grad: bfloat16 [8, 512, 1024], P('dp', 'seq')
- key_grad: bfloat16 [8, 512, 1024], P('dp', 'seq')
- value_grad: bfloat16 [8, 512, 1024], P('dp', 'seq')
- input_grad: bfloat16 [8, 512, 2048], P('dp', 'seq')
- residual_grad: bfloat16 [8, 512, 1024], P('dp', 'seq')
- kernel_grad: float32 [31, 1024], replicated
- gain_grad: float32 [1024], replicated
- bias_grad: float32 [1024], replicated
The draws below stay inside these ranges and needn't reach their ends.
All inputs are finite; a program needn't handle non-finite values.
Results may differ from the reference program's by a relative error of at most 0.0049.
The reference program's roundings to bfloat16 on the way count: a program that leaves them out, or rounds other values in their place, can miss the bound.
Values may be sent and summed in bfloat16 or wider, within the bound.
A program may use at most 64 MiB of HBM per device.

```python
import math
import jax
import jax.numpy as jnp
from jax import lax

D = 1024
HEADS = 16
KERNEL = 31
HD = 64
FRAMES = 512
RECS = 8


def drawn_pair(key):
    query_key = jax.random.fold_in(key, 101)
    keys_key = jax.random.fold_in(key, 102)
    full_shape = (RECS, FRAMES, D)
    query_base = jnp.clip(jax.random.normal(query_key, full_shape, jnp.float32), -4.0, 4.0)
    key_base = jnp.clip(jax.random.normal(keys_key, full_shape, jnp.float32), -4.0, 4.0)
    return (query_base, key_base)


def draw_queries(key, part):
    return drawn_pair(key)[0].astype(jnp.bfloat16)


def draw_key_vecs(key, part):
    return drawn_pair(key)[1].astype(jnp.bfloat16)


def draw_residual_in(key, part):
    full_shape = (RECS, FRAMES, D)
    column_scale = jnp.exp(jax.random.uniform(jax.random.fold_in(key, 201), (1, 1, D), jnp.float32, 0.0, math.log(10.0))) * 0.5
    row_scale = jnp.exp(jax.random.uniform(jax.random.fold_in(key, 202), (RECS, FRAMES, 1), jnp.float32, 0.0, math.log(10.0))) * 0.5
    base_values = jax.random.normal(jax.random.fold_in(key, 203), full_shape, jnp.float32)
    return jnp.clip(base_values * column_scale * row_scale, -8.0, 8.0).astype(jnp.bfloat16)


def draw_point_weight(key, part):
    full_shape = (D, 2 * D)
    column_scale = jnp.exp(jax.random.uniform(jax.random.fold_in(key, 301), (1, 2 * D), jnp.float32, 0.0, math.log(10.0))) * 0.1
    base_values = jnp.clip(jax.random.normal(jax.random.fold_in(key, 302), full_shape, jnp.float32), -4.0, 4.0)
    return jnp.clip(base_values * column_scale * D ** (-0.5), -0.5, 0.5).astype(jnp.bfloat16)


def level_of(own_key, extent, shards, low, high):
    factor_of = 1.0
    for position, parts in shards:
        steps = jax.random.uniform(jax.random.fold_in(jax.random.fold_in(own_key, 6), position), (parts,), jnp.float32, low / len(shards), high / len(shards))
        factor_of = factor_of * jnp.repeat(jnp.exp(steps), extent[position] // parts).reshape((-1,) + (1,) * (len(extent) - 1 - position))
    return factor_of


def centred(rng, shape, width, limit, cuts=(), held_as=jnp.bfloat16):
    level = level_of(rng, shape, cuts, -0.22, 0.18) if cuts else 1.0
    drawn = jax.random.normal(rng, shape, jnp.float32) * width * level
    return jnp.minimum(jnp.maximum(drawn, -limit), limit).astype(held_as)


def setup_inputs(seed: int = 0) -> dict:
    splits = jax.random.split(jax.random.key(seed), 11)
    queries = draw_queries(jax.random.fold_in(splits[10], 71), 0)
    key_vecs = draw_key_vecs(jax.random.fold_in(splits[10], 71), 0)
    value_vecs = centred(splits[2], (RECS, FRAMES, D), 1.0, 6.0, ((0, 8), (1, 4)))
    residual_in = draw_residual_in(jax.random.fold_in(splits[10], 71), 0)
    point_weight = draw_point_weight(jax.random.fold_in(splits[10], 71), 0)
    context_grad = centred(splits[5], (RECS, FRAMES, D), 1.0, 6.0, ((0, 8), (1, 4)))
    depth_kernel = centred(splits[6], (KERNEL, D), KERNEL ** -0.5, 1.0, (), jnp.float32)
    norm_gain = jnp.clip(1.0 + 0.1 * jax.random.normal(splits[7], (D,), jnp.float32), 0.5, 1.5)
    norm_bias = centred(splits[8], (D,), 0.5, 3.0, (), jnp.float32)
    conv_grad = centred(splits[9], (RECS, FRAMES, D), 0.25, 1.5, ((0, 8), (1, 4)))
    return dict(queries=queries, key_vecs=key_vecs, value_vecs=value_vecs, residual_in=residual_in, point_weight=point_weight, context_grad=context_grad, depth_kernel=depth_kernel, norm_gain=norm_gain, norm_bias=norm_bias, conv_grad=conv_grad)


def to_heads(array):
    return array.reshape(RECS, FRAMES, HEADS, HD).transpose(0, 2, 1, 3).reshape(RECS * HEADS, FRAMES, HD)

def from_heads(array):
    return array.reshape(RECS, HEADS, FRAMES, HD).transpose(0, 2, 1, 3).reshape(RECS, FRAMES, D)

def head_probs(query_head, key_head):
    scores = jnp.dot(query_head, key_head.T, preferred_element_type=jnp.float32) * HD ** (-0.5)
    shifted = jnp.exp(scores - lax.optimization_barrier(jnp.max(scores, axis=1, keepdims=True)))
    return shifted / lax.optimization_barrier(jnp.sum(shifted, axis=1, keepdims=True))

def attend_forward(operands):
    query_head, key_head, value_head = operands
    rounded = head_probs(query_head, key_head).astype(jnp.bfloat16)
    return jnp.dot(rounded, value_head, preferred_element_type=jnp.float32).astype(jnp.bfloat16)

def attend_backward(operands):
    query_head, key_head, value_head, grad_head, context_head = operands
    scaling = HD ** (-0.5)
    probabilities = head_probs(query_head, key_head)
    rounded = probabilities.astype(jnp.bfloat16)
    row_dots = lax.optimization_barrier(jnp.sum(grad_head.astype(jnp.float32) * context_head.astype(jnp.float32), axis=1, keepdims=True))
    prob_grad = jnp.dot(grad_head, value_head.T, preferred_element_type=jnp.float32)
    score_grad = (probabilities * (prob_grad - row_dots) * scaling).astype(jnp.bfloat16)
    query_grad = jnp.dot(score_grad, key_head, preferred_element_type=jnp.float32).astype(jnp.bfloat16)
    key_grad = jnp.dot(score_grad.T, query_head, preferred_element_type=jnp.float32).astype(jnp.bfloat16)
    value_grad = jnp.dot(rounded.T, grad_head, preferred_element_type=jnp.float32).astype(jnp.bfloat16)
    return (query_grad, key_grad, value_grad)

def reference(queries, key_vecs, value_vecs, residual_in, point_weight, context_grad, depth_kernel, norm_gain, norm_bias, conv_grad):
    query_split = to_heads(queries)
    key_split = to_heads(key_vecs)
    value_split = to_heads(value_vecs)
    context_split = lax.map(attend_forward, (query_split, key_split, value_split))
    context = from_heads(context_split)
    mixed = (residual_in.astype(jnp.float32) + context.astype(jnp.float32)).astype(jnp.bfloat16)
    conv_input = jnp.dot(mixed.reshape(RECS * FRAMES, D), point_weight, preferred_element_type=jnp.float32).astype(jnp.bfloat16).reshape(RECS, FRAMES, 2 * D)
    span = KERNEL - 1
    value_half = conv_input[:, :, :D].astype(jnp.float32)
    gate_sig = jax.nn.sigmoid(conv_input[:, :, D:].astype(jnp.float32))
    glu = (value_half * gate_sig).astype(jnp.bfloat16)
    glu_view = lax.optimization_barrier(glu).astype(jnp.float32)
    glu_wide = jnp.pad(glu_view, ((0, 0), (span, 0), (0, 0)))
    depthwise = jnp.zeros((RECS, FRAMES, D), jnp.float32)
    for offset in range(KERNEL):
        depthwise = depthwise + depth_kernel[offset] * glu_wide[:, offset:offset + FRAMES]
    average = lax.optimization_barrier(jnp.mean(depthwise, axis=2, keepdims=True))
    centered = depthwise - average
    variance = lax.optimization_barrier(jnp.mean(centered * centered, axis=2, keepdims=True))
    inverse = lax.rsqrt(variance + 1e-05)
    normed = centered * inverse
    affine = normed * norm_gain + norm_bias
    sig_affine = jax.nn.sigmoid(affine)
    conv_output = (affine * sig_affine).astype(jnp.bfloat16)
    affine_grad = conv_grad.astype(jnp.float32) * (sig_affine * (1.0 + affine * (1.0 - sig_affine)))
    gain_grad = lax.optimization_barrier(jnp.sum(affine_grad * normed, axis=(0, 1))) / RECS
    bias_grad = lax.optimization_barrier(jnp.sum(affine_grad, axis=(0, 1))) / RECS
    normed_grad = affine_grad * norm_gain
    depth_grad = inverse * (normed_grad - lax.optimization_barrier(jnp.mean(normed_grad, axis=2, keepdims=True)) - normed * lax.optimization_barrier(jnp.mean(normed_grad * normed, axis=2, keepdims=True)))
    kernel_grad = jnp.stack([lax.optimization_barrier(jnp.sum(depth_grad * glu_wide[:, offset:offset + FRAMES], axis=(0, 1))) for offset in range(KERNEL)]) / RECS
    grad_wide = jnp.pad(depth_grad, ((0, 0), (0, span), (0, 0)))
    glu_grad = jnp.zeros((RECS, FRAMES, D), jnp.float32)
    for offset in range(KERNEL):
        begin = span - offset
        glu_grad = glu_grad + depth_kernel[offset] * grad_wide[:, begin:begin + FRAMES]
    input_grad = jnp.concatenate([glu_grad * gate_sig, glu_grad * value_half * gate_sig * (1.0 - gate_sig)], axis=2).astype(jnp.bfloat16)
    mixed_grad = jnp.dot(input_grad.reshape(RECS * FRAMES, 2 * D), point_weight.T, preferred_element_type=jnp.float32).reshape(RECS, FRAMES, D)
    residual_grad = (context_grad.astype(jnp.float32) + mixed_grad).astype(jnp.bfloat16)
    grads = lax.map(attend_backward, (query_split, key_split, value_split, to_heads(residual_grad), context_split))
    query_grad = from_heads(grads[0])
    key_grad = from_heads(grads[1])
    value_grad = from_heads(grads[2])
    return (context, conv_output, query_grad, key_grad, value_grad, input_grad, residual_grad, kernel_grad, gain_grad, bias_grad)
```

```python
import functools
import jax
import jax.numpy as jnp
from jax import lax
from jax.sharding import PartitionSpec as P
from jax.experimental import pallas as pl
from jax.experimental.pallas import tpu as pltpu

HEADS = 16


def from_behind(block, axis, distance):
    devices = range(lax.axis_size(axis))
    route = [(i - distance, i) for i in devices if i - distance in devices]
    return lax.ppermute(block, axis, route)


def block_probs(query_block, key_heads, scaling):
    scores = (
        jnp.einsum("qhd,khd->hqk", query_block, key_heads, preferred_element_type=jnp.float32)
        * scaling
    )
    shifted = jnp.exp(scores - jnp.max(scores, axis=2, keepdims=True))
    return shifted / jnp.sum(shifted, axis=2, keepdims=True)


def attend_forward(query_part, key_part, value_part, head_count):
    frames, channels = query_part.shape
    head_depth = channels // head_count
    scaling = head_depth ** (-0.5)
    query_heads = query_part.reshape(frames, head_count, head_depth)
    key_heads = key_part.reshape(frames, head_count, head_depth)
    value_heads = value_part.reshape(frames, head_count, head_depth)
    block_rows = min(512, frames)

    def one_block(running, index):
        query_block = lax.dynamic_slice_in_dim(query_heads, index * block_rows, block_rows, 0)
        rounded = block_probs(query_block, key_heads, scaling).astype(jnp.bfloat16)
        context = jnp.einsum(
            "hqk,khd->qhd", rounded, value_heads, preferred_element_type=jnp.float32
        ).astype(jnp.bfloat16)
        return (running, context)

    unused, blocks = lax.scan(
        one_block, jnp.zeros((), jnp.float32), jnp.arange(frames // block_rows)
    )
    return blocks.reshape(frames, channels)


def attend_backward(query_part, key_part, value_part, grad_part, context_part, head_count):
    frames, channels = query_part.shape
    head_depth = channels // head_count
    scaling = head_depth ** (-0.5)
    query_heads = query_part.reshape(frames, head_count, head_depth)
    key_heads = key_part.reshape(frames, head_count, head_depth)
    value_heads = value_part.reshape(frames, head_count, head_depth)
    grad_heads = grad_part.reshape(frames, head_count, head_depth)
    context_heads = context_part.reshape(frames, head_count, head_depth)
    block_rows = min(512, frames)

    def one_block(running, index):
        key_total, value_total = running
        start = index * block_rows
        query_block = lax.dynamic_slice_in_dim(query_heads, start, block_rows, 0)
        grad_block = lax.dynamic_slice_in_dim(grad_heads, start, block_rows, 0)
        context_block = lax.dynamic_slice_in_dim(context_heads, start, block_rows, 0)
        probabilities = block_probs(query_block, key_heads, scaling)
        rounded = probabilities.astype(jnp.bfloat16)
        row_dots = jnp.sum(
            grad_block.astype(jnp.float32) * context_block.astype(jnp.float32), axis=2
        )
        prob_grad = jnp.einsum(
            "qhd,khd->hqk", grad_block, value_heads, preferred_element_type=jnp.float32
        )
        score_grad = (probabilities * (prob_grad - row_dots.T[:, :, None]) * scaling).astype(
            jnp.bfloat16
        )
        query_grad = jnp.einsum(
            "hqk,khd->qhd", score_grad, key_heads, preferred_element_type=jnp.float32
        ).astype(jnp.bfloat16)
        key_total = key_total + jnp.einsum(
            "hqk,qhd->khd", score_grad, query_block, preferred_element_type=jnp.float32
        )
        value_total = value_total + jnp.einsum(
            "hqk,qhd->khd", rounded, grad_block, preferred_element_type=jnp.float32
        )
        return ((key_total, value_total), query_grad)

    empty = jnp.zeros((frames, head_count, head_depth), jnp.float32)
    totals, blocks = lax.scan(one_block, (empty, empty), jnp.arange(frames // block_rows))
    query_grad = blocks.reshape(frames, channels)
    key_grad = totals[0].astype(jnp.bfloat16).reshape(frames, channels)
    value_grad = totals[1].astype(jnp.bfloat16).reshape(frames, channels)
    return (query_grad, key_grad, value_grad)


def shards(
    queries,
    key_vecs,
    value_vecs,
    residual_in,
    point_weight,
    context_grad,
    depth_kernel,
    norm_gain,
    norm_bias,
    conv_grad,
):
    head_count = HEADS // lax.axis_size("seq")
    query_heads, key_heads, value_heads = (
        lax.all_to_all(queries, "seq", split_axis=2, concat_axis=1, tiled=True),
        lax.all_to_all(key_vecs, "seq", split_axis=2, concat_axis=1, tiled=True),
        lax.all_to_all(value_vecs, "seq", split_axis=2, concat_axis=1, tiled=True),
    )
    context_local = attend_forward(query_heads[0], key_heads[0], value_heads[0], head_count)
    context_out = lax.all_to_all(
        context_local[None], "seq", split_axis=1, concat_axis=2, tiled=True
    )
    taps = depth_kernel.shape[0]
    channels = depth_kernel.shape[1]
    span = taps - 1
    frames = residual_in.shape[1]
    mixed = (residual_in[0].astype(jnp.float32) + context_out[0].astype(jnp.float32)).astype(
        jnp.bfloat16
    )
    pre_conv = jnp.dot(
        mixed,
        lax.all_gather(point_weight, "seq", axis=0, tiled=True),
        preferred_element_type=jnp.float32,
    )
    conv_input = pre_conv.astype(jnp.bfloat16)[None]
    value_half = conv_input[:, :, :channels].astype(jnp.float32)
    gate_sig = jax.nn.sigmoid(conv_input[:, :, channels:].astype(jnp.float32))
    glu = (value_half * gate_sig).astype(jnp.bfloat16)
    earlier = from_behind(glu[:, frames - span :], "seq", 1)
    glu_wide = jnp.concatenate([earlier, glu], axis=1)
    glu_view = lax.optimization_barrier(glu_wide).astype(jnp.float32)
    depthwise = jnp.zeros((1, frames, channels), jnp.float32)
    for offset in range(taps):
        depthwise = depthwise + depth_kernel[offset] * glu_view[:, offset : offset + frames]
    average = jnp.mean(depthwise, axis=2, keepdims=True)
    centered = depthwise - average
    variance = jnp.mean(centered * centered, axis=2, keepdims=True)
    inverse = lax.rsqrt(variance + 1e-05)
    normed = centered * inverse
    affine = normed * norm_gain + norm_bias
    sig_affine = jax.nn.sigmoid(affine)
    conv_output = (affine * sig_affine).astype(jnp.bfloat16)
    affine_grad = conv_grad.astype(jnp.float32) * (sig_affine * (1.0 + affine * (1.0 - sig_affine)))
    gain_term = jnp.sum(affine_grad * normed, axis=(0, 1))
    bias_term = jnp.sum(affine_grad, axis=(0, 1))
    normed_grad = affine_grad * norm_gain
    depth_grad = inverse * (
        normed_grad
        - jnp.mean(normed_grad, axis=2, keepdims=True)
        - normed * jnp.mean(normed_grad * normed, axis=2, keepdims=True)
    )
    kernel_term = jnp.stack(
        [
            jnp.sum(depth_grad * glu_view[:, offset : offset + frames], axis=(0, 1))
            for offset in range(taps)
        ]
    )
    kernel_total, gain_total, bias_total = lax.psum(
        (kernel_term, gain_term, bias_term), ("dp", "seq")
    )
    recordings = lax.axis_size("dp")
    kernel_grad = kernel_total / recordings
    gain_grad = gain_total / recordings
    bias_grad = bias_total / recordings
    later = from_behind(depth_grad[:, :span], "seq", -1)
    grad_wide = jnp.concatenate([depth_grad, later], axis=1)
    glu_grad = jnp.zeros((1, frames, channels), jnp.float32)
    for offset in range(taps):
        begin = span - offset
        glu_grad = glu_grad + depth_kernel[offset] * grad_wide[:, begin : begin + frames]
    input_grad = jnp.concatenate(
        [glu_grad * gate_sig, glu_grad * value_half * gate_sig * (1.0 - gate_sig)], axis=2
    ).astype(jnp.bfloat16)
    slope_rows = input_grad[0]
    mixed_grad = jnp.einsum(
        "fc,dc->fd",
        slope_rows,
        lax.all_gather(point_weight, "seq", axis=0, tiled=True),
        preferred_element_type=jnp.float32,
    )
    residual_grad = (context_grad.astype(jnp.float32) + mixed_grad[None]).astype(jnp.bfloat16)
    grad_heads = lax.all_to_all(residual_grad, "seq", split_axis=2, concat_axis=1, tiled=True)
    query_grad, key_grad, value_grad = attend_backward(
        query_heads[0], key_heads[0], value_heads[0], grad_heads[0], context_local, head_count
    )
    query_out, key_out, value_out = (
        lax.all_to_all(query_grad[None], "seq", split_axis=1, concat_axis=2, tiled=True),
        lax.all_to_all(key_grad[None], "seq", split_axis=1, concat_axis=2, tiled=True),
        lax.all_to_all(value_grad[None], "seq", split_axis=1, concat_axis=2, tiled=True),
    )
    return (
        context_out,
        conv_output,
        query_out,
        key_out,
        value_out,
        input_grad,
        residual_grad,
        kernel_grad,
        gain_grad,
        bias_grad,
    )


BF = jnp.bfloat16
F32 = jnp.float32
HALO = 32
LANES = 128
TERM_ROWS = 40


SEMS = dict(
    send_a=1, send_b=1, send_out=1, send_r1=1, send_r2=1, send_r3=1, z_up_send=3, z_dn_send=3,
    qkv=4, w_y=1, w_mate=1, w_pair=1, z_up=3, z_dn=3, w_x=4, ctx_mate=1, ctx_far=1, halo1=1, halo2=1,
    grad=1, red1=1, red2=1, red3=1, outs=1, keep=2, w_self=1, loads=6, ctx_keep=1, out_keep=1,
)


def sem_base(name):
    names = list(SEMS)
    return sum(SEMS[n] for n in names[: names.index(name)])


def fused_kernel(
    dims,
    q_ref, k_ref, v_ref, res_ref, w_ref, cg_ref, taps_hbm, gain_hbm, bias_hbm, og_ref,
    ctx_out, conv_out, dq_out, dk_out, dv_out, ig_out, rg_out, kg_out, gg_out, bg_out,
    q_h, k_h, v_h, g_h, qt, kt, vt, gt, ctxt, ctx_h, prob, pb_s, ds_s, dqt, dq_h, dk_h, dv_h,
    res_v, cg_v, og_v, w_full, pre, mixed, a_s, sig_s, glu_f, dw, ng_s, dg, part, rs_buf, s2_buf, fin,
    taps_ref, gain_ref, bias_ref, hs1, hr1, hs2, hr2,
    sems,
):
    n_seq, n_dp, rows, channels, taps, depth = dims
    own = channels // n_seq
    pairs = own // LANES
    frames = rows * n_seq
    chunks = channels // LANES
    scaling = depth ** (-0.5)
    line = n_dp // 2
    me = lax.axis_index("seq")
    dp = lax.axis_index("dp")
    core = lax.rem(me, 2)
    mate = me + 1 - 2 * core
    across = lax.rem(me + 2, n_seq)
    diag = lax.rem(mate + 2, n_seq)
    chip = lax.div(me, 2)
    x_pos = lax.rem(dp, 2)
    z_pos = lax.div(dp, 2)
    x_dp = dp + 1 - 2 * x_pos
    peers = [across, diag, mate]
    dp_peers = [lax.rem(dp + d, n_dp) for d in range(1, n_dp)]
    has_up = z_pos < line - 1
    has_down = z_pos > 0

    def sem(name, index=0):
        return sems.at[sem_base(name) + index]

    def local(src, dst, name, index=0):
        copy = pltpu.make_async_copy(src, dst, sem(name, index))
        copy.start()
        return copy

    def remote(src, dst, device, send, recv):
        copy = pltpu.make_async_remote_copy(
            src_ref=src, dst_ref=dst, send_sem=sem(*send), recv_sem=sem(*recv),
            device_id=device, device_id_type=pl.DeviceIdType.MESH,
        )
        copy.start()
        return copy

    def drain(ref, name, index=0):
        pltpu.make_async_copy(ref, ref, sem(name, index)).wait()

    def at(value, size):
        return pl.ds(pl.multiple_of(value * size, size), size)

    loads = [
        local(src, dst, "loads", t)
        for t, (src, dst) in enumerate(
            ((res_ref, res_v), (cg_ref, cg_v), (og_ref, og_v), (taps_hbm, taps_ref), (gain_hbm, gain_ref), (bias_hbm, bias_ref))
        )
    ]
    w_rows = w_ref.shape[0]
    w_self = local(w_ref, w_full.at[at(me, w_rows), :], "w_self")

    barrier = pltpu.get_barrier_semaphore()

    def greet(device):
        pl.semaphore_signal(barrier, inc=1, device_id=device, device_id_type=pl.DeviceIdType.MESH)

    for p in peers:
        greet((dp, p))
    greet((x_dp, me))

    @pl.when(has_up)
    def _():
        greet((dp + 2, me))

    @pl.when(has_down)
    def _():
        greet((dp - 2, me))

    pl.semaphore_wait(barrier, n_seq + has_up.astype(jnp.int32) + has_down.astype(jnp.int32))

    piece = w_rows // n_dp

    def w_piece(owner, x, z):
        return pl.ds(pl.multiple_of(owner * w_rows + (z * 2 + x) * piece, piece), piece)

    remote(
        w_ref.at[at(dp, piece), :], w_full.at[w_piece(me, x_pos, z_pos), :], (dp, across),
        ("send_a",), ("w_y",),
    )

    def head_cols(owner, pair):
        return pl.ds(pl.multiple_of(owner * own + pair * LANES, LANES), LANES)

    for pair in range(pairs):
        pc = slice(pair * LANES, (pair + 1) * LANES)
        for t, (src, dst) in enumerate(((q_ref, q_h), (k_ref, k_h), (v_ref, v_h))):
            for p in peers:
                remote(
                    src.at[:, head_cols(p, pair)], dst.at[at(me, rows), pc], (dp, p),
                    ("send_a",), ("qkv", 2 * pair + min(t, 1)),
                )
            local(src.at[:, head_cols(me, pair)], dst.at[at(me, rows), pc], "keep", pair)
    remote(w_ref, w_full.at[at(me, w_rows), :], (dp, mate), ("send_a",), ("w_mate",))

    def pass_on(x, z):
        here = w_full.at[w_piece(across, x, z), :]
        remote(here, here, (dp, mate), ("send_a",), ("w_pair",))

    def pass_x(z):
        here = w_full.at[w_piece(across, x_pos, z), :]
        remote(here, here, (x_dp, me), ("send_a",), ("w_x", z))

    def pass_up(z, step):
        here = w_full.at[w_piece(across, x_pos, z), :]
        remote(here, here, (dp + 2, me), ("z_up_send", step), ("z_up", step))

    def pass_down(z, step):
        here = w_full.at[w_piece(across, x_pos, z), :]
        remote(here, here, (dp - 2, me), ("z_dn_send", step), ("z_dn", step))

    def w_first():
        drain(w_full.at[w_piece(across, x_pos, z_pos), :], "w_y")

        @pl.when(has_up)
        def _():
            pass_up(z_pos, 0)

        @pl.when(has_down)
        def _():
            pass_down(z_pos, 0)

        pass_x(z_pos)
        pass_on(x_pos, z_pos)

    def w_step(step):
        @pl.when(z_pos >= step)
        def _():
            z = z_pos - step
            drain(w_full.at[w_piece(across, x_pos, z), :], "z_up", step - 1)
            if step < line - 1:
                @pl.when(has_up)
                def _():
                    pass_up(z, step)
            pass_x(z)
            pass_on(x_pos, z)

        @pl.when(z_pos + step < line)
        def _():
            z = z_pos + step
            drain(w_full.at[w_piece(across, x_pos, z), :], "z_dn", step - 1)
            if step < line - 1:
                @pl.when(has_down)
                def _():
                    pass_down(z, step)
            pass_x(z)
            pass_on(x_pos, z)

    def w_across_x():
        for z in range(line):
            drain(w_full.at[w_piece(across, 1 - x_pos, z), :], "w_x", z)
            pass_on(1 - x_pos, z)

    def flip(value):
        return value.astype(F32).T

    q_block = 2 * rows

    def forward_head(h, b):
        hr = slice(h * depth, (h + 1) * depth)
        cols = at(b, q_block)
        scores = jnp.dot(k_h[:, hr], qt[hr, cols], preferred_element_type=F32)
        shifted = jnp.exp(scores - jnp.max(scores, axis=0, keepdims=True))
        p = shifted * (1.0 / jnp.sum(shifted, axis=0, keepdims=True))
        rounded = p.astype(BF)
        prob[h, :, cols] = p
        pb_s[h, :, cols] = rounded
        ctxt[hr, cols] = jnp.dot(vt[hr, :], rounded, preferred_element_type=F32).astype(BF)

    def send_rows(src, dst, pair, p, send, recv):
        source = slice(pair * LANES, (pair + 1) * LANES)
        remote(src.at[at(p, rows), source], dst.at[:, head_cols(me, pair)], (dp, p), send, recv)

    def keep_rows(src, dst, pair, name):
        source = slice(pair * LANES, (pair + 1) * LANES)
        local(src.at[at(me, rows), source], dst.at[:, head_cols(me, pair)], name)

    def send_out(src, dst, pair):
        for p in peers:
            send_rows(src, dst, pair, p, ("send_out",), ("outs",))
        keep_rows(src, dst, pair, "out_keep")

    w_first()
    for pair in range(pairs):
        pc = slice(pair * LANES, (pair + 1) * LANES)
        drain(k_h.at[0 : 3 * rows, 0:LANES], "qkv", 2 * pair)
        drain(k_h.at[0 : 3 * rows, 0:LANES], "keep", pair)
        qt[pc, :] = (flip(q_h[:, pc]) * scaling).astype(BF)
        if pair == 0:
            w_step(1)
        drain(k_h.at[0 : 3 * rows, 0 : 2 * LANES], "qkv", 2 * pair + 1)
        vt[pc, :] = flip(v_h[:, pc]).astype(BF)
        for turn, b in enumerate((1 - chip, chip)):
            forward_head(2 * pair, b)
            forward_head(2 * pair + 1, b)
            ctx_h[at(b, q_block), pc] = flip(ctxt[pc, at(b, q_block)]).astype(BF)
            if turn == 0:
                send_rows(ctx_h, ctx_out, pair, across, ("send_a",), ("ctx_far",))
                send_rows(ctx_h, ctx_out, pair, diag, ("send_a",), ("ctx_far",))
            else:
                send_rows(ctx_h, ctx_out, pair, mate, ("send_a",), ("ctx_mate",))
                keep_rows(ctx_h, ctx_out, pair, "ctx_keep")
        w_step(2 + pair)

    for pair in range(pairs):
        pc = slice(pair * LANES, (pair + 1) * LANES)
        kt[pc, :] = flip(k_h[:, pc]).astype(BF)
    loads[0].wait()
    w_self.wait()
    drain(w_full.at[at(mate, w_rows), :], "w_mate")
    drain(ctx_h.at[0:rows, :], "ctx_keep")
    drain(ctx_h.at[0:rows, :], "ctx_mate")
    near = at(chip, 2 * own)
    far = at(1 - chip, 2 * own)
    wide = 2 * LANES
    mixed[:, near] = (res_v[:, near].astype(F32) + ctx_out[:, near].astype(F32)).astype(BF)

    def conv_near(i, carry):
        cols = at(i, wide)
        pre[:, cols] = jnp.dot(mixed[:, near], w_full[near, cols], preferred_element_type=F32)
        return carry

    lax.fori_loop(0, 2 * channels // wide, conv_near, 0)
    w_across_x()
    drain(ctx_h.at[0 : 2 * rows, :], "ctx_far")
    mixed[:, far] = (res_v[:, far].astype(F32) + ctx_out[:, far].astype(F32)).astype(BF)
    drain(w_full.at[at(diag, w_rows), :], "w_pair")

    def conv_in(i, carry):
        cols = at(i, wide)
        gates = pl.ds(pl.multiple_of(channels + i * wide, wide), wide)
        a = jnp.dot(mixed[:, far], w_full[far, cols], preferred_element_type=F32)
        b = jnp.dot(mixed[:, far], w_full[far, gates], preferred_element_type=F32)
        a = (a + pre[:, cols]).astype(BF)
        b = (b + pre[:, gates]).astype(BF)
        sig = jax.nn.sigmoid(b.astype(F32))
        a_s[:, cols] = a
        sig_s[:, cols] = sig
        rounded = (a.astype(F32) * sig).astype(BF)
        glu = rounded.astype(F32)
        for half in range(2):
            lanes = slice(half * LANES, (half + 1) * LANES)
            glu_f[2 * i + half, HALO : HALO + rows, :] = glu[:, lanes]
            hs1[2 * i + half] = rounded[rows - HALO :, lanes]
        return carry

    lax.fori_loop(0, channels // wide, conv_in, 0)
    remote(hs1, hr1, (dp, lax.rem(me + 1, n_seq)), ("send_a",), ("halo1",))
    for copy in loads[2:]:
        copy.wait()
    span = taps - 1
    base = HALO - span

    def norm_rows(first, count, unroll):
        here = slice(first, first + count)
        zero = jnp.zeros((count, LANES), F32)

        def conv(c, total):
            lanes = at(c, LANES)
            acc = zero
            for o in range(taps):
                low = base + first + o
                acc = acc + taps_ref[o : o + 1, lanes] * glu_f[c, low : low + count, :]
            dw[c, here, :] = acc
            return total + acc

        total = lax.fori_loop(0, chunks, conv, zero)
        average = jnp.sum(total, axis=1, keepdims=True) * (1.0 / channels)

        def squares(c, total):
            centered = dw[c, here, :] - average
            return total + centered * centered

        total = lax.fori_loop(0, chunks, squares, zero, unroll=unroll)
        variance = jnp.sum(total, axis=1, keepdims=True) * (1.0 / channels)
        inverse = lax.rsqrt(variance + 1e-05)

        def norm_step(c, carry):
            s1, s2 = carry
            lanes = at(c, LANES)
            normed = (dw[c, here, :] - average) * inverse
            affine = normed * gain_ref[:, lanes] + bias_ref[:, lanes]
            sig = jax.nn.sigmoid(affine)
            conv_out[here, lanes] = (affine * sig).astype(BF)
            affine_grad = og_v[here, lanes].astype(F32) * (sig * (1.0 + affine * (1.0 - sig)))
            gain_term = jnp.sum(affine_grad * normed, axis=0, keepdims=True)
            bias_term = jnp.sum(affine_grad, axis=0, keepdims=True)
            if first == 0:
                gain_term = gain_term + part[c, taps : taps + 1, :]
                bias_term = bias_term + part[c, taps + 1 : taps + 2, :]
            part[c, taps : taps + 1, :] = gain_term
            part[c, taps + 1 : taps + 2, :] = bias_term
            normed_grad = affine_grad * gain_ref[:, lanes]
            dw[c, here, :] = normed
            ng_s[c, here, :] = normed_grad
            return s1 + normed_grad, s2 + normed_grad * normed

        s1, s2 = lax.fori_loop(0, chunks, norm_step, (zero, zero), unroll=unroll)
        m1 = jnp.sum(s1, axis=1, keepdims=True) * (1.0 / channels)
        m2 = jnp.sum(s2, axis=1, keepdims=True) * (1.0 / channels)

        def depth_grad_step(c, carry):
            grad = inverse * (ng_s[c, here, :] - m1 - dw[c, here, :] * m2)
            dg[c, here, :] = grad
            if first == 0:
                hs2[c] = grad[0:HALO].astype(BF)
            return carry

        lax.fori_loop(0, chunks, depth_grad_step, 0, unroll=unroll)

    norm_rows(HALO, rows - HALO, 1)
    drain(hr1, "halo1")
    edge = (me > 0).astype(F32)
    glu_f[:, 0:HALO, :] = hr1[...].astype(F32) * edge
    norm_rows(0, HALO, chunks)
    remote(hs2, hr2, (dp, lax.rem(me + n_seq - 1, n_seq)), ("send_b",), ("halo2",))

    def glu_back(first, count):
        def body(c, carry):
            lanes = at(c, LANES)
            gates = pl.ds(pl.multiple_of(channels + c * LANES, LANES), LANES)
            here = slice(first, first + count)
            acc = jnp.zeros((count, LANES), F32)
            for o in range(taps):
                low = first + span - o
                acc = acc + taps_ref[o : o + 1, lanes] * dg[c, low : low + count, :]
            sig = sig_s[here, lanes]
            ig_out[here, lanes] = (acc * sig).astype(BF)
            slope = acc * a_s[here, lanes].astype(F32) * sig * (1.0 - sig)
            ig_out[here, gates] = slope.astype(BF)
            return carry

        lax.fori_loop(0, chunks, body, 0)

    def tap_grad(c, carry):
        grad = dg[c, 0:rows, :]
        for o in range(taps):
            part[c, o : o + 1, :] = jnp.sum(
                grad * glu_f[c, base + o : base + o + rows, :], axis=0, keepdims=True
            )
        part[c, taps + 2 : TERM_ROWS, :] = jnp.zeros((TERM_ROWS - taps - 2, LANES), F32)
        return carry

    glu_back(0, rows - HALO)
    early = chunks // 2
    lax.fori_loop(0, early, tap_grad, 0)
    drain(hr2, "halo2")
    edge = (me < n_seq - 1).astype(F32)
    dg[:, rows : rows + HALO, :] = hr2[...].astype(F32) * edge
    glu_back(rows - HALO, HALO)
    loads[1].wait()
    for p in peers + [me]:
        cols = at(p, own)
        grad = lax.dot_general(
            ig_out[...], w_full[cols, :], (((1,), (1,)), ((), ())), preferred_element_type=F32
        )
        rg_out[:, cols] = (cg_v[:, cols].astype(F32) + grad).astype(BF)
        if p is me:
            g_h[at(me, rows), :] = rg_out[:, cols]
        else:
            remote(rg_out.at[:, cols], g_h.at[at(me, rows), :], (dp, p), ("send_b",), ("grad",))

    lax.fori_loop(early, chunks, tap_grad, 0)
    for d, p in enumerate(dp_peers):
        remote(part.at[p], rs_buf.at[d], (p, me), ("send_r1",), ("red1",))

    drain(q_h.at[0 : 3 * rows, :], "grad")

    def backward_head(h, b):
        hr = slice(h * depth, (h + 1) * depth)
        cols = at(b, q_block)
        grad = gt[hr, cols]
        dots = jnp.sum(grad.astype(F32) * ctxt[hr, cols].astype(F32), axis=0, keepdims=True)
        prob_grad = jnp.dot(v_h[:, hr], grad, preferred_element_type=F32)
        score_grad = (prob[h, :, cols] * (prob_grad - dots) * scaling).astype(BF)
        ds_s[h % 2, :, cols] = score_grad
        dqt[hr, cols] = jnp.dot(kt[hr, :], score_grad, preferred_element_type=F32)

    first_head = lax.broadcasted_iota(jnp.int32, (frames, LANES), 1) < depth
    for pair in range(pairs):
        pc = slice(pair * LANES, (pair + 1) * LANES)
        left = jnp.dot(pb_s[2 * pair], g_h[:, pc], preferred_element_type=F32)
        right = jnp.dot(pb_s[2 * pair + 1], g_h[:, pc], preferred_element_type=F32)
        dv_h[:, pc] = jnp.where(first_head, left, right).astype(BF)
        send_out(dv_h, dv_out, pair)
        gt[pc, :] = flip(g_h[:, pc]).astype(BF)

    for pair in range(pairs):
        pc = slice(pair * LANES, (pair + 1) * LANES)
        for b in (1 - chip, chip):
            backward_head(2 * pair, b)
            backward_head(2 * pair + 1, b)
        dq_h[:, pc] = dqt[pc, :].T.astype(BF)
        send_out(dq_h, dq_out, pair)
        if pair == 0:
            drain(rs_buf, "red1")
            total = part[dp]
            for d in range(n_dp - 1):
                total = total + rs_buf[d]
            s2_buf[me] = total
            for p in peers:
                remote(s2_buf.at[me], s2_buf.at[me], (dp, p), ("send_r2",), ("red2",))
        left = jnp.dot(ds_s[0], q_h[:, pc], preferred_element_type=F32)
        right = jnp.dot(ds_s[1], q_h[:, pc], preferred_element_type=F32)
        dk_h[:, pc] = jnp.where(first_head, left, right).astype(BF)
        send_out(dk_h, dk_out, pair)

    drain(s2_buf.at[0 : n_seq - 1], "red2")
    total = s2_buf[0]
    for s in range(1, n_seq):
        total = total + s2_buf[s]
    fin[dp] = total * (1.0 / n_dp)
    for p in dp_peers:
        remote(fin.at[dp], fin.at[dp], (p, me), ("send_r3",), ("red3",))

    wide_rows = 2 * channels
    count = 2 * w_rows + (1 + line) * piece
    count += (12 * pairs * rows * LANES + chunks * HALO * LANES) // wide_rows
    drain(w_full.at[0:count, :], "send_a")
    drain(rs_buf, "send_r1")
    drain(s2_buf.at[0 : n_seq - 1], "send_r2")

    for step in range(line - 1):
        @pl.when(jnp.logical_and(has_up, z_pos >= step))
        def _():
            drain(w_full.at[0:piece, :], "z_up_send", step)

        @pl.when(jnp.logical_and(has_down, z_pos + step < line))
        def _():
            drain(w_full.at[0:piece, :], "z_dn_send", step)

    drain(rs_buf, "red3")
    for c in range(chunks):
        lanes = slice(c * LANES, (c + 1) * LANES)
        kg_out[:, lanes] = fin[c, 0:taps, :]
        gg_out[:, lanes] = fin[c, taps : taps + 1, :]
        bg_out[:, lanes] = fin[c, taps + 1 : taps + 2, :]
    drain(rs_buf, "send_r3")
    drain(w_full.at[0 : 3 * pairs * rows * LANES // wide_rows, :], "out_keep")
    drain(w_full.at[0 : 9 * pairs * rows * LANES // wide_rows, :], "outs")
    drain(w_full.at[0 : 9 * pairs * rows * LANES // wide_rows, :], "send_out")
    drain(w_full.at[0 : (chunks * HALO * LANES + 3 * rows * own) // wide_rows, :], "send_b")


def place_outputs(*refs):
    sems = refs[20]
    copies = [pltpu.make_async_copy(refs[i], refs[10 + i], sems.at[i]) for i in range(10)]
    for copy in copies:
        copy.start()
    for copy in copies:
        copy.wait()


def fused_shards(
    queries, key_vecs, value_vecs, residual_in, point_weight, context_grad, depth_kernel,
    norm_gain, norm_bias, conv_grad,
):
    n_seq = lax.axis_size("seq")
    n_dp = lax.axis_size("dp")
    rows, channels = queries.shape[1:]
    taps = depth_kernel.shape[0]
    depth = channels // HEADS
    frames = rows * n_seq
    own = channels // n_seq
    heads = own // depth
    chunks = channels // LANES
    s = jax.ShapeDtypeStruct
    vm = pltpu.VMEM
    block = s((rows, channels), BF)
    head_rows = vm((frames, own), BF)
    head_cols = vm((own, frames), BF)
    scratch = (
        [head_rows] * 4 + [head_cols] * 5 + [head_rows]
        + [vm((heads, frames, frames), F32), vm((heads, frames, frames), BF), vm((2, frames, frames), BF)]
        + [vm((own, frames), F32)] + [head_rows] * 3
        + [
            vm((rows, channels), BF),
            vm((rows, channels), BF),
            vm((rows, channels), BF),
            vm((channels, 2 * channels), BF),
            vm((rows, 2 * channels), F32),
            vm((rows, channels), BF),
            vm((rows, channels), BF),
            vm((rows, channels), F32),
            vm((chunks, HALO + rows, LANES), F32),
            vm((chunks, rows, LANES), F32),
            vm((chunks, rows, LANES), F32),
            vm((chunks, rows + HALO, LANES), F32),
            vm((chunks, TERM_ROWS, LANES), F32),
            vm((n_dp - 1, TERM_ROWS, LANES), F32),
            vm((n_seq, TERM_ROWS, LANES), F32),
            vm((chunks, TERM_ROWS, LANES), F32),
            vm((taps, channels), F32),
            vm((1, channels), F32),
            vm((1, channels), F32),
            vm((chunks, HALO, LANES), BF),
            vm((chunks, HALO, LANES), BF),
            vm((chunks, HALO, LANES), BF),
            vm((chunks, HALO, LANES), BF),
            pltpu.SemaphoreType.DMA((sum(SEMS.values()),)),
        ]
    )
    spec = pl.BlockSpec(memory_space=pltpu.VMEM)
    hbm = pl.BlockSpec(memory_space=pl.ANY)
    outs = pl.pallas_call(
        functools.partial(fused_kernel, (n_seq, n_dp, rows, channels, taps, depth)),
        out_shape=(
            block, block, block, block, block, s((rows, 2 * channels), BF), block,
            s((taps, channels), F32), s((1, channels), F32), s((1, channels), F32),
        ),
        in_specs=[hbm] * 10,
        out_specs=(spec,) * 10,
        scratch_shapes=scratch,
        compiler_params=pltpu.CompilerParams(
            collective_id=0, has_side_effects=True, vmem_limit_bytes=56 * 1024 * 1024
        ),
    )(
        queries[0], key_vecs[0], value_vecs[0], residual_in[0], point_weight, context_grad[0],
        depth_kernel, norm_gain[None], norm_bias[None], conv_grad[0],
    )
    outs = pl.pallas_call(
        place_outputs,
        out_shape=tuple(s(o.shape, o.dtype) for o in outs),
        in_specs=[spec] * 10,
        out_specs=(hbm,) * 10,
        scratch_shapes=[pltpu.SemaphoreType.DMA((10,))],
    )(*outs)
    return tuple(o[None] for o in outs[:7]) + (outs[7], outs[8][0], outs[9][0])


def chosen(*args):
    n_seq = lax.axis_size("seq")
    n_dp = lax.axis_size("dp")
    recs, rows, channels = args[0].shape
    fits = (
        n_seq == 4
        and recs == 1
        and rows % 128 == 0
        and channels % (LANES * n_seq) == 0
        and 2 * channels == LANES * HEADS
        and channels // LANES == n_dp
        and rows * n_seq <= 512
        and args[4].shape[0] == channels // n_seq == 2 * LANES
        and args[6].shape[0] <= 31
    )
    return fused_shards(*args) if fits else shards(*args)


def solution(mesh):
    in_specs = (
        P("dp", "seq", None),
        P("dp", "seq", None),
        P("dp", "seq", None),
        P("dp", "seq", None),
        P("seq", None),
        P("dp", "seq", None),
        P(),
        P(),
        P(),
        P("dp", "seq", None),
    )
    out_specs = (
        P("dp", "seq", None),
        P("dp", "seq", None),
        P("dp", "seq", None),
        P("dp", "seq", None),
        P("dp", "seq", None),
        P("dp", "seq", None),
        P("dp", "seq", None),
        P(),
        P(),
        P(),
    )
    return jax.shard_map(chosen, mesh=mesh, in_specs=in_specs, out_specs=out_specs, check_vma=False)
```

```python
import functools
import jax
import jax.numpy as jnp
from jax import lax
from jax.sharding import PartitionSpec as P
from jax.experimental import pallas as pl
from jax.experimental.pallas import tpu as pltpu

HEADS = 16


def from_behind(block, axis, distance):
    devices = range(lax.axis_size(axis))
    route = [(i - distance, i) for i in devices if i - distance in devices]
    return lax.ppermute(block, axis, route)


def block_probs(query_block, key_heads, scaling):
    scores = (
        jnp.einsum("qhd,khd->hqk", query_block, key_heads, preferred_element_type=jnp.float32)
        * scaling
    )
    shifted = jnp.exp(scores - jnp.max(scores, axis=2, keepdims=True))
    return shifted / jnp.sum(shifted, axis=2, keepdims=True)


def attend_forward(query_part, key_part, value_part, head_count):
    frames, channels = query_part.shape
    head_depth = channels // head_count
    scaling = head_depth ** (-0.5)
    query_heads = query_part.reshape(frames, head_count, head_depth)
    key_heads = key_part.reshape(frames, head_count, head_depth)
    value_heads = value_part.reshape(frames, head_count, head_depth)
    block_rows = min(512, frames)

    def one_block(running, index):
        query_block = lax.dynamic_slice_in_dim(query_heads, index * block_rows, block_rows, 0)
        rounded = block_probs(query_block, key_heads, scaling).astype(jnp.bfloat16)
        context = jnp.einsum(
            "hqk,khd->qhd", rounded, value_heads, preferred_element_type=jnp.float32
        ).astype(jnp.bfloat16)
        return (running, context)

    unused, blocks = lax.scan(
        one_block, jnp.zeros((), jnp.float32), jnp.arange(frames // block_rows)
    )
    return blocks.reshape(frames, channels)


def attend_backward(query_part, key_part, value_part, grad_part, context_part, head_count):
    frames, channels = query_part.shape
    head_depth = channels // head_count
    scaling = head_depth ** (-0.5)
    query_heads = query_part.reshape(frames, head_count, head_depth)
    key_heads = key_part.reshape(frames, head_count, head_depth)
    value_heads = value_part.reshape(frames, head_count, head_depth)
    grad_heads = grad_part.reshape(frames, head_count, head_depth)
    context_heads = context_part.reshape(frames, head_count, head_depth)
    block_rows = min(512, frames)

    def one_block(running, index):
        key_total, value_total = running
        start = index * block_rows
        query_block = lax.dynamic_slice_in_dim(query_heads, start, block_rows, 0)
        grad_block = lax.dynamic_slice_in_dim(grad_heads, start, block_rows, 0)
        context_block = lax.dynamic_slice_in_dim(context_heads, start, block_rows, 0)
        probabilities = block_probs(query_block, key_heads, scaling)
        rounded = probabilities.astype(jnp.bfloat16)
        row_dots = jnp.sum(
            grad_block.astype(jnp.float32) * context_block.astype(jnp.float32), axis=2
        )
        prob_grad = jnp.einsum(
            "qhd,khd->hqk", grad_block, value_heads, preferred_element_type=jnp.float32
        )
        score_grad = (probabilities * (prob_grad - row_dots.T[:, :, None]) * scaling).astype(
            jnp.bfloat16
        )
        query_grad = jnp.einsum(
            "hqk,khd->qhd", score_grad, key_heads, preferred_element_type=jnp.float32
        ).astype(jnp.bfloat16)
        key_total = key_total + jnp.einsum(
            "hqk,qhd->khd", score_grad, query_block, preferred_element_type=jnp.float32
        )
        value_total = value_total + jnp.einsum(
            "hqk,qhd->khd", rounded, grad_block, preferred_element_type=jnp.float32
        )
        return ((key_total, value_total), query_grad)

    empty = jnp.zeros((frames, head_count, head_depth), jnp.float32)
    totals, blocks = lax.scan(one_block, (empty, empty), jnp.arange(frames // block_rows))
    query_grad = blocks.reshape(frames, channels)
    key_grad = totals[0].astype(jnp.bfloat16).reshape(frames, channels)
    value_grad = totals[1].astype(jnp.bfloat16).reshape(frames, channels)
    return (query_grad, key_grad, value_grad)


def shards(
    queries,
    key_vecs,
    value_vecs,
    residual_in,
    point_weight,
    context_grad,
    depth_kernel,
    norm_gain,
    norm_bias,
    conv_grad,
):
    head_count = HEADS // lax.axis_size("seq")
    query_heads, key_heads, value_heads = (
        lax.all_to_all(queries, "seq", split_axis=2, concat_axis=1, tiled=True),
        lax.all_to_all(key_vecs, "seq", split_axis=2, concat_axis=1, tiled=True),
        lax.all_to_all(value_vecs, "seq", split_axis=2, concat_axis=1, tiled=True),
    )
    context_local = attend_forward(query_heads[0], key_heads[0], value_heads[0], head_count)
    context_out = lax.all_to_all(
        context_local[None], "seq", split_axis=1, concat_axis=2, tiled=True
    )
    taps = depth_kernel.shape[0]
    channels = depth_kernel.shape[1]
    span = taps - 1
    frames = residual_in.shape[1]
    mixed = (residual_in[0].astype(jnp.float32) + context_out[0].astype(jnp.float32)).astype(
        jnp.bfloat16
    )
    pre_conv = jnp.dot(
        mixed,
        lax.all_gather(point_weight, "seq", axis=0, tiled=True),
        preferred_element_type=jnp.float32,
    )
    conv_input = pre_conv.astype(jnp.bfloat16)[None]
    value_half = conv_input[:, :, :channels].astype(jnp.float32)
    gate_sig = jax.nn.sigmoid(conv_input[:, :, channels:].astype(jnp.float32))
    glu = (value_half * gate_sig).astype(jnp.bfloat16)
    earlier = from_behind(glu[:, frames - span :], "seq", 1)
    glu_wide = jnp.concatenate([earlier, glu], axis=1)
    glu_view = lax.optimization_barrier(glu_wide).astype(jnp.float32)
    depthwise = jnp.zeros((1, frames, channels), jnp.float32)
    for offset in range(taps):
        depthwise = depthwise + depth_kernel[offset] * glu_view[:, offset : offset + frames]
    average = jnp.mean(depthwise, axis=2, keepdims=True)
    centered = depthwise - average
    variance = jnp.mean(centered * centered, axis=2, keepdims=True)
    inverse = lax.rsqrt(variance + 1e-05)
    normed = centered * inverse
    affine = normed * norm_gain + norm_bias
    sig_affine = jax.nn.sigmoid(affine)
    conv_output = (affine * sig_affine).astype(jnp.bfloat16)
    affine_grad = conv_grad.astype(jnp.float32) * (sig_affine * (1.0 + affine * (1.0 - sig_affine)))
    gain_term = jnp.sum(affine_grad * normed, axis=(0, 1))
    bias_term = jnp.sum(affine_grad, axis=(0, 1))
    normed_grad = affine_grad * norm_gain
    depth_grad = inverse * (
        normed_grad
        - jnp.mean(normed_grad, axis=2, keepdims=True)
        - normed * jnp.mean(normed_grad * normed, axis=2, keepdims=True)
    )
    kernel_term = jnp.stack(
        [
            jnp.sum(depth_grad * glu_view[:, offset : offset + frames], axis=(0, 1))
            for offset in range(taps)
        ]
    )
    kernel_total, gain_total, bias_total = lax.psum(
        (kernel_term, gain_term, bias_term), ("dp", "seq")
    )
    recordings = lax.axis_size("dp")
    kernel_grad = kernel_total / recordings
    gain_grad = gain_total / recordings
    bias_grad = bias_total / recordings
    later = from_behind(depth_grad[:, :span], "seq", -1)
    grad_wide = jnp.concatenate([depth_grad, later], axis=1)
    glu_grad = jnp.zeros((1, frames, channels), jnp.float32)
    for offset in range(taps):
        begin = span - offset
        glu_grad = glu_grad + depth_kernel[offset] * grad_wide[:, begin : begin + frames]
    input_grad = jnp.concatenate(
        [glu_grad * gate_sig, glu_grad * value_half * gate_sig * (1.0 - gate_sig)], axis=2
    ).astype(jnp.bfloat16)
    slope_rows = input_grad[0]
    mixed_grad = jnp.einsum(
        "fc,dc->fd",
        slope_rows,
        lax.all_gather(point_weight, "seq", axis=0, tiled=True),
        preferred_element_type=jnp.float32,
    )
    residual_grad = (context_grad.astype(jnp.float32) + mixed_grad[None]).astype(jnp.bfloat16)
    grad_heads = lax.all_to_all(residual_grad, "seq", split_axis=2, concat_axis=1, tiled=True)
    query_grad, key_grad, value_grad = attend_backward(
        query_heads[0], key_heads[0], value_heads[0], grad_heads[0], context_local, head_count
    )
    query_out, key_out, value_out = (
        lax.all_to_all(query_grad[None], "seq", split_axis=1, concat_axis=2, tiled=True),
        lax.all_to_all(key_grad[None], "seq", split_axis=1, concat_axis=2, tiled=True),
        lax.all_to_all(value_grad[None], "seq", split_axis=1, concat_axis=2, tiled=True),
    )
    return (
        context_out,
        conv_output,
        query_out,
        key_out,
        value_out,
        input_grad,
        residual_grad,
        kernel_grad,
        gain_grad,
        bias_grad,
    )


BF = jnp.bfloat16
F32 = jnp.float32
HALO = 32
LANES = 128
TERM_ROWS = 40


HALVES = 2
SEMS = dict(
    send_a=1, send_b=1, send_out=1, send_r1=1, send_r2=1, send_r3=1, z_up_send=3, z_dn_send=3,
    w_send=HALVES, halo1_send=1, halo2_send=1,
    qkv=4, w_y=HALVES, w_mate=1, w_pair=1, z_up=3 * HALVES, z_dn=3 * HALVES, w_x=4 * HALVES,
    ctx_mate=1, ctx_far=1, halo1=1, halo2=1,
    grad=1, red1=1, red2=1, red3=1, outs=1, keep=2, w_self=1, loads=6, ctx_keep=1, out_keep=1,
)


def sem_base(name):
    names = list(SEMS)
    return sum(SEMS[n] for n in names[: names.index(name)])


def fused_kernel(
    dims,
    q_ref, k_ref, v_ref, res_ref, w_ref, cg_ref, taps_hbm, gain_hbm, bias_hbm, og_ref,
    ctx_out, conv_out, dq_out, dk_out, dv_out, ig_out, rg_out, kg_out, gg_out, bg_out,
    q_h, k_h, v_h, g_h, qt, kt, vt, gt, ctxt, ctx_h, prob, pb_s, ds_s, dqt, dq_h, dk_h, dv_h,
    res_v, cg_v, og_v, w_full, pre, mixed, a_s, sig_s, glu_f, dw, ng_s, dg, part, rs_buf, s2_buf, fin,
    taps_ref, gain_ref, bias_ref, hs1, hr1,
    sems,
):
    n_seq, n_dp, rows, channels, taps, depth = dims
    own = channels // n_seq
    pairs = own // LANES
    frames = rows * n_seq
    chunks = channels // LANES
    scaling = depth ** (-0.5)
    line = n_dp // 2
    me = lax.axis_index("seq")
    dp = lax.axis_index("dp")
    core = lax.rem(me, 2)
    mate = me + 1 - 2 * core
    across = lax.rem(me + 2, n_seq)
    diag = lax.rem(mate + 2, n_seq)
    chip = lax.div(me, 2)
    x_pos = lax.rem(dp, 2)
    z_pos = lax.div(dp, 2)
    x_dp = dp + 1 - 2 * x_pos
    peers = [across, diag, mate]
    dp_peers = [lax.rem(dp + d, n_dp) for d in range(1, n_dp)]
    has_up = z_pos < line - 1
    has_down = z_pos > 0

    def sem(name, index=0):
        return sems.at[sem_base(name) + index]

    def local(src, dst, name, index=0):
        copy = pltpu.make_async_copy(src, dst, sem(name, index))
        copy.start()
        return copy

    def remote(src, dst, device, send, recv):
        copy = pltpu.make_async_remote_copy(
            src_ref=src, dst_ref=dst, send_sem=sem(*send), recv_sem=sem(*recv),
            device_id=device, device_id_type=pl.DeviceIdType.MESH,
        )
        copy.start()
        return copy

    def drain(ref, name, index=0):
        pltpu.make_async_copy(ref, ref, sem(name, index)).wait()

    def at(value, size):
        return pl.ds(pl.multiple_of(value * size, size), size)

    barrier = pltpu.get_barrier_semaphore()

    def greet(device):
        pl.semaphore_signal(barrier, inc=1, device_id=device, device_id_type=pl.DeviceIdType.MESH)

    for p in peers:
        greet((dp, p))
    greet((x_dp, me))

    @pl.when(has_up)
    def _():
        greet((dp + 2, me))

    @pl.when(has_down)
    def _():
        greet((dp - 2, me))

    pl.semaphore_wait(barrier, n_seq + has_up.astype(jnp.int32) + has_down.astype(jnp.int32))

    w_rows = w_ref.shape[0]
    part_rows = w_rows // n_dp
    piece = part_rows // HALVES

    def w_piece(owner, x, z, u):
        start = owner * w_rows + (z * 2 + x) * part_rows + u * piece
        return pl.ds(pl.multiple_of(start, piece), piece)

    w_sends = [
        remote(
            w_ref.at[at(dp * HALVES + u, piece), :], w_full.at[w_piece(me, x_pos, z_pos, u), :],
            (dp, across), ("w_send", u), ("w_y", u),
        )
        for u in range(HALVES)
    ]

    def head_cols(owner, pair):
        return pl.ds(pl.multiple_of(owner * own + pair * LANES, LANES), LANES)

    arrays = ((q_ref, q_h), (k_ref, k_h), (v_ref, v_h))

    def send_heads(pair, first, last):
        pc = slice(pair * LANES, (pair + 1) * LANES)
        for t in range(first, last):
            src, dst = arrays[t]
            for p in peers:
                remote(
                    src.at[:, head_cols(p, pair)], dst.at[at(me, rows), pc], (dp, p),
                    ("send_a",), ("qkv", 2 * pair + min(t, 1)),
                )

    def pass_on(x, z, u):
        here = w_full.at[w_piece(across, x, z, u), :]
        remote(here, here, (dp, mate), ("send_a",), ("w_pair",))

    def pass_x(z, u):
        here = w_full.at[w_piece(across, x_pos, z, u), :]
        remote(here, here, (x_dp, me), ("send_a",), ("w_x", z * HALVES + u))

    def pass_up(z, step, u):
        here = w_full.at[w_piece(across, x_pos, z, u), :]
        remote(here, here, (dp + 2, me), ("z_up_send", step), ("z_up", step * HALVES + u))

    def pass_down(z, step, u):
        here = w_full.at[w_piece(across, x_pos, z, u), :]
        remote(here, here, (dp - 2, me), ("z_dn_send", step), ("z_dn", step * HALVES + u))

    def w_first(u):
        drain(w_full.at[w_piece(across, x_pos, z_pos, u), :], "w_y", u)

        @pl.when(has_up)
        def _():
            pass_up(z_pos, 0, u)

        @pl.when(has_down)
        def _():
            pass_down(z_pos, 0, u)

        pass_x(z_pos, u)
        pass_on(x_pos, z_pos, u)

    def w_step(step, u):
        @pl.when(z_pos >= step)
        def _():
            z = z_pos - step
            drain(w_full.at[w_piece(across, x_pos, z, u), :], "z_up", (step - 1) * HALVES + u)
            if step < line - 1:
                @pl.when(has_up)
                def _():
                    pass_up(z, step, u)
            pass_x(z, u)
            pass_on(x_pos, z, u)

        @pl.when(z_pos + step < line)
        def _():
            z = z_pos + step
            drain(w_full.at[w_piece(across, x_pos, z, u), :], "z_dn", (step - 1) * HALVES + u)
            if step < line - 1:
                @pl.when(has_down)
                def _():
                    pass_down(z, step, u)
            pass_x(z, u)
            pass_on(x_pos, z, u)

    def w_across_x():
        for z in range(line):
            for u in range(HALVES):
                drain(w_full.at[w_piece(across, 1 - x_pos, z, u), :], "w_x", z * HALVES + u)
                pass_on(1 - x_pos, z, u)

    def flip(value):
        return value.astype(F32).T

    q_block = 2 * rows

    def forward_head(h, b):
        hr = slice(h * depth, (h + 1) * depth)
        cols = at(b, q_block)
        scores = jnp.dot(k_h[:, hr], qt[hr, cols], preferred_element_type=F32)
        shifted = jnp.exp(scores - jnp.max(scores, axis=0, keepdims=True))
        p = shifted * (1.0 / jnp.sum(shifted, axis=0, keepdims=True))
        rounded = p.astype(BF)
        prob[h, :, cols] = p
        pb_s[h, :, cols] = rounded
        ctxt[hr, cols] = jnp.dot(vt[hr, :], rounded, preferred_element_type=F32).astype(BF)

    def send_rows(src, dst, pair, p, send, recv):
        source = slice(pair * LANES, (pair + 1) * LANES)
        remote(src.at[at(p, rows), source], dst.at[:, head_cols(me, pair)], (dp, p), send, recv)

    def keep_rows(src, dst, pair, name):
        source = slice(pair * LANES, (pair + 1) * LANES)
        local(src.at[at(me, rows), source], dst.at[:, head_cols(me, pair)], name)

    def send_out(src, dst, pair):
        for p in peers:
            send_rows(src, dst, pair, p, ("send_out",), ("outs",))
        keep_rows(src, dst, pair, "out_keep")

    def queries_in(pair):
        pc = slice(pair * LANES, (pair + 1) * LANES)
        drain(k_h.at[0 : 3 * rows, 0:LANES], "qkv", 2 * pair)
        drain(k_h.at[0 : 3 * rows, 0:LANES], "keep", pair)
        qt[pc, :] = (flip(q_h[:, pc]) * scaling).astype(BF)

    def values_in(pair):
        pc = slice(pair * LANES, (pair + 1) * LANES)
        drain(k_h.at[0 : 3 * rows, 0 : 2 * LANES], "qkv", 2 * pair + 1)
        vt[pc, :] = flip(v_h[:, pc]).astype(BF)

    def attend(pair, b):
        pc = slice(pair * LANES, (pair + 1) * LANES)
        forward_head(2 * pair, b)
        forward_head(2 * pair + 1, b)
        ctx_h[at(b, q_block), pc] = flip(ctxt[pc, at(b, q_block)]).astype(BF)

    def attend_far(pair):
        attend(pair, 1 - chip)
        send_rows(ctx_h, ctx_out, pair, across, ("send_a",), ("ctx_far",))
        send_rows(ctx_h, ctx_out, pair, diag, ("send_a",), ("ctx_far",))

    def attend_near(pair):
        attend(pair, chip)
        send_rows(ctx_h, ctx_out, pair, mate, ("send_a",), ("ctx_mate",))
        keep_rows(ctx_h, ctx_out, pair, "ctx_keep")

    w_sends[0].wait_send()
    send_heads(0, 0, 1)
    w_first(0)
    w_sends[1].wait_send()
    send_heads(0, 1, 3)
    for pair in range(pairs):
        pc = slice(pair * LANES, (pair + 1) * LANES)
        for src, dst in arrays:
            local(src.at[:, head_cols(me, pair)], dst.at[at(me, rows), pc], "keep", pair)
    w_first(1)
    loads = [
        local(src, dst, "loads", t)
        for t, (src, dst) in enumerate(
            ((res_ref, res_v), (cg_ref, cg_v), (og_ref, og_v), (taps_hbm, taps_ref), (gain_hbm, gain_ref), (bias_hbm, bias_ref))
        )
    ]
    w_self = local(w_ref, w_full.at[at(me, w_rows), :], "w_self")
    w_step(1, 0)
    queries_in(0)
    w_step(1, 1)
    send_heads(1, 0, 3)
    remote(w_ref, w_full.at[at(me, w_rows), :], (dp, mate), ("send_a",), ("w_mate",))
    values_in(0)
    attend_far(0)
    w_step(2, 0)
    w_step(2, 1)
    attend_near(0)
    queries_in(1)
    w_step(3, 0)
    values_in(1)
    attend_far(1)
    w_step(3, 1)
    attend_near(1)

    for pair in range(pairs):
        pc = slice(pair * LANES, (pair + 1) * LANES)
        kt[pc, :] = flip(k_h[:, pc]).astype(BF)
    loads[0].wait()
    w_self.wait()
    drain(w_full.at[at(mate, w_rows), :], "w_mate")
    drain(ctx_h.at[0:rows, :], "ctx_keep")
    drain(ctx_h.at[0:rows, :], "ctx_mate")
    near = at(chip, 2 * own)
    far = at(1 - chip, 2 * own)
    wide = 2 * LANES
    mixed[:, near] = (res_v[:, near].astype(F32) + ctx_out[:, near].astype(F32)).astype(BF)

    def conv_near(i, carry):
        cols = at(i, 2 * wide)
        pre[:, cols] = jnp.dot(mixed[:, near], w_full[near, cols], preferred_element_type=F32)
        return carry

    lax.fori_loop(0, channels // wide, conv_near, 0)
    w_across_x()
    drain(ctx_h.at[0 : 2 * rows, :], "ctx_far")
    mixed[:, far] = (res_v[:, far].astype(F32) + ctx_out[:, far].astype(F32)).astype(BF)
    drain(w_full.at[at(diag, w_rows), :], "w_pair")

    def conv_in(i, carry):
        cols = at(i, wide)
        gates = pl.ds(pl.multiple_of(channels + i * wide, wide), wide)
        a = jnp.dot(mixed[:, far], w_full[far, cols], preferred_element_type=F32)
        b = jnp.dot(mixed[:, far], w_full[far, gates], preferred_element_type=F32)
        a = (a + pre[:, cols]).astype(BF)
        b = (b + pre[:, gates]).astype(BF)
        sig = jax.nn.sigmoid(b.astype(F32))
        a_s[:, cols] = a
        sig_s[:, cols] = sig
        rounded = (a.astype(F32) * sig).astype(BF)
        glu = rounded.astype(F32)
        for half in range(2):
            lanes = slice(half * LANES, (half + 1) * LANES)
            glu_f[2 * i + half, HALO : HALO + rows, :] = glu[:, lanes]
            hs1[2 * i + half] = rounded[rows - HALO :, lanes]
        return carry

    lax.fori_loop(0, channels // wide, conv_in, 0)
    @pl.when(me < n_seq - 1)
    def _():
        remote(hs1, hr1, (dp, me + 1), ("halo1_send",), ("halo1",))

    for copy in loads[2:]:
        copy.wait()
    span = taps - 1
    base = HALO - span

    def norm_rows(first, count, unroll):
        here = slice(first, first + count)
        zero = jnp.zeros((count, LANES), F32)

        def conv(c, total):
            lanes = at(c, LANES)
            acc = zero
            for o in range(taps):
                low = base + first + o
                acc = acc + taps_ref[o : o + 1, lanes] * glu_f[c, low : low + count, :]
            dw[c, here, :] = acc
            return total + acc

        total = lax.fori_loop(0, chunks, conv, zero)
        average = jnp.sum(total, axis=1, keepdims=True) * (1.0 / channels)

        def squares(c, total):
            centered = dw[c, here, :] - average
            return total + centered * centered

        total = lax.fori_loop(0, chunks, squares, zero, unroll=unroll)
        variance = jnp.sum(total, axis=1, keepdims=True) * (1.0 / channels)
        inverse = lax.rsqrt(variance + 1e-05)

        def norm_step(c, carry):
            s1, s2 = carry
            lanes = at(c, LANES)
            normed = (dw[c, here, :] - average) * inverse
            affine = normed * gain_ref[:, lanes] + bias_ref[:, lanes]
            sig = jax.nn.sigmoid(affine)
            conv_out[here, lanes] = (affine * sig).astype(BF)
            affine_grad = og_v[here, lanes].astype(F32) * (sig * (1.0 + affine * (1.0 - sig)))
            gain_term = jnp.sum(affine_grad * normed, axis=0, keepdims=True)
            bias_term = jnp.sum(affine_grad, axis=0, keepdims=True)
            if first == 0:
                gain_term = gain_term + part[c, taps : taps + 1, :]
                bias_term = bias_term + part[c, taps + 1 : taps + 2, :]
            part[c, taps : taps + 1, :] = gain_term
            part[c, taps + 1 : taps + 2, :] = bias_term
            normed_grad = affine_grad * gain_ref[:, lanes]
            dw[c, here, :] = normed
            ng_s[c, here, :] = normed_grad
            return s1 + normed_grad, s2 + normed_grad * normed

        s1, s2 = lax.fori_loop(0, chunks, norm_step, (zero, zero), unroll=unroll)
        m1 = jnp.sum(s1, axis=1, keepdims=True) * (1.0 / channels)
        m2 = jnp.sum(s2, axis=1, keepdims=True) * (1.0 / channels)

        def depth_grad_step(c, carry):
            grad = inverse * (ng_s[c, here, :] - m1 - dw[c, here, :] * m2)
            dg[c, here, :] = grad
            return carry

        lax.fori_loop(0, chunks, depth_grad_step, 0, unroll=unroll)

    norm_rows(HALO, rows - HALO, 1)
    @pl.when(me > 0)
    def _():
        drain(hr1, "halo1")
        glu_f[:, 0:HALO, :] = hr1[...].astype(F32)

    @pl.when(me == 0)
    def _():
        glu_f[:, 0:HALO, :] = jnp.zeros((chunks, HALO, LANES), F32)

    norm_rows(0, HALO, chunks)
    tail = dg.at[:, rows : rows + HALO, :]

    @pl.when(me > 0)
    def _():
        remote(dg.at[:, 0:HALO, :], tail, (dp, me - 1), ("halo2_send",), ("halo2",))

    def glu_back(first, count):
        def body(c, carry):
            lanes = at(c, LANES)
            gates = pl.ds(pl.multiple_of(channels + c * LANES, LANES), LANES)
            here = slice(first, first + count)
            acc = jnp.zeros((count, LANES), F32)
            for o in range(taps):
                low = first + span - o
                acc = acc + taps_ref[o : o + 1, lanes] * dg[c, low : low + count, :]
            sig = sig_s[here, lanes]
            ig_out[here, lanes] = (acc * sig).astype(BF)
            slope = acc * a_s[here, lanes].astype(F32) * sig * (1.0 - sig)
            ig_out[here, gates] = slope.astype(BF)
            return carry

        lax.fori_loop(0, chunks, body, 0)

    def tap_grad(c, carry):
        grad = dg[c, 0:rows, :]
        for o in range(taps):
            part[c, o : o + 1, :] = jnp.sum(
                grad * glu_f[c, base + o : base + o + rows, :], axis=0, keepdims=True
            )
        part[c, taps + 2 : TERM_ROWS, :] = jnp.zeros((TERM_ROWS - taps - 2, LANES), F32)
        return carry

    lax.fori_loop(0, chunks, tap_grad, 0)
    for d, p in enumerate(dp_peers):
        remote(part.at[p], rs_buf.at[d], (p, me), ("send_r1",), ("red1",))
    glu_back(0, rows - HALO)

    @pl.when(me < n_seq - 1)
    def _():
        drain(tail, "halo2")

    @pl.when(me == n_seq - 1)
    def _():
        tail[...] = jnp.zeros((chunks, HALO, LANES), F32)

    glu_back(rows - HALO, HALO)
    loads[1].wait()
    for p in peers + [me]:
        cols = at(p, own)
        grad = lax.dot_general(
            ig_out[...], w_full[cols, :], (((1,), (1,)), ((), ())), preferred_element_type=F32
        )
        rg_out[:, cols] = (cg_v[:, cols].astype(F32) + grad).astype(BF)
        if p is me:
            g_h[at(me, rows), :] = rg_out[:, cols]
        else:
            remote(rg_out.at[:, cols], g_h.at[at(me, rows), :], (dp, p), ("send_b",), ("grad",))

    drain(rs_buf, "red1")
    total = part[dp]
    for d in range(n_dp - 1):
        total = total + rs_buf[d]
    s2_buf[me] = total
    for p in peers:
        remote(s2_buf.at[me], s2_buf.at[me], (dp, p), ("send_r2",), ("red2",))

    drain(q_h.at[0 : 3 * rows, :], "grad")

    def backward_head(h, b):
        hr = slice(h * depth, (h + 1) * depth)
        cols = at(b, q_block)
        grad = gt[hr, cols]
        dots = jnp.sum(grad.astype(F32) * ctxt[hr, cols].astype(F32), axis=0, keepdims=True)
        prob_grad = jnp.dot(v_h[:, hr], grad, preferred_element_type=F32)
        score_grad = (prob[h, :, cols] * (prob_grad - dots) * scaling).astype(BF)
        ds_s[h % 2, :, cols] = score_grad
        dqt[hr, cols] = jnp.dot(kt[hr, :], score_grad, preferred_element_type=F32)

    first_head = lax.broadcasted_iota(jnp.int32, (frames, LANES), 1) < depth
    for pair in range(pairs):
        pc = slice(pair * LANES, (pair + 1) * LANES)
        left = jnp.dot(pb_s[2 * pair], g_h[:, pc], preferred_element_type=F32)
        right = jnp.dot(pb_s[2 * pair + 1], g_h[:, pc], preferred_element_type=F32)
        dv_h[:, pc] = jnp.where(first_head, left, right).astype(BF)
        send_out(dv_h, dv_out, pair)
        gt[pc, :] = flip(g_h[:, pc]).astype(BF)

    for pair in range(pairs):
        pc = slice(pair * LANES, (pair + 1) * LANES)
        for b in (1 - chip, chip):
            backward_head(2 * pair, b)
            backward_head(2 * pair + 1, b)
        dq_h[:, pc] = dqt[pc, :].T.astype(BF)
        send_out(dq_h, dq_out, pair)
        left = jnp.dot(ds_s[0], q_h[:, pc], preferred_element_type=F32)
        right = jnp.dot(ds_s[1], q_h[:, pc], preferred_element_type=F32)
        dk_h[:, pc] = jnp.where(first_head, left, right).astype(BF)
        send_out(dk_h, dk_out, pair)
        if pair == 0:
            drain(s2_buf.at[0 : n_seq - 1], "red2")
            total = s2_buf[0]
            for s in range(1, n_seq):
                total = total + s2_buf[s]
            fin[dp] = total * (1.0 / n_dp)
            for p in dp_peers:
                remote(fin.at[dp], fin.at[dp], (p, me), ("send_r3",), ("red3",))

    wide_rows = 2 * channels
    count = 2 * w_rows + line * part_rows + 12 * pairs * rows * LANES // wide_rows
    drain(w_full.at[0:count, :], "send_a")
    drain(rs_buf, "send_r1")
    drain(s2_buf.at[0 : n_seq - 1], "send_r2")

    for step in range(line - 1):
        @pl.when(jnp.logical_and(has_up, z_pos >= step))
        def _():
            drain(w_full.at[0:part_rows, :], "z_up_send", step)

        @pl.when(jnp.logical_and(has_down, z_pos + step < line))
        def _():
            drain(w_full.at[0:part_rows, :], "z_dn_send", step)

    @pl.when(me < n_seq - 1)
    def _():
        drain(hr1, "halo1_send")

    @pl.when(me > 0)
    def _():
        drain(tail, "halo2_send")

    drain(rs_buf, "red3")
    for c in range(chunks):
        lanes = slice(c * LANES, (c + 1) * LANES)
        kg_out[:, lanes] = fin[c, 0:taps, :]
        gg_out[:, lanes] = fin[c, taps : taps + 1, :]
        bg_out[:, lanes] = fin[c, taps + 1 : taps + 2, :]
    drain(rs_buf, "send_r3")
    drain(w_full.at[0 : 3 * pairs * rows * LANES // wide_rows, :], "out_keep")
    drain(w_full.at[0 : 9 * pairs * rows * LANES // wide_rows, :], "outs")
    drain(w_full.at[0 : 9 * pairs * rows * LANES // wide_rows, :], "send_out")
    drain(w_full.at[0 : 3 * rows * own // wide_rows, :], "send_b")


def place_outputs(*refs):
    sems = refs[20]
    copies = [pltpu.make_async_copy(refs[i], refs[10 + i], sems.at[i]) for i in range(10)]
    for copy in copies:
        copy.start()
    for copy in copies:
        copy.wait()


def fused_shards(
    queries, key_vecs, value_vecs, residual_in, point_weight, context_grad, depth_kernel,
    norm_gain, norm_bias, conv_grad,
):
    n_seq = lax.axis_size("seq")
    n_dp = lax.axis_size("dp")
    rows, channels = queries.shape[1:]
    taps = depth_kernel.shape[0]
    depth = channels // HEADS
    frames = rows * n_seq
    own = channels // n_seq
    heads = own // depth
    chunks = channels // LANES
    s = jax.ShapeDtypeStruct
    vm = pltpu.VMEM
    block = s((rows, channels), BF)
    head_rows = vm((frames, own), BF)
    head_cols = vm((own, frames), BF)
    scratch = (
        [head_rows] * 4 + [head_cols] * 5 + [head_rows]
        + [vm((heads, frames, frames), F32), vm((heads, frames, frames), BF), vm((2, frames, frames), BF)]
        + [vm((own, frames), F32)] + [head_rows] * 3
        + [
            vm((rows, channels), BF),
            vm((rows, channels), BF),
            vm((rows, channels), BF),
            vm((channels, 2 * channels), BF),
            vm((rows, 2 * channels), F32),
            vm((rows, channels), BF),
            vm((rows, channels), BF),
            vm((rows, channels), F32),
            vm((chunks, HALO + rows, LANES), F32),
            vm((chunks, rows, LANES), F32),
            vm((chunks, rows, LANES), F32),
            vm((chunks, rows + HALO, LANES), F32),
            vm((chunks, TERM_ROWS, LANES), F32),
            vm((n_dp - 1, TERM_ROWS, LANES), F32),
            vm((n_seq, TERM_ROWS, LANES), F32),
            vm((chunks, TERM_ROWS, LANES), F32),
            vm((taps, channels), F32),
            vm((1, channels), F32),
            vm((1, channels), F32),
            vm((chunks, HALO, LANES), BF),
            vm((chunks, HALO, LANES), BF),
            pltpu.SemaphoreType.DMA((sum(SEMS.values()),)),
        ]
    )
    spec = pl.BlockSpec(memory_space=pltpu.VMEM)
    hbm = pl.BlockSpec(memory_space=pl.ANY)
    outs = pl.pallas_call(
        functools.partial(fused_kernel, (n_seq, n_dp, rows, channels, taps, depth)),
        out_shape=(
            block, block, block, block, block, s((rows, 2 * channels), BF), block,
            s((taps, channels), F32), s((1, channels), F32), s((1, channels), F32),
        ),
        in_specs=[hbm] * 10,
        out_specs=(spec,) * 10,
        scratch_shapes=scratch,
        compiler_params=pltpu.CompilerParams(
            collective_id=0, has_side_effects=True, vmem_limit_bytes=56 * 1024 * 1024
        ),
    )(
        queries[0], key_vecs[0], value_vecs[0], residual_in[0], point_weight, context_grad[0],
        depth_kernel, norm_gain[None], norm_bias[None], conv_grad[0],
    )
    outs = pl.pallas_call(
        place_outputs,
        out_shape=tuple(s(o.shape, o.dtype) for o in outs),
        in_specs=[spec] * 10,
        out_specs=(hbm,) * 10,
        scratch_shapes=[pltpu.SemaphoreType.DMA((10,))],
    )(*outs)
    return tuple(o[None] for o in outs[:7]) + (outs[7], outs[8][0], outs[9][0])


def chosen(*args):
    n_seq = lax.axis_size("seq")
    n_dp = lax.axis_size("dp")
    recs, rows, channels = args[0].shape
    fits = (
        n_seq == 4
        and recs == 1
        and rows % 128 == 0
        and channels % (LANES * n_seq) == 0
        and 2 * channels == LANES * HEADS
        and channels // LANES == n_dp
        and rows * n_seq <= 512
        and args[4].shape[0] == channels // n_seq == 2 * LANES
        and args[6].shape[0] <= 31
    )
    return fused_shards(*args) if fits else shards(*args)


def solution(mesh):
    in_specs = (
        P("dp", "seq", None),
        P("dp", "seq", None),
        P("dp", "seq", None),
        P("dp", "seq", None),
        P("seq", None),
        P("dp", "seq", None),
        P(),
        P(),
        P(),
        P("dp", "seq", None),
    )
    out_specs = (
        P("dp", "seq", None),
        P("dp", "seq", None),
        P("dp", "seq", None),
        P("dp", "seq", None),
        P("dp", "seq", None),
        P("dp", "seq", None),
        P("dp", "seq", None),
        P(),
        P(),
        P(),
    )
    return jax.shard_map(chosen, mesh=mesh, in_specs=in_specs, out_specs=out_specs, check_vma=False)
```

```python
import functools
import jax
import jax.numpy as jnp
from jax import lax
from jax.sharding import PartitionSpec as P
from jax.experimental import pallas as pl
from jax.experimental.pallas import tpu as pltpu

HEADS = 16


def from_behind(block, axis, distance):
    devices = range(lax.axis_size(axis))
    route = [(i - distance, i) for i in devices if i - distance in devices]
    return lax.ppermute(block, axis, route)


def block_probs(query_block, key_heads, scaling):
    scores = (
        jnp.einsum("qhd,khd->hqk", query_block, key_heads, preferred_element_type=jnp.float32)
        * scaling
    )
    shifted = jnp.exp(scores - jnp.max(scores, axis=2, keepdims=True))
    return shifted / jnp.sum(shifted, axis=2, keepdims=True)


def attend_forward(query_part, key_part, value_part, head_count):
    frames, channels = query_part.shape
    head_depth = channels // head_count
    scaling = head_depth ** (-0.5)
    query_heads = query_part.reshape(frames, head_count, head_depth)
    key_heads = key_part.reshape(frames, head_count, head_depth)
    value_heads = value_part.reshape(frames, head_count, head_depth)
    block_rows = min(512, frames)

    def one_block(running, index):
        query_block = lax.dynamic_slice_in_dim(query_heads, index * block_rows, block_rows, 0)
        rounded = block_probs(query_block, key_heads, scaling).astype(jnp.bfloat16)
        context = jnp.einsum(
            "hqk,khd->qhd", rounded, value_heads, preferred_element_type=jnp.float32
        ).astype(jnp.bfloat16)
        return (running, context)

    unused, blocks = lax.scan(
        one_block, jnp.zeros((), jnp.float32), jnp.arange(frames // block_rows)
    )
    return blocks.reshape(frames, channels)


def attend_backward(query_part, key_part, value_part, grad_part, context_part, head_count):
    frames, channels = query_part.shape
    head_depth = channels // head_count
    scaling = head_depth ** (-0.5)
    query_heads = query_part.reshape(frames, head_count, head_depth)
    key_heads = key_part.reshape(frames, head_count, head_depth)
    value_heads = value_part.reshape(frames, head_count, head_depth)
    grad_heads = grad_part.reshape(frames, head_count, head_depth)
    context_heads = context_part.reshape(frames, head_count, head_depth)
    block_rows = min(512, frames)

    def one_block(running, index):
        key_total, value_total = running
        start = index * block_rows
        query_block = lax.dynamic_slice_in_dim(query_heads, start, block_rows, 0)
        grad_block = lax.dynamic_slice_in_dim(grad_heads, start, block_rows, 0)
        context_block = lax.dynamic_slice_in_dim(context_heads, start, block_rows, 0)
        probabilities = block_probs(query_block, key_heads, scaling)
        rounded = probabilities.astype(jnp.bfloat16)
        row_dots = jnp.sum(
            grad_block.astype(jnp.float32) * context_block.astype(jnp.float32), axis=2
        )
        prob_grad = jnp.einsum(
            "qhd,khd->hqk", grad_block, value_heads, preferred_element_type=jnp.float32
        )
        score_grad = (probabilities * (prob_grad - row_dots.T[:, :, None]) * scaling).astype(
            jnp.bfloat16
        )
        query_grad = jnp.einsum(
            "hqk,khd->qhd", score_grad, key_heads, preferred_element_type=jnp.float32
        ).astype(jnp.bfloat16)
        key_total = key_total + jnp.einsum(
            "hqk,qhd->khd", score_grad, query_block, preferred_element_type=jnp.float32
        )
        value_total = value_total + jnp.einsum(
            "hqk,qhd->khd", rounded, grad_block, preferred_element_type=jnp.float32
        )
        return ((key_total, value_total), query_grad)

    empty = jnp.zeros((frames, head_count, head_depth), jnp.float32)
    totals, blocks = lax.scan(one_block, (empty, empty), jnp.arange(frames // block_rows))
    query_grad = blocks.reshape(frames, channels)
    key_grad = totals[0].astype(jnp.bfloat16).reshape(frames, channels)
    value_grad = totals[1].astype(jnp.bfloat16).reshape(frames, channels)
    return (query_grad, key_grad, value_grad)


def shards(
    queries,
    key_vecs,
    value_vecs,
    residual_in,
    point_weight,
    context_grad,
    depth_kernel,
    norm_gain,
    norm_bias,
    conv_grad,
):
    head_count = HEADS // lax.axis_size("seq")
    query_heads, key_heads, value_heads = (
        lax.all_to_all(queries, "seq", split_axis=2, concat_axis=1, tiled=True),
        lax.all_to_all(key_vecs, "seq", split_axis=2, concat_axis=1, tiled=True),
        lax.all_to_all(value_vecs, "seq", split_axis=2, concat_axis=1, tiled=True),
    )
    context_local = attend_forward(query_heads[0], key_heads[0], value_heads[0], head_count)
    context_out = lax.all_to_all(
        context_local[None], "seq", split_axis=1, concat_axis=2, tiled=True
    )
    taps = depth_kernel.shape[0]
    channels = depth_kernel.shape[1]
    span = taps - 1
    frames = residual_in.shape[1]
    mixed = (residual_in[0].astype(jnp.float32) + context_out[0].astype(jnp.float32)).astype(
        jnp.bfloat16
    )
    pre_conv = jnp.dot(
        mixed,
        lax.all_gather(point_weight, "seq", axis=0, tiled=True),
        preferred_element_type=jnp.float32,
    )
    conv_input = pre_conv.astype(jnp.bfloat16)[None]
    value_half = conv_input[:, :, :channels].astype(jnp.float32)
    gate_sig = jax.nn.sigmoid(conv_input[:, :, channels:].astype(jnp.float32))
    glu = (value_half * gate_sig).astype(jnp.bfloat16)
    earlier = from_behind(glu[:, frames - span :], "seq", 1)
    glu_wide = jnp.concatenate([earlier, glu], axis=1)
    glu_view = lax.optimization_barrier(glu_wide).astype(jnp.float32)
    depthwise = jnp.zeros((1, frames, channels), jnp.float32)
    for offset in range(taps):
        depthwise = depthwise + depth_kernel[offset] * glu_view[:, offset : offset + frames]
    average = jnp.mean(depthwise, axis=2, keepdims=True)
    centered = depthwise - average
    variance = jnp.mean(centered * centered, axis=2, keepdims=True)
    inverse = lax.rsqrt(variance + 1e-05)
    normed = centered * inverse
    affine = normed * norm_gain + norm_bias
    sig_affine = jax.nn.sigmoid(affine)
    conv_output = (affine * sig_affine).astype(jnp.bfloat16)
    affine_grad = conv_grad.astype(jnp.float32) * (sig_affine * (1.0 + affine * (1.0 - sig_affine)))
    gain_term = jnp.sum(affine_grad * normed, axis=(0, 1))
    bias_term = jnp.sum(affine_grad, axis=(0, 1))
    normed_grad = affine_grad * norm_gain
    depth_grad = inverse * (
        normed_grad
        - jnp.mean(normed_grad, axis=2, keepdims=True)
        - normed * jnp.mean(normed_grad * normed, axis=2, keepdims=True)
    )
    kernel_term = jnp.stack(
        [
            jnp.sum(depth_grad * glu_view[:, offset : offset + frames], axis=(0, 1))
            for offset in range(taps)
        ]
    )
    kernel_total, gain_total, bias_total = lax.psum(
        (kernel_term, gain_term, bias_term), ("dp", "seq")
    )
    recordings = lax.axis_size("dp")
    kernel_grad = kernel_total / recordings
    gain_grad = gain_total / recordings
    bias_grad = bias_total / recordings
    later = from_behind(depth_grad[:, :span], "seq", -1)
    grad_wide = jnp.concatenate([depth_grad, later], axis=1)
    glu_grad = jnp.zeros((1, frames, channels), jnp.float32)
    for offset in range(taps):
        begin = span - offset
        glu_grad = glu_grad + depth_kernel[offset] * grad_wide[:, begin : begin + frames]
    input_grad = jnp.concatenate(
        [glu_grad * gate_sig, glu_grad * value_half * gate_sig * (1.0 - gate_sig)], axis=2
    ).astype(jnp.bfloat16)
    slope_rows = input_grad[0]
    mixed_grad = jnp.einsum(
        "fc,dc->fd",
        slope_rows,
        lax.all_gather(point_weight, "seq", axis=0, tiled=True),
        preferred_element_type=jnp.float32,
    )
    residual_grad = (context_grad.astype(jnp.float32) + mixed_grad[None]).astype(jnp.bfloat16)
    grad_heads = lax.all_to_all(residual_grad, "seq", split_axis=2, concat_axis=1, tiled=True)
    query_grad, key_grad, value_grad = attend_backward(
        query_heads[0], key_heads[0], value_heads[0], grad_heads[0], context_local, head_count
    )
    query_out, key_out, value_out = (
        lax.all_to_all(query_grad[None], "seq", split_axis=1, concat_axis=2, tiled=True),
        lax.all_to_all(key_grad[None], "seq", split_axis=1, concat_axis=2, tiled=True),
        lax.all_to_all(value_grad[None], "seq", split_axis=1, concat_axis=2, tiled=True),
    )
    return (
        context_out,
        conv_output,
        query_out,
        key_out,
        value_out,
        input_grad,
        residual_grad,
        kernel_grad,
        gain_grad,
        bias_grad,
    )


BF = jnp.bfloat16
F32 = jnp.float32
HALO = 32
LANES = 128
TERM_ROWS = 40


SEMS = dict(
    send_a=1, send_kv=4, send_b=1, send_out=1, send_stats=1, send_r1=1, send_r2=1, send_r3=1,
    w_send=2, halo1_send=1, halo2_send=1,
    near=1, kv=4, q_far=1, w_y=2, w_mate=1, w_pair=1, w_z=3, w_x=3, ctx_mate=4, halo1=1, halo2=1,
    grad_near=2, grad_far=2, stats=2, red1=1, red2=1, red3=1, outs=1, keep=1, w_self=1, loads=6,
    ctx_keep=4, out_keep=1,
)


def sem_base(name):
    names = list(SEMS)
    return sum(SEMS[n] for n in names[: names.index(name)])


def fused_kernel(
    dims,
    q_ref, k_ref, v_ref, res_ref, w_ref, cg_ref, taps_hbm, gain_hbm, bias_hbm, og_ref,
    ctx_out, conv_out, dq_out, dk_out, dv_out, ig_out, rg_out, kg_out, gg_out, bg_out,
    q_h, k_h, v_h, g_h, qt, kt, vt, gt, ctxt, ctx_h, prob, p_f, pb_s, ds_s, dqt, dq_h, dk_h, dv_h,
    stat_s, stat_r,
    res_v, cg_v, og_v, w_full, pre, mixed, a_s, sig_s, glu_f, dw, ng_s, dg, part, rs_buf, s2_buf, fin,
    taps_ref, gain_ref, bias_ref, hs1, hr1,
    sems, token,
):
    n_seq, n_dp, rows, channels, taps, depth = dims
    own = channels // 2
    pairs = own // LANES
    frames = rows * n_seq
    block = 2 * rows
    chunks = channels // LANES
    scaling = depth ** (-0.5)
    line = n_dp // 2
    me = lax.axis_index("seq")
    dp = lax.axis_index("dp")
    core = lax.rem(me, 2)
    mate = me + 1 - 2 * core
    across = lax.rem(me + 2, n_seq)
    diag = lax.rem(mate + 2, n_seq)
    x_pos = lax.rem(dp, 2)
    z_pos = lax.div(dp, 2)
    x_dp = dp + 1 - 2 * x_pos
    peers = [across, diag, mate]
    chip = lax.div(me, 2)
    other = 2 * (1 - chip)
    dp_peers = [lax.rem(dp + d, n_dp) for d in range(1, n_dp)]
    has_up = z_pos < line - 1
    has_down = z_pos > 0

    def sem(name, index=0):
        return sems.at[sem_base(name) + index]

    def local(src, dst, name, index=0):
        copy = pltpu.make_async_copy(src, dst, sem(name, index))
        copy.start()
        return copy

    def remote(src, dst, device, send, recv):
        copy = pltpu.make_async_remote_copy(
            src_ref=src, dst_ref=dst, send_sem=sem(*send), recv_sem=sem(*recv),
            device_id=device, device_id_type=pl.DeviceIdType.MESH,
        )
        copy.start()
        return copy

    def drain(ref, name, index=0):
        pltpu.make_async_copy(ref, ref, sem(name, index)).wait()

    def at(value, size):
        return pl.ds(pl.multiple_of(value * size, size), size)

    barrier = pltpu.get_barrier_semaphore()

    def greet(device):
        pl.semaphore_signal(barrier, inc=1, device_id=device, device_id_type=pl.DeviceIdType.MESH)

    for p in peers:
        greet((dp, p))
    greet((x_dp, me))

    @pl.when(has_up)
    def _():
        greet((dp + 2, me))

    @pl.when(has_down)
    def _():
        greet((dp - 2, me))

    pl.semaphore_wait(barrier, n_seq + has_up.astype(jnp.int32) + has_down.astype(jnp.int32))

    w_rows = w_ref.shape[0]
    piece = w_rows // 8
    z_odd = lax.rem(z_pos, 2)
    z_dp = dp + 2 - 4 * z_odd

    def w_piece(owner, x, z, u):
        start = owner * w_rows + (4 * z + 2 * x + u) * piece
        return pl.ds(pl.multiple_of(start, piece), piece)

    w_sends = [
        remote(
            w_ref.at[at(4 * z_odd + 2 * x_pos + u, piece), :],
            w_full.at[w_piece(me, x_pos, z_odd, u), :],
            (dp, across), ("w_send", u), ("w_y", u),
        )
        for u in range(2)
    ]

    def tell(step):
        @pl.when(has_up)
        def _():
            pl.semaphore_signal(
                token.at[2 * step], inc=1, device_id=(dp + 2, me),
                device_id_type=pl.DeviceIdType.MESH,
            )

        @pl.when(has_down)
        def _():
            pl.semaphore_signal(
                token.at[2 * step + 1], inc=1, device_id=(dp - 2, me),
                device_id_type=pl.DeviceIdType.MESH,
            )

    def told(step):
        @pl.when(has_down)
        def _():
            pl.semaphore_wait(token.at[2 * step], 1)

        @pl.when(has_up)
        def _():
            pl.semaphore_wait(token.at[2 * step + 1], 1)

    tell(0)

    def head_cols(owner, pair):
        return pl.ds(pl.multiple_of(owner * own + pair * LANES, LANES), LANES)

    spot = at(core, rows)
    far_spot = pl.ds(pl.multiple_of(block + core * rows, rows), rows)

    def half_cols(half):
        return pl.ds(pl.multiple_of(half * own, own), own)

    for src, dst in ((q_ref, q_h), (k_ref, k_h), (v_ref, v_h)):
        remote(src.at[:, half_cols(1 - core)], dst.at[spot, :], (dp, mate), ("send_a",), ("near",))
        local(src.at[:, half_cols(core)], dst.at[spot, :], "keep")

    def send_far(src, dst, pair, send, recv):
        pc = slice(pair * LANES, (pair + 1) * LANES)
        for half in range(2):
            cols = slice(half * own + pair * LANES, half * own + (pair + 1) * LANES)
            remote(src.at[:, cols], dst.at[far_spot, pc], (dp, other + half), send, recv)

    def send_kv(pair):
        send_far(k_ref, k_h, pair, ("send_kv", pair), ("kv", pair))
        send_far(v_ref, v_h, pair, ("send_kv", pair), ("kv", pair))

    def sent_kv(pair):
        drain(w_full.at[0 : 4 * rows * LANES // (2 * channels), :], "send_kv", pair)

    def w_take(x, z, u, name, index, *onward):
        here = w_full.at[w_piece(across, x, z, u), :]
        drain(here, name, index)
        for device, to_name, to_index in onward:
            remote(here, here, (device, me), ("send_a",), (to_name, to_index))
        remote(here, here, (dp, mate), ("send_a",), ("w_pair",))

    z_other, x_other = 1 - z_odd, 1 - x_pos

    def flip(value):
        return value.astype(F32).T

    def attend(pair):
        heads = (2 * pair, 2 * pair + 1)
        for h in heads:
            hr = slice(h * depth, (h + 1) * depth)
            scores = jnp.dot(k_h[:, hr], qt[hr, 0:block], preferred_element_type=F32)
            prob[h] = scores
            stat_s[0, h : h + 1, :] = jnp.max(scores, axis=0, keepdims=True)
        for h in heads:
            shifted = jnp.exp(prob[h] - stat_s[0, h : h + 1, :])
            prob[h] = shifted
            stat_s[1, h : h + 1, :] = 1.0 / jnp.sum(shifted, axis=0, keepdims=True)
        for h in heads:
            hr = slice(h * depth, (h + 1) * depth)
            p = prob[h] * stat_s[1, h : h + 1, :]
            rounded = p.astype(BF)
            prob[h] = p
            pb_s[h, :, 0:block] = rounded[0:block]
            ctxt[hr, :] = jnp.dot(vt[hr, :], rounded, preferred_element_type=F32).astype(BF)
        pc = slice(pair * LANES, (pair + 1) * LANES)
        ctx_h[:, pc] = flip(ctxt[pc, :]).astype(BF)
        send_rows(ctx_h, ctx_out, pair, ("send_a",), ("ctx_mate", pair))
        keep_rows(ctx_h, ctx_out, pair, "ctx_keep", pair)

    def send_rows(src, dst, pair, send, recv):
        source = slice(pair * LANES, (pair + 1) * LANES)
        remote(src.at[at(1 - core, rows), source], dst.at[:, head_cols(core, pair)], (dp, mate), send, recv)

    def keep_rows(src, dst, pair, name, index=0):
        source = slice(pair * LANES, (pair + 1) * LANES)
        local(src.at[spot, source], dst.at[:, head_cols(core, pair)], name, index)

    def send_out(src, dst, pair):
        send_rows(src, dst, pair, ("send_out",), ("outs",))
        keep_rows(src, dst, pair, "out_keep")

    def values_in(pair):
        pc = slice(pair * LANES, (pair + 1) * LANES)
        drain(w_full.at[0 : 4 * rows * LANES // (2 * channels), :], "kv", pair)
        vt[pc, block:] = flip(v_h[block:, pc]).astype(BF)

    w_sends[0].wait_send()
    w_sends[1].wait_send()
    send_kv(0)
    send_kv(1)
    w_take(x_pos, z_odd, 0, "w_y", 0, (z_dp, "w_z", 0), (x_dp, "w_x", 0))
    loads = [
        local(src, dst, "loads", t)
        for t, (src, dst) in enumerate(
            ((res_ref, res_v), (cg_ref, cg_v), (og_ref, og_v), (taps_hbm, taps_ref), (gain_hbm, gain_ref), (bias_hbm, bias_ref))
        )
    ]
    w_self = local(w_ref, w_full.at[at(me, w_rows), :], "w_self")
    w_take(x_pos, z_odd, 1, "w_y", 1, (x_dp, "w_x", 1), (z_dp, "w_z", 1))
    told(0)
    tell(1)
    drain(w_full.at[0 : 3 * rows * own // (2 * channels), :], "near")
    drain(w_full.at[0 : 3 * rows * own // (2 * channels), :], "keep")
    for pair in range(pairs):
        pc = slice(pair * LANES, (pair + 1) * LANES)
        qt[pc, 0:block] = (flip(q_h[0:block, pc]) * scaling).astype(BF)
        vt[pc, 0:block] = flip(v_h[0:block, pc]).astype(BF)
    w_take(x_pos, z_other, 0, "w_z", 0, (x_dp, "w_x", 2))
    sent_kv(0)
    send_kv(2)
    remote(w_ref, w_full.at[at(me, w_rows), :], (dp, mate), ("send_a",), ("w_mate",))
    values_in(0)
    attend(0)
    w_take(x_other, z_odd, 0, "w_x", 0)
    w_take(x_other, z_odd, 1, "w_x", 1, (z_dp, "w_z", 2))
    told(1)
    tell(2)
    sent_kv(1)
    send_kv(3)
    values_in(1)
    attend(1)
    w_take(x_pos, z_other, 1, "w_z", 1)
    w_take(x_other, z_other, 0, "w_x", 2)
    sent_kv(2)
    for pair in range(pairs):
        send_far(q_ref, q_h, pair, ("send_a",), ("q_far",))
    values_in(2)
    attend(2)
    told(2)
    w_take(x_other, z_other, 1, "w_z", 2)
    values_in(3)
    attend(3)
    stats = (dp, across)
    remote(stat_s.at[0:2], stat_r.at[0:2], stats, ("send_stats",), ("stats", 0))

    for pair in range(pairs):
        pc = slice(pair * LANES, (pair + 1) * LANES)
        kt[pc, :] = flip(k_h[:, pc]).astype(BF)
    loads[0].wait()
    w_self.wait()
    drain(w_full.at[at(mate, w_rows), :], "w_mate")
    drain(w_full.at[at(diag, w_rows), :], "w_pair")
    wide = 2 * LANES
    spans = [
        [slice(o * own + pair * LANES, o * own + (pair + 1) * LANES) for o in range(2)]
        for pair in range(pairs)
    ]

    def mix(pair):
        drain(ctx_h.at[0:rows, 0:LANES], "ctx_keep", pair)
        drain(ctx_h.at[0:rows, 0:LANES], "ctx_mate", pair)
        for n, cols in enumerate(spans[pair]):
            both = res_v[:, cols].astype(F32) + ctx_out[:, cols].astype(F32)
            mixed[:, (pair * 2 + n) * LANES : (pair * 2 + n + 1) * LANES] = both.astype(BF)

    def weigh(some, cols):
        weights = jnp.concatenate([w_full[r, cols] for pair in some for r in spans[pair]], axis=0)
        lanes = slice(some[0] * 2 * LANES, (some[-1] + 1) * 2 * LANES)
        return jnp.dot(mixed[:, lanes], weights, preferred_element_type=F32)

    early, late = range(pairs - 1), range(pairs - 1, pairs)
    for pair in early:
        mix(pair)

    def conv_first(i, carry):
        cols = at(i, 2 * wide)
        pre[:, cols] = weigh(early, cols)
        return carry

    lax.fori_loop(0, channels // wide, conv_first, 0)
    mix(pairs - 1)

    for i in range(channels // wide):
        cols = slice(i * wide, (i + 1) * wide)
        gates = slice(channels + i * wide, channels + (i + 1) * wide)
        a = (weigh(late, cols) + pre[:, cols]).astype(BF)
        b = (weigh(late, gates) + pre[:, gates]).astype(BF)
        sig = jax.nn.sigmoid(b.astype(F32))
        a_s[:, cols] = a
        sig_s[:, cols] = sig
        rounded = (a.astype(F32) * sig).astype(BF)
        glu = rounded.astype(F32)
        for half in range(2):
            lanes = slice(half * LANES, (half + 1) * LANES)
            glu_f[2 * i + half, HALO : HALO + rows, :] = glu[:, lanes]
            hs1[2 * i + half] = rounded[rows - HALO :, lanes]
        two = slice(2 * i, 2 * i + 2)

        @pl.when(me < n_seq - 1)
        def _():
            remote(hs1.at[two], hr1.at[two], (dp, me + 1), ("halo1_send",), ("halo1",))

    for copy in loads[2:]:
        copy.wait()
    span = taps - 1
    base = HALO - span

    def norm_rows(first, count, unroll):
        here = slice(first, first + count)
        zero = jnp.zeros((count, LANES), F32)

        def conv(c, total):
            lanes = at(c, LANES)
            acc = zero
            for o in range(taps):
                low = base + first + o
                acc = acc + taps_ref[o : o + 1, lanes] * glu_f[c, low : low + count, :]
            dw[c, here, :] = acc
            return total + acc

        total = lax.fori_loop(0, chunks, conv, zero)
        average = jnp.sum(total, axis=1, keepdims=True) * (1.0 / channels)

        def squares(c, total):
            centered = dw[c, here, :] - average
            return total + centered * centered

        total = lax.fori_loop(0, chunks, squares, zero, unroll=unroll)
        variance = jnp.sum(total, axis=1, keepdims=True) * (1.0 / channels)
        inverse = lax.rsqrt(variance + 1e-05)

        def norm_step(c, carry):
            s1, s2 = carry
            lanes = at(c, LANES)
            normed = (dw[c, here, :] - average) * inverse
            affine = normed * gain_ref[:, lanes] + bias_ref[:, lanes]
            sig = jax.nn.sigmoid(affine)
            conv_out[here, lanes] = (affine * sig).astype(BF)
            affine_grad = og_v[here, lanes].astype(F32) * (sig * (1.0 + affine * (1.0 - sig)))
            gain_term = jnp.sum(affine_grad * normed, axis=0, keepdims=True)
            bias_term = jnp.sum(affine_grad, axis=0, keepdims=True)
            if first == 0:
                gain_term = gain_term + part[c, taps : taps + 1, :]
                bias_term = bias_term + part[c, taps + 1 : taps + 2, :]
            part[c, taps : taps + 1, :] = gain_term
            part[c, taps + 1 : taps + 2, :] = bias_term
            normed_grad = affine_grad * gain_ref[:, lanes]
            dw[c, here, :] = normed
            ng_s[c, here, :] = normed_grad
            return s1 + normed_grad, s2 + normed_grad * normed

        s1, s2 = lax.fori_loop(0, chunks, norm_step, (zero, zero), unroll=unroll)
        m1 = jnp.sum(s1, axis=1, keepdims=True) * (1.0 / channels)
        m2 = jnp.sum(s2, axis=1, keepdims=True) * (1.0 / channels)

        def depth_grad_step(c, carry):
            grad = inverse * (ng_s[c, here, :] - m1 - dw[c, here, :] * m2)
            dg[c, here, :] = grad
            return carry

        lax.fori_loop(0, chunks, depth_grad_step, 0, unroll=unroll)

    norm_rows(HALO, rows - HALO, 1)
    @pl.when(me > 0)
    def _():
        drain(hr1, "halo1")
        glu_f[:, 0:HALO, :] = hr1[...].astype(F32)

    @pl.when(me == 0)
    def _():
        glu_f[:, 0:HALO, :] = jnp.zeros((chunks, HALO, LANES), F32)

    norm_rows(0, HALO, chunks)
    tail = dg.at[:, rows : rows + HALO, :]

    @pl.when(me > 0)
    def _():
        remote(dg.at[:, 0:HALO, :], tail, (dp, me - 1), ("halo2_send",), ("halo2",))

    def glu_back(first, count):
        def body(c, carry):
            lanes = at(c, LANES)
            gates = pl.ds(pl.multiple_of(channels + c * LANES, LANES), LANES)
            here = slice(first, first + count)
            acc = jnp.zeros((count, LANES), F32)
            for o in range(taps):
                low = first + span - o
                acc = acc + taps_ref[o : o + 1, lanes] * dg[c, low : low + count, :]
            sig = sig_s[here, lanes]
            ig_out[here, lanes] = (acc * sig).astype(BF)
            slope = acc * a_s[here, lanes].astype(F32) * sig * (1.0 - sig)
            ig_out[here, gates] = slope.astype(BF)
            return carry

        lax.fori_loop(0, chunks, body, 0)

    def tap_grad(c, carry):
        grad = dg[c, 0:rows, :]
        for o in range(taps):
            part[c, o : o + 1, :] = jnp.sum(
                grad * glu_f[c, base + o : base + o + rows, :], axis=0, keepdims=True
            )
        part[c, taps + 2 : TERM_ROWS, :] = jnp.zeros((TERM_ROWS - taps - 2, LANES), F32)
        return carry

    lax.fori_loop(0, chunks, tap_grad, 0)
    for d, p in enumerate(dp_peers):
        remote(part.at[p], rs_buf.at[d], (p, me), ("send_r1",), ("red1",))
    glu_back(0, rows - HALO)

    @pl.when(me < n_seq - 1)
    def _():
        drain(tail, "halo2")

    @pl.when(me == n_seq - 1)
    def _():
        tail[...] = jnp.zeros((chunks, HALO, LANES), F32)

    glu_back(rows - HALO, HALO)
    loads[1].wait()
    quad = 2 * LANES
    behind = z_pos >= line // 2

    def grad_away(half, step):
        cols = pl.ds(pl.multiple_of(half * own + step * quad, quad), quad)
        within = slice(step * quad, (step + 1) * quad)
        remote(
            rg_out.at[:, cols], g_h.at[far_spot, within], (dp, other + half),
            ("send_b",), ("grad_far", step),
        )

    for step in range(pairs // 2):
        within = slice(step * quad, (step + 1) * quad)
        for half, mine in ((core, True), (1 - core, False)):
            cols = pl.ds(pl.multiple_of(half * own + step * quad, quad), quad)
            grad = lax.dot_general(
                ig_out[...], w_full[cols, :], (((1,), (1,)), ((), ())), preferred_element_type=F32
            )
            rg_out[:, cols] = (cg_v[:, cols].astype(F32) + grad).astype(BF)
            if step == 0:
                grad_away(half, step)
            else:
                pl.when(jnp.logical_not(behind))(functools.partial(grad_away, half, step))
            if mine:
                g_h[spot, within] = rg_out[:, cols]
            else:
                remote(
                    rg_out.at[:, cols], g_h.at[spot, within], (dp, mate), ("send_b",), ("grad_near", step)
                )

    def sum_recordings():
        drain(rs_buf, "red1")
        total = part[dp]
        for d in range(n_dp - 1):
            total = total + rs_buf[d]
        s2_buf[me] = total
        for p in peers:
            remote(s2_buf.at[me], s2_buf.at[me], (dp, p), ("send_r2",), ("red2",))

    def sum_frames():
        drain(s2_buf.at[0 : n_seq - 1], "red2")
        total = s2_buf[0]
        for s in range(1, n_seq):
            total = total + s2_buf[s]
        fin[dp] = total * (1.0 / n_dp)
        for p in dp_peers:
            remote(fin.at[dp], fin.at[dp], (p, me), ("send_r3",), ("red3",))

    @pl.when(behind)
    def _():
        sum_recordings()
        for half in (core, 1 - core):
            grad_away(half, pairs // 2 - 1)

    drain(w_full.at[0 : 2 * pairs * rows * LANES // (2 * channels), :], "q_far")
    drain(stat_r.at[0:2], "stats", 0)
    for pair in range(pairs):
        pc = slice(pair * LANES, (pair + 1) * LANES)
        qt[pc, block:] = (flip(q_h[block:, pc]) * scaling).astype(BF)
        for h in (2 * pair, 2 * pair + 1):
            hr = slice(h * depth, (h + 1) * depth)
            p_f[h] = jnp.dot(k_h[0:block, hr], qt[hr, block:], preferred_element_type=F32)
        for h in (2 * pair, 2 * pair + 1):
            p = jnp.exp(p_f[h] - stat_r[0, h : h + 1, :]) * stat_r[1, h : h + 1, :]
            p_f[h] = p
            pb_s[h, :, block:] = p.astype(BF)

    pl.when(jnp.logical_not(behind))(sum_recordings)
    for step in range(pairs // 2):
        drain(g_h.at[0:rows, 0:quad], "grad_near", step)
    for pair in range(pairs):
        pc = slice(pair * LANES, (pair + 1) * LANES)
        gt[pc, 0:block] = flip(g_h[0:block, pc]).astype(BF)
        for h in (2 * pair, 2 * pair + 1):
            hr = slice(h * depth, (h + 1) * depth)
            both = gt[hr, 0:block].astype(F32) * ctxt[hr, :].astype(F32)
            stat_s[2, h : h + 1, :] = jnp.sum(both, axis=0, keepdims=True)
    remote(stat_s.at[2:3], stat_r.at[2:3], stats, ("send_stats",), ("stats", 1))

    for pair in range(pairs):
        pc = slice(pair * LANES, (pair + 1) * LANES)
        for h in (2 * pair, 2 * pair + 1):
            hr = slice(h * depth, (h + 1) * depth)
            prob_grad = jnp.dot(v_h[:, hr], gt[hr, 0:block], preferred_element_type=F32)
            score_grad = (prob[h] * (prob_grad - stat_s[2, h : h + 1, :]) * scaling).astype(BF)
            ds_s[h, :, 0:block] = score_grad[0:block]
            dqt[hr, :] = jnp.dot(kt[hr, :], score_grad, preferred_element_type=F32)
        dq_h[:, pc] = dqt[pc, :].T.astype(BF)
        send_out(dq_h, dq_out, pair)
        if pair == 1:
            pl.when(behind)(sum_frames)

    pl.when(jnp.logical_not(behind))(sum_frames)
    drain(stat_r.at[2:3], "stats", 1)
    first_head = lax.broadcasted_iota(jnp.int32, (block, LANES), 1) < depth
    for pair in range(pairs):
        pc = slice(pair * LANES, (pair + 1) * LANES)
        if pair % 2 == 0:
            drain(g_h.at[0:block, 0:quad], "grad_far", pair // 2)
        gt[pc, block:] = flip(g_h[block:, pc]).astype(BF)
        for h in (2 * pair, 2 * pair + 1):
            hr = slice(h * depth, (h + 1) * depth)
            prob_grad = jnp.dot(v_h[0:block, hr], gt[hr, block:], preferred_element_type=F32)
            score_grad = p_f[h] * (prob_grad - stat_r[2, h : h + 1, :]) * scaling
            ds_s[h, :, block:] = score_grad.astype(BF)
        left = jnp.dot(pb_s[2 * pair], g_h[:, pc], preferred_element_type=F32)
        right = jnp.dot(pb_s[2 * pair + 1], g_h[:, pc], preferred_element_type=F32)
        dv_h[:, pc] = jnp.where(first_head, left, right).astype(BF)
        send_out(dv_h, dv_out, pair)
        left = jnp.dot(ds_s[2 * pair], q_h[:, pc], preferred_element_type=F32)
        right = jnp.dot(ds_s[2 * pair + 1], q_h[:, pc], preferred_element_type=F32)
        dk_h[:, pc] = jnp.where(first_head, left, right).astype(BF)
        send_out(dk_h, dk_out, pair)

    wide_rows = 2 * channels
    count = 2 * w_rows + 6 * piece + 6 * pairs * rows * LANES // wide_rows
    drain(w_full.at[0:count, :], "send_a")
    sent_kv(pairs - 1)
    drain(stat_r, "send_stats")
    drain(rs_buf, "send_r1")
    drain(s2_buf.at[0 : n_seq - 1], "send_r2")

    @pl.when(me < n_seq - 1)
    def _():
        drain(hr1, "halo1_send")

    @pl.when(me > 0)
    def _():
        drain(tail, "halo2_send")

    drain(rs_buf, "red3")
    for c in range(chunks):
        lanes = slice(c * LANES, (c + 1) * LANES)
        kg_out[:, lanes] = fin[c, 0:taps, :]
        gg_out[:, lanes] = fin[c, taps : taps + 1, :]
        bg_out[:, lanes] = fin[c, taps + 1 : taps + 2, :]
    drain(rs_buf, "send_r3")
    drain(w_full.at[0 : 3 * pairs * rows * LANES // wide_rows, :], "out_keep")
    drain(w_full.at[0 : 3 * pairs * rows * LANES // wide_rows, :], "outs")
    drain(w_full.at[0 : 3 * pairs * rows * LANES // wide_rows, :], "send_out")
    drain(w_full.at[0 : 3 * rows * own // wide_rows, :], "send_b")


def place_outputs(*refs):
    sems = refs[20]
    copies = [pltpu.make_async_copy(refs[i], refs[10 + i], sems.at[i]) for i in range(10)]
    for copy in copies:
        copy.start()
    for copy in copies:
        copy.wait()


def fused_shards(
    queries, key_vecs, value_vecs, residual_in, point_weight, context_grad, depth_kernel,
    norm_gain, norm_bias, conv_grad,
):
    n_seq = lax.axis_size("seq")
    n_dp = lax.axis_size("dp")
    rows, channels = queries.shape[1:]
    taps = depth_kernel.shape[0]
    depth = channels // HEADS
    frames = rows * n_seq
    own = channels // n_seq
    heads = own // depth
    chunks = channels // LANES
    s = jax.ShapeDtypeStruct
    vm = pltpu.VMEM
    block = s((rows, channels), BF)
    half = channels // 2
    block_rows = 2 * rows
    heads = HEADS // 2
    all_rows = vm((frames, half), BF)
    all_cols = vm((half, frames), BF)
    some_rows = vm((block_rows, half), BF)
    scratch = (
        [all_rows] * 4 + [all_cols] * 4 + [vm((half, block_rows), BF), some_rows]
        + [vm((heads, frames, block_rows), F32), vm((heads, block_rows, block_rows), F32)]
        + [vm((heads, block_rows, frames), BF)] * 2
        + [vm((half, block_rows), F32)] + [some_rows] * 3
        + [vm((3, heads, block_rows), F32)] * 2
        + [
            vm((rows, channels), BF),
            vm((rows, channels), BF),
            vm((rows, channels), BF),
            vm((channels, 2 * channels), BF),
            vm((rows, 2 * channels), F32),
            vm((rows, channels), BF),
            vm((rows, channels), BF),
            vm((rows, channels), F32),
            vm((chunks, HALO + rows, LANES), F32),
            vm((chunks, rows, LANES), F32),
            vm((chunks, rows, LANES), F32),
            vm((chunks, rows + HALO, LANES), F32),
            vm((chunks, TERM_ROWS, LANES), F32),
            vm((n_dp - 1, TERM_ROWS, LANES), F32),
            vm((n_seq, TERM_ROWS, LANES), F32),
            vm((chunks, TERM_ROWS, LANES), F32),
            vm((taps, channels), F32),
            vm((1, channels), F32),
            vm((1, channels), F32),
            vm((chunks, HALO, LANES), BF),
            vm((chunks, HALO, LANES), BF),
            pltpu.SemaphoreType.DMA((sum(SEMS.values()),)),
            pltpu.SemaphoreType.REGULAR((6,)),
        ]
    )
    spec = pl.BlockSpec(memory_space=pltpu.VMEM)
    hbm = pl.BlockSpec(memory_space=pl.ANY)
    outs = pl.pallas_call(
        functools.partial(fused_kernel, (n_seq, n_dp, rows, channels, taps, depth)),
        out_shape=(
            block, block, block, block, block, s((rows, 2 * channels), BF), block,
            s((taps, channels), F32), s((1, channels), F32), s((1, channels), F32),
        ),
        in_specs=[hbm] * 10,
        out_specs=(spec,) * 10,
        scratch_shapes=scratch,
        compiler_params=pltpu.CompilerParams(
            collective_id=0, has_side_effects=True, vmem_limit_bytes=56 * 1024 * 1024
        ),
    )(
        queries[0], key_vecs[0], value_vecs[0], residual_in[0], point_weight, context_grad[0],
        depth_kernel, norm_gain[None], norm_bias[None], conv_grad[0],
    )
    outs = pl.pallas_call(
        place_outputs,
        out_shape=tuple(s(o.shape, o.dtype) for o in outs),
        in_specs=[spec] * 10,
        out_specs=(hbm,) * 10,
        scratch_shapes=[pltpu.SemaphoreType.DMA((10,))],
    )(*outs)
    return tuple(o[None] for o in outs[:7]) + (outs[7], outs[8][0], outs[9][0])


def chosen(*args):
    n_seq = lax.axis_size("seq")
    n_dp = lax.axis_size("dp")
    recs, rows, channels = args[0].shape
    fits = (
        n_seq == 4
        and recs == 1
        and rows % 128 == 0
        and channels % (LANES * n_seq) == 0
        and 2 * channels == LANES * HEADS
        and channels // LANES == n_dp
        and rows * n_seq <= 512
        and args[4].shape[0] == channels // n_seq == 2 * LANES
        and args[6].shape[0] <= 31
    )
    return fused_shards(*args) if fits else shards(*args)


def solution(mesh):
    in_specs = (
        P("dp", "seq", None),
        P("dp", "seq", None),
        P("dp", "seq", None),
        P("dp", "seq", None),
        P("seq", None),
        P("dp", "seq", None),
        P(),
        P(),
        P(),
        P("dp", "seq", None),
    )
    out_specs = (
        P("dp", "seq", None),
        P("dp", "seq", None),
        P("dp", "seq", None),
        P("dp", "seq", None),
        P("dp", "seq", None),
        P("dp", "seq", None),
        P("dp", "seq", None),
        P(),
        P(),
        P(),
    )
    return jax.shard_map(chosen, mesh=mesh, in_specs=in_specs, out_specs=out_specs, check_vma=False)
```

```python
import functools
import jax
import jax.numpy as jnp
from jax import lax
from jax.sharding import PartitionSpec as P
from jax.experimental import pallas as pl
from jax.experimental.pallas import tpu as pltpu

HEADS = 16


def from_behind(block, axis, distance):
    devices = range(lax.axis_size(axis))
    route = [(i - distance, i) for i in devices if i - distance in devices]
    return lax.ppermute(block, axis, route)


def block_probs(query_block, key_heads, scaling):
    scores = (
        jnp.einsum("qhd,khd->hqk", query_block, key_heads, preferred_element_type=jnp.float32)
        * scaling
    )
    shifted = jnp.exp(scores - jnp.max(scores, axis=2, keepdims=True))
    return shifted / jnp.sum(shifted, axis=2, keepdims=True)


def attend_forward(query_part, key_part, value_part, head_count):
    frames, channels = query_part.shape
    head_depth = channels // head_count
    scaling = head_depth ** (-0.5)
    query_heads = query_part.reshape(frames, head_count, head_depth)
    key_heads = key_part.reshape(frames, head_count, head_depth)
    value_heads = value_part.reshape(frames, head_count, head_depth)
    block_rows = min(512, frames)

    def one_block(running, index):
        query_block = lax.dynamic_slice_in_dim(query_heads, index * block_rows, block_rows, 0)
        rounded = block_probs(query_block, key_heads, scaling).astype(jnp.bfloat16)
        context = jnp.einsum(
            "hqk,khd->qhd", rounded, value_heads, preferred_element_type=jnp.float32
        ).astype(jnp.bfloat16)
        return (running, context)

    unused, blocks = lax.scan(
        one_block, jnp.zeros((), jnp.float32), jnp.arange(frames // block_rows)
    )
    return blocks.reshape(frames, channels)


def attend_backward(query_part, key_part, value_part, grad_part, context_part, head_count):
    frames, channels = query_part.shape
    head_depth = channels // head_count
    scaling = head_depth ** (-0.5)
    query_heads = query_part.reshape(frames, head_count, head_depth)
    key_heads = key_part.reshape(frames, head_count, head_depth)
    value_heads = value_part.reshape(frames, head_count, head_depth)
    grad_heads = grad_part.reshape(frames, head_count, head_depth)
    context_heads = context_part.reshape(frames, head_count, head_depth)
    block_rows = min(512, frames)

    def one_block(running, index):
        key_total, value_total = running
        start = index * block_rows
        query_block = lax.dynamic_slice_in_dim(query_heads, start, block_rows, 0)
        grad_block = lax.dynamic_slice_in_dim(grad_heads, start, block_rows, 0)
        context_block = lax.dynamic_slice_in_dim(context_heads, start, block_rows, 0)
        probabilities = block_probs(query_block, key_heads, scaling)
        rounded = probabilities.astype(jnp.bfloat16)
        row_dots = jnp.sum(
            grad_block.astype(jnp.float32) * context_block.astype(jnp.float32), axis=2
        )
        prob_grad = jnp.einsum(
            "qhd,khd->hqk", grad_block, value_heads, preferred_element_type=jnp.float32
        )
        score_grad = (probabilities * (prob_grad - row_dots.T[:, :, None]) * scaling).astype(
            jnp.bfloat16
        )
        query_grad = jnp.einsum(
            "hqk,khd->qhd", score_grad, key_heads, preferred_element_type=jnp.float32
        ).astype(jnp.bfloat16)
        key_total = key_total + jnp.einsum(
            "hqk,qhd->khd", score_grad, query_block, preferred_element_type=jnp.float32
        )
        value_total = value_total + jnp.einsum(
            "hqk,qhd->khd", rounded, grad_block, preferred_element_type=jnp.float32
        )
        return ((key_total, value_total), query_grad)

    empty = jnp.zeros((frames, head_count, head_depth), jnp.float32)
    totals, blocks = lax.scan(one_block, (empty, empty), jnp.arange(frames // block_rows))
    query_grad = blocks.reshape(frames, channels)
    key_grad = totals[0].astype(jnp.bfloat16).reshape(frames, channels)
    value_grad = totals[1].astype(jnp.bfloat16).reshape(frames, channels)
    return (query_grad, key_grad, value_grad)


def shards(
    queries,
    key_vecs,
    value_vecs,
    residual_in,
    point_weight,
    context_grad,
    depth_kernel,
    norm_gain,
    norm_bias,
    conv_grad,
):
    head_count = HEADS // lax.axis_size("seq")
    query_heads, key_heads, value_heads = (
        lax.all_to_all(queries, "seq", split_axis=2, concat_axis=1, tiled=True),
        lax.all_to_all(key_vecs, "seq", split_axis=2, concat_axis=1, tiled=True),
        lax.all_to_all(value_vecs, "seq", split_axis=2, concat_axis=1, tiled=True),
    )
    context_local = attend_forward(query_heads[0], key_heads[0], value_heads[0], head_count)
    context_out = lax.all_to_all(
        context_local[None], "seq", split_axis=1, concat_axis=2, tiled=True
    )
    taps = depth_kernel.shape[0]
    channels = depth_kernel.shape[1]
    span = taps - 1
    frames = residual_in.shape[1]
    mixed = (residual_in[0].astype(jnp.float32) + context_out[0].astype(jnp.float32)).astype(
        jnp.bfloat16
    )
    pre_conv = jnp.dot(
        mixed,
        lax.all_gather(point_weight, "seq", axis=0, tiled=True),
        preferred_element_type=jnp.float32,
    )
    conv_input = pre_conv.astype(jnp.bfloat16)[None]
    value_half = conv_input[:, :, :channels].astype(jnp.float32)
    gate_sig = jax.nn.sigmoid(conv_input[:, :, channels:].astype(jnp.float32))
    glu = (value_half * gate_sig).astype(jnp.bfloat16)
    earlier = from_behind(glu[:, frames - span :], "seq", 1)
    glu_wide = jnp.concatenate([earlier, glu], axis=1)
    glu_view = lax.optimization_barrier(glu_wide).astype(jnp.float32)
    depthwise = jnp.zeros((1, frames, channels), jnp.float32)
    for offset in range(taps):
        depthwise = depthwise + depth_kernel[offset] * glu_view[:, offset : offset + frames]
    average = jnp.mean(depthwise, axis=2, keepdims=True)
    centered = depthwise - average
    variance = jnp.mean(centered * centered, axis=2, keepdims=True)
    inverse = lax.rsqrt(variance + 1e-05)
    normed = centered * inverse
    affine = normed * norm_gain + norm_bias
    sig_affine = jax.nn.sigmoid(affine)
    conv_output = (affine * sig_affine).astype(jnp.bfloat16)
    affine_grad = conv_grad.astype(jnp.float32) * (sig_affine * (1.0 + affine * (1.0 - sig_affine)))
    gain_term = jnp.sum(affine_grad * normed, axis=(0, 1))
    bias_term = jnp.sum(affine_grad, axis=(0, 1))
    normed_grad = affine_grad * norm_gain
    depth_grad = inverse * (
        normed_grad
        - jnp.mean(normed_grad, axis=2, keepdims=True)
        - normed * jnp.mean(normed_grad * normed, axis=2, keepdims=True)
    )
    kernel_term = jnp.stack(
        [
            jnp.sum(depth_grad * glu_view[:, offset : offset + frames], axis=(0, 1))
            for offset in range(taps)
        ]
    )
    kernel_total, gain_total, bias_total = lax.psum(
        (kernel_term, gain_term, bias_term), ("dp", "seq")
    )
    recordings = lax.axis_size("dp")
    kernel_grad = kernel_total / recordings
    gain_grad = gain_total / recordings
    bias_grad = bias_total / recordings
    later = from_behind(depth_grad[:, :span], "seq", -1)
    grad_wide = jnp.concatenate([depth_grad, later], axis=1)
    glu_grad = jnp.zeros((1, frames, channels), jnp.float32)
    for offset in range(taps):
        begin = span - offset
        glu_grad = glu_grad + depth_kernel[offset] * grad_wide[:, begin : begin + frames]
    input_grad = jnp.concatenate(
        [glu_grad * gate_sig, glu_grad * value_half * gate_sig * (1.0 - gate_sig)], axis=2
    ).astype(jnp.bfloat16)
    slope_rows = input_grad[0]
    mixed_grad = jnp.einsum(
        "fc,dc->fd",
        slope_rows,
        lax.all_gather(point_weight, "seq", axis=0, tiled=True),
        preferred_element_type=jnp.float32,
    )
    residual_grad = (context_grad.astype(jnp.float32) + mixed_grad[None]).astype(jnp.bfloat16)
    grad_heads = lax.all_to_all(residual_grad, "seq", split_axis=2, concat_axis=1, tiled=True)
    query_grad, key_grad, value_grad = attend_backward(
        query_heads[0], key_heads[0], value_heads[0], grad_heads[0], context_local, head_count
    )
    query_out, key_out, value_out = (
        lax.all_to_all(query_grad[None], "seq", split_axis=1, concat_axis=2, tiled=True),
        lax.all_to_all(key_grad[None], "seq", split_axis=1, concat_axis=2, tiled=True),
        lax.all_to_all(value_grad[None], "seq", split_axis=1, concat_axis=2, tiled=True),
    )
    return (
        context_out,
        conv_output,
        query_out,
        key_out,
        value_out,
        input_grad,
        residual_grad,
        kernel_grad,
        gain_grad,
        bias_grad,
    )


BF = jnp.bfloat16
F32 = jnp.float32
HALO = 32
LANES = 128
TERM_ROWS = 40


SEMS = dict(
    send_a=1, send_kv=4, send_b=1, send_out=1, send_stats=1, send_r1=1, send_r2=1, send_r3=1,
    w_send=2, halo1_send=1, halo2_send=1,
    near=1, kv=4, q_far=1, w_y=2, w_mate=1, w_pair=1, w_z=3, w_x=3, ctx_mate=4, halo1=1, halo2=1,
    grad_near=2, grad_far=2, stats=3, red1=1, red2=1, red3=1, outs=1, keep=1, w_self=1, loads=6,
    ctx_keep=4, out_keep=1,
)


def sem_base(name):
    names = list(SEMS)
    return sum(SEMS[n] for n in names[: names.index(name)])


def fused_kernel(
    dims,
    q_ref, k_ref, v_ref, res_ref, w_ref, cg_ref, taps_hbm, gain_hbm, bias_hbm, og_ref,
    ctx_out, conv_out, dq_out, dk_out, dv_out, ig_out, rg_out, kg_out, gg_out, bg_out,
    q_h, k_h, v_h, g_h, qt, kt, vt, gt, ctxt, ctx_h, prob, p_f, pb_s, ds_s, dqt, dq_h, dk_h, dv_h,
    ds_f, stat_s, stat_r,
    res_v, cg_v, og_v, w_full, pre, mixed, a_s, sig_s, glu_f, dw, ng_s, dg, part, rs_buf, s2_buf, fin,
    taps_ref, gain_ref, bias_ref, hs1, hr1,
    sems, token,
):
    n_seq, n_dp, rows, channels, taps, depth = dims
    own = channels // 2
    pairs = own // LANES
    frames = rows * n_seq
    block = 2 * rows
    chunks = channels // LANES
    scaling = depth ** (-0.5)
    line = n_dp // 2
    me = lax.axis_index("seq")
    dp = lax.axis_index("dp")
    core = lax.rem(me, 2)
    mate = me + 1 - 2 * core
    across = lax.rem(me + 2, n_seq)
    diag = lax.rem(mate + 2, n_seq)
    x_pos = lax.rem(dp, 2)
    z_pos = lax.div(dp, 2)
    x_dp = dp + 1 - 2 * x_pos
    peers = [across, diag, mate]
    chip = lax.div(me, 2)
    other = 2 * (1 - chip)
    dp_peers = [lax.rem(dp + d, n_dp) for d in range(1, n_dp)]
    has_up = z_pos < line - 1
    has_down = z_pos > 0

    def sem(name, index=0):
        return sems.at[sem_base(name) + index]

    def local(src, dst, name, index=0):
        copy = pltpu.make_async_copy(src, dst, sem(name, index))
        copy.start()
        return copy

    def remote(src, dst, device, send, recv):
        copy = pltpu.make_async_remote_copy(
            src_ref=src, dst_ref=dst, send_sem=sem(*send), recv_sem=sem(*recv),
            device_id=device, device_id_type=pl.DeviceIdType.MESH,
        )
        copy.start()
        return copy

    def drain(ref, name, index=0):
        pltpu.make_async_copy(ref, ref, sem(name, index)).wait()

    def at(value, size):
        return pl.ds(pl.multiple_of(value * size, size), size)

    barrier = pltpu.get_barrier_semaphore()

    def greet(device):
        pl.semaphore_signal(barrier, inc=1, device_id=device, device_id_type=pl.DeviceIdType.MESH)

    for p in peers:
        greet((dp, p))
    greet((x_dp, me))

    @pl.when(has_up)
    def _():
        greet((dp + 2, me))

    @pl.when(has_down)
    def _():
        greet((dp - 2, me))

    pl.semaphore_wait(barrier, n_seq + has_up.astype(jnp.int32) + has_down.astype(jnp.int32))

    w_rows = w_ref.shape[0]
    piece = w_rows // 8
    z_odd = lax.rem(z_pos, 2)
    z_dp = dp + 2 - 4 * z_odd

    def w_piece(owner, x, z, u):
        start = owner * w_rows + (4 * z + 2 * x + u) * piece
        return pl.ds(pl.multiple_of(start, piece), piece)

    w_sends = [
        remote(
            w_ref.at[at(4 * z_odd + 2 * x_pos + u, piece), :],
            w_full.at[w_piece(me, x_pos, z_odd, u), :],
            (dp, across), ("w_send", u), ("w_y", u),
        )
        for u in range(2)
    ]

    def tell(step):
        @pl.when(has_up)
        def _():
            pl.semaphore_signal(
                token.at[2 * step], inc=1, device_id=(dp + 2, me),
                device_id_type=pl.DeviceIdType.MESH,
            )

        @pl.when(has_down)
        def _():
            pl.semaphore_signal(
                token.at[2 * step + 1], inc=1, device_id=(dp - 2, me),
                device_id_type=pl.DeviceIdType.MESH,
            )

    def told(step):
        @pl.when(has_down)
        def _():
            pl.semaphore_wait(token.at[2 * step], 1)

        @pl.when(has_up)
        def _():
            pl.semaphore_wait(token.at[2 * step + 1], 1)

    tell(0)

    def head_cols(owner, pair):
        return pl.ds(pl.multiple_of(owner * own + pair * LANES, LANES), LANES)

    spot = at(core, rows)
    far_spot = pl.ds(pl.multiple_of(block + core * rows, rows), rows)

    def half_cols(half):
        return pl.ds(pl.multiple_of(half * own, own), own)

    for src, dst in ((q_ref, q_h), (k_ref, k_h), (v_ref, v_h)):
        remote(src.at[:, half_cols(1 - core)], dst.at[spot, :], (dp, mate), ("send_a",), ("near",))
        local(src.at[:, half_cols(core)], dst.at[spot, :], "keep")

    def send_far(src, dst, pair, send, recv):
        pc = slice(pair * LANES, (pair + 1) * LANES)
        for half in range(2):
            cols = slice(half * own + pair * LANES, half * own + (pair + 1) * LANES)
            remote(src.at[:, cols], dst.at[far_spot, pc], (dp, other + half), send, recv)

    def send_kv(pair):
        send_far(k_ref, k_h, pair, ("send_kv", pair), ("kv", pair))
        send_far(v_ref, v_h, pair, ("send_kv", pair), ("kv", pair))

    def sent_kv(pair):
        drain(w_full.at[0 : 4 * rows * LANES // (2 * channels), :], "send_kv", pair)

    def w_take(x, z, u, name, index, *onward):
        here = w_full.at[w_piece(across, x, z, u), :]
        drain(here, name, index)
        for device, to_name, to_index in onward:
            remote(here, here, (device, me), ("send_a",), (to_name, to_index))
        remote(here, here, (dp, mate), ("send_a",), ("w_pair",))

    z_other, x_other = 1 - z_odd, 1 - x_pos

    def flip(value):
        return value.astype(F32).T

    def attend(pair):
        heads = (2 * pair, 2 * pair + 1)
        for h in heads:
            hr = slice(h * depth, (h + 1) * depth)
            scores = jnp.dot(k_h[:, hr], qt[hr, 0:block], preferred_element_type=F32)
            prob[h] = scores
            stat_s[0, h : h + 1, :] = jnp.max(scores, axis=0, keepdims=True)
        for h in heads:
            shifted = jnp.exp(prob[h] - stat_s[0, h : h + 1, :])
            prob[h] = shifted
            stat_s[1, h : h + 1, :] = 1.0 / jnp.sum(shifted, axis=0, keepdims=True)
        for h in heads:
            hr = slice(h * depth, (h + 1) * depth)
            p = prob[h] * stat_s[1, h : h + 1, :]
            rounded = p.astype(BF)
            prob[h] = p
            pb_s[h, :, 0:block] = rounded[0:block]
            ctxt[hr, :] = jnp.dot(vt[hr, :], rounded, preferred_element_type=F32).astype(BF)
        pc = slice(pair * LANES, (pair + 1) * LANES)
        ctx_h[:, pc] = flip(ctxt[pc, :]).astype(BF)
        send_rows(ctx_h, ctx_out, pair, ("send_a",), ("ctx_mate", pair))
        keep_rows(ctx_h, ctx_out, pair, "ctx_keep", pair)

    def send_rows(src, dst, pair, send, recv):
        source = slice(pair * LANES, (pair + 1) * LANES)
        remote(src.at[at(1 - core, rows), source], dst.at[:, head_cols(core, pair)], (dp, mate), send, recv)

    def keep_rows(src, dst, pair, name, index=0):
        source = slice(pair * LANES, (pair + 1) * LANES)
        local(src.at[spot, source], dst.at[:, head_cols(core, pair)], name, index)

    def send_out(src, dst, pair):
        send_rows(src, dst, pair, ("send_out",), ("outs",))
        keep_rows(src, dst, pair, "out_keep")

    def values_in(pair):
        pc = slice(pair * LANES, (pair + 1) * LANES)
        drain(w_full.at[0 : 4 * rows * LANES // (2 * channels), :], "kv", pair)
        vt[pc, block:] = flip(v_h[block:, pc]).astype(BF)

    w_sends[0].wait_send()
    w_sends[1].wait_send()
    send_kv(0)
    send_kv(1)
    w_take(x_pos, z_odd, 0, "w_y", 0, (z_dp, "w_z", 0), (x_dp, "w_x", 0))
    loads = [
        local(src, dst, "loads", t)
        for t, (src, dst) in enumerate(
            ((res_ref, res_v), (cg_ref, cg_v), (og_ref, og_v), (taps_hbm, taps_ref), (gain_hbm, gain_ref), (bias_hbm, bias_ref))
        )
    ]
    w_self = local(w_ref, w_full.at[at(me, w_rows), :], "w_self")
    w_take(x_pos, z_odd, 1, "w_y", 1, (x_dp, "w_x", 1), (z_dp, "w_z", 1))
    told(0)
    tell(1)
    drain(w_full.at[0 : 3 * rows * own // (2 * channels), :], "near")
    drain(w_full.at[0 : 3 * rows * own // (2 * channels), :], "keep")
    for pair in range(pairs):
        pc = slice(pair * LANES, (pair + 1) * LANES)
        qt[pc, 0:block] = (flip(q_h[0:block, pc]) * scaling).astype(BF)
        vt[pc, 0:block] = flip(v_h[0:block, pc]).astype(BF)
    w_take(x_pos, z_other, 0, "w_z", 0, (x_dp, "w_x", 2))
    sent_kv(0)
    send_kv(2)
    remote(w_ref, w_full.at[at(me, w_rows), :], (dp, mate), ("send_a",), ("w_mate",))
    values_in(0)
    attend(0)
    w_take(x_other, z_odd, 0, "w_x", 0)
    w_take(x_other, z_odd, 1, "w_x", 1, (z_dp, "w_z", 2))
    told(1)
    tell(2)
    sent_kv(1)
    send_kv(3)
    values_in(1)
    attend(1)
    w_take(x_pos, z_other, 1, "w_z", 1)
    w_take(x_other, z_other, 0, "w_x", 2)
    sent_kv(2)
    for pair in range(pairs):
        send_far(q_ref, q_h, pair, ("send_a",), ("q_far",))
    values_in(2)
    attend(2)
    told(2)
    w_take(x_other, z_other, 1, "w_z", 2)
    values_in(3)
    attend(3)
    stats = (dp, across)
    remote(stat_s.at[0:2], stat_r.at[0:2], stats, ("send_stats",), ("stats", 0))

    for pair in range(pairs):
        pc = slice(pair * LANES, (pair + 1) * LANES)
        kt[pc, :] = flip(k_h[:, pc]).astype(BF)
    loads[0].wait()
    w_self.wait()
    drain(w_full.at[at(mate, w_rows), :], "w_mate")
    drain(w_full.at[at(diag, w_rows), :], "w_pair")
    wide = 2 * LANES
    spans = [
        [slice(o * own + pair * LANES, o * own + (pair + 1) * LANES) for o in range(2)]
        for pair in range(pairs)
    ]

    def mix(pair):
        drain(ctx_h.at[0:rows, 0:LANES], "ctx_keep", pair)
        drain(ctx_h.at[0:rows, 0:LANES], "ctx_mate", pair)
        for n, cols in enumerate(spans[pair]):
            both = res_v[:, cols].astype(F32) + ctx_out[:, cols].astype(F32)
            mixed[:, (pair * 2 + n) * LANES : (pair * 2 + n + 1) * LANES] = both.astype(BF)

    def weigh(some, cols):
        weights = jnp.concatenate([w_full[r, cols] for pair in some for r in spans[pair]], axis=0)
        lanes = slice(some[0] * 2 * LANES, (some[-1] + 1) * 2 * LANES)
        return jnp.dot(mixed[:, lanes], weights, preferred_element_type=F32)

    early, late = range(pairs - 1), range(pairs - 1, pairs)
    for pair in early:
        mix(pair)

    def conv_first(i, carry):
        cols = at(i, 2 * wide)
        pre[:, cols] = weigh(early, cols)
        return carry

    lax.fori_loop(0, channels // wide, conv_first, 0)
    mix(pairs - 1)

    for i in range(channels // wide):
        cols = slice(i * wide, (i + 1) * wide)
        gates = slice(channels + i * wide, channels + (i + 1) * wide)
        a = (weigh(late, cols) + pre[:, cols]).astype(BF)
        b = (weigh(late, gates) + pre[:, gates]).astype(BF)
        sig = jax.nn.sigmoid(b.astype(F32))
        a_s[:, cols] = a
        sig_s[:, cols] = sig
        rounded = (a.astype(F32) * sig).astype(BF)
        glu = rounded.astype(F32)
        for half in range(2):
            lanes = slice(half * LANES, (half + 1) * LANES)
            glu_f[2 * i + half, HALO : HALO + rows, :] = glu[:, lanes]
            hs1[2 * i + half] = rounded[rows - HALO :, lanes]
        two = slice(2 * i, 2 * i + 2)

        @pl.when(me < n_seq - 1)
        def _():
            remote(hs1.at[two], hr1.at[two], (dp, me + 1), ("halo1_send",), ("halo1",))

    for copy in loads[2:]:
        copy.wait()
    span = taps - 1
    base = HALO - span

    def norm_rows(first, count, unroll):
        here = slice(first, first + count)
        zero = jnp.zeros((count, LANES), F32)

        def conv(c, total):
            lanes = at(c, LANES)
            acc = zero
            for o in range(taps):
                low = base + first + o
                acc = acc + taps_ref[o : o + 1, lanes] * glu_f[c, low : low + count, :]
            dw[c, here, :] = acc
            return total + acc

        total = lax.fori_loop(0, chunks, conv, zero)
        average = jnp.sum(total, axis=1, keepdims=True) * (1.0 / channels)

        def squares(c, total):
            centered = dw[c, here, :] - average
            return total + centered * centered

        total = lax.fori_loop(0, chunks, squares, zero, unroll=unroll)
        variance = jnp.sum(total, axis=1, keepdims=True) * (1.0 / channels)
        inverse = lax.rsqrt(variance + 1e-05)

        def norm_step(c, carry):
            s1, s2 = carry
            lanes = at(c, LANES)
            normed = (dw[c, here, :] - average) * inverse
            affine = normed * gain_ref[:, lanes] + bias_ref[:, lanes]
            sig = jax.nn.sigmoid(affine)
            conv_out[here, lanes] = (affine * sig).astype(BF)
            affine_grad = og_v[here, lanes].astype(F32) * (sig * (1.0 + affine * (1.0 - sig)))
            gain_term = jnp.sum(affine_grad * normed, axis=0, keepdims=True)
            bias_term = jnp.sum(affine_grad, axis=0, keepdims=True)
            if first == 0:
                gain_term = gain_term + part[c, taps : taps + 1, :]
                bias_term = bias_term + part[c, taps + 1 : taps + 2, :]
            part[c, taps : taps + 1, :] = gain_term
            part[c, taps + 1 : taps + 2, :] = bias_term
            normed_grad = affine_grad * gain_ref[:, lanes]
            dw[c, here, :] = normed
            ng_s[c, here, :] = normed_grad
            return s1 + normed_grad, s2 + normed_grad * normed

        s1, s2 = lax.fori_loop(0, chunks, norm_step, (zero, zero), unroll=unroll)
        m1 = jnp.sum(s1, axis=1, keepdims=True) * (1.0 / channels)
        m2 = jnp.sum(s2, axis=1, keepdims=True) * (1.0 / channels)

        def depth_grad_step(c, carry):
            grad = inverse * (ng_s[c, here, :] - m1 - dw[c, here, :] * m2)
            dg[c, here, :] = grad
            return carry

        lax.fori_loop(0, chunks, depth_grad_step, 0, unroll=unroll)

    norm_rows(HALO, rows - HALO, 1)
    @pl.when(me > 0)
    def _():
        drain(hr1, "halo1")
        glu_f[:, 0:HALO, :] = hr1[...].astype(F32)

    @pl.when(me == 0)
    def _():
        glu_f[:, 0:HALO, :] = jnp.zeros((chunks, HALO, LANES), F32)

    norm_rows(0, HALO, chunks)
    tail = dg.at[:, rows : rows + HALO, :]

    @pl.when(me > 0)
    def _():
        remote(dg.at[:, 0:HALO, :], tail, (dp, me - 1), ("halo2_send",), ("halo2",))

    def glu_back(first, count):
        def body(c, carry):
            lanes = at(c, LANES)
            gates = pl.ds(pl.multiple_of(channels + c * LANES, LANES), LANES)
            here = slice(first, first + count)
            acc = jnp.zeros((count, LANES), F32)
            for o in range(taps):
                low = first + span - o
                acc = acc + taps_ref[o : o + 1, lanes] * dg[c, low : low + count, :]
            sig = sig_s[here, lanes]
            ig_out[here, lanes] = (acc * sig).astype(BF)
            slope = acc * a_s[here, lanes].astype(F32) * sig * (1.0 - sig)
            ig_out[here, gates] = slope.astype(BF)
            return carry

        lax.fori_loop(0, chunks, body, 0)

    def tap_grad(c, carry):
        grad = dg[c, 0:rows, :]
        for o in range(taps):
            part[c, o : o + 1, :] = jnp.sum(
                grad * glu_f[c, base + o : base + o + rows, :], axis=0, keepdims=True
            )
        part[c, taps + 2 : TERM_ROWS, :] = jnp.zeros((TERM_ROWS - taps - 2, LANES), F32)
        return carry

    lax.fori_loop(0, chunks, tap_grad, 0)
    for d, p in enumerate(dp_peers):
        remote(part.at[p], rs_buf.at[d], (p, me), ("send_r1",), ("red1",))
    glu_back(0, rows - HALO)

    @pl.when(me < n_seq - 1)
    def _():
        drain(tail, "halo2")

    @pl.when(me == n_seq - 1)
    def _():
        tail[...] = jnp.zeros((chunks, HALO, LANES), F32)

    glu_back(rows - HALO, HALO)
    loads[1].wait()
    quad = 2 * LANES
    behind = z_pos >= line // 2

    def grad_away(half, step):
        cols = pl.ds(pl.multiple_of(half * own + step * quad, quad), quad)
        within = slice(step * quad, (step + 1) * quad)
        remote(
            rg_out.at[:, cols], g_h.at[far_spot, within], (dp, other + half),
            ("send_b",), ("grad_far", step),
        )

    for step in range(pairs // 2):
        within = slice(step * quad, (step + 1) * quad)
        for half, mine in ((core, True), (1 - core, False)):
            cols = pl.ds(pl.multiple_of(half * own + step * quad, quad), quad)
            grad = lax.dot_general(
                ig_out[...], w_full[cols, :], (((1,), (1,)), ((), ())), preferred_element_type=F32
            )
            rg_out[:, cols] = (cg_v[:, cols].astype(F32) + grad).astype(BF)
            if step == 0:
                grad_away(half, step)
            if mine:
                g_h[spot, within] = rg_out[:, cols]
            else:
                remote(
                    rg_out.at[:, cols], g_h.at[spot, within], (dp, mate), ("send_b",), ("grad_near", step)
                )

    def sum_recordings():
        drain(rs_buf, "red1")
        total = part[dp]
        for d in range(n_dp - 1):
            total = total + rs_buf[d]
        s2_buf[me] = total
        for p in peers:
            remote(s2_buf.at[me], s2_buf.at[me], (dp, p), ("send_r2",), ("red2",))

    def sum_frames():
        drain(s2_buf.at[0 : n_seq - 1], "red2")
        total = s2_buf[0]
        for s in range(1, n_seq):
            total = total + s2_buf[s]
        fin[dp] = total * (1.0 / n_dp)
        for p in dp_peers:
            remote(fin.at[dp], fin.at[dp], (p, me), ("send_r3",), ("red3",))

    def row_dots(step):
        drain(g_h.at[0:rows, 0:quad], "grad_near", step)
        stat_s[2 + step] = jnp.zeros((2 * pairs, block), F32)
        for pair in (2 * step, 2 * step + 1):
            pc = slice(pair * LANES, (pair + 1) * LANES)
            gt[pc, 0:block] = flip(g_h[0:block, pc]).astype(BF)
            for h in (2 * pair, 2 * pair + 1):
                hr = slice(h * depth, (h + 1) * depth)
                both = gt[hr, 0:block].astype(F32) * ctxt[hr, :].astype(F32)
                stat_s[2 + step, h : h + 1, :] = jnp.sum(both, axis=0, keepdims=True)
        slab = slice(2 + step, 3 + step)
        remote(stat_s.at[slab], stat_r.at[slab], stats, ("send_stats",), ("stats", 1 + step))

    row_dots(0)
    pl.when(behind)(sum_recordings)
    for half in (core, 1 - core):
        grad_away(half, pairs // 2 - 1)

    drain(w_full.at[0 : 2 * pairs * rows * LANES // (2 * channels), :], "q_far")
    drain(stat_r.at[0:2], "stats", 0)
    def far_scores(pair):
        pc = slice(pair * LANES, (pair + 1) * LANES)
        qt[pc, block:] = (flip(q_h[block:, pc]) * scaling).astype(BF)
        for h in (2 * pair, 2 * pair + 1):
            hr = slice(h * depth, (h + 1) * depth)
            p_f[h] = jnp.dot(k_h[0:block, hr], qt[hr, block:], preferred_element_type=F32)

    far_scores(0)
    for pair in range(pairs):
        if pair + 1 < pairs:
            far_scores(pair + 1)
        for h in (2 * pair, 2 * pair + 1):
            p = jnp.exp(p_f[h] - stat_r[0, h : h + 1, :]) * stat_r[1, h : h + 1, :]
            p_f[h] = p
            pb_s[h, :, block:] = p.astype(BF)

    pl.when(jnp.logical_not(behind))(sum_recordings)
    row_dots(1)
    for pair in range(pairs):
        pc = slice(pair * LANES, (pair + 1) * LANES)
        heads = (2 * pair, 2 * pair + 1)
        spots = [slice(h * depth, (h + 1) * depth) for h in heads]
        prob_grads = [
            jnp.dot(v_h[:, hr], gt[hr, 0:block], preferred_element_type=F32) for hr in spots
        ]
        for h, prob_grad in zip(heads, prob_grads):
            score_grad = (prob[h] * (prob_grad - stat_s[2 + pair // 2, h : h + 1, :]) * scaling).astype(BF)
            ds_s[h, :, 0:block] = score_grad[0:block]
            ds_f[h % 2] = score_grad[block:]
        for h, hr in zip(heads, spots):
            score_grad = jnp.concatenate([ds_s[h, :, 0:block], ds_f[h % 2]], axis=0)
            dqt[hr, :] = jnp.dot(kt[hr, :], score_grad, preferred_element_type=F32)
        dq_h[:, pc] = dqt[pc, :].T.astype(BF)
        send_out(dq_h, dq_out, pair)
        if pair == 0:
            pl.when(behind)(sum_frames)

    pl.when(jnp.logical_not(behind))(sum_frames)
    first_head = lax.broadcasted_iota(jnp.int32, (block, LANES), 1) < depth
    for pair in range(pairs):
        pc = slice(pair * LANES, (pair + 1) * LANES)
        if pair % 2 == 0:
            drain(stat_r.at[2:3], "stats", 1 + pair // 2)
            drain(g_h.at[0:block, 0:quad], "grad_far", pair // 2)
        gt[pc, block:] = flip(g_h[block:, pc]).astype(BF)
        heads = (2 * pair, 2 * pair + 1)
        spots = [slice(h * depth, (h + 1) * depth) for h in heads]
        prob_grads = [
            jnp.dot(v_h[0:block, hr], gt[hr, block:], preferred_element_type=F32) for hr in spots
        ]
        for h, prob_grad in zip(heads, prob_grads):
            score_grad = p_f[h] * (prob_grad - stat_r[2 + pair // 2, h : h + 1, :]) * scaling
            ds_s[h, :, block:] = score_grad.astype(BF)
        left = jnp.dot(pb_s[2 * pair], g_h[:, pc], preferred_element_type=F32)
        right = jnp.dot(pb_s[2 * pair + 1], g_h[:, pc], preferred_element_type=F32)
        dv_h[:, pc] = jnp.where(first_head, left, right).astype(BF)
        send_out(dv_h, dv_out, pair)
        left = jnp.dot(ds_s[2 * pair], q_h[:, pc], preferred_element_type=F32)
        right = jnp.dot(ds_s[2 * pair + 1], q_h[:, pc], preferred_element_type=F32)
        dk_h[:, pc] = jnp.where(first_head, left, right).astype(BF)
        send_out(dk_h, dk_out, pair)

    wide_rows = 2 * channels
    count = 2 * w_rows + 6 * piece + 6 * pairs * rows * LANES // wide_rows
    drain(w_full.at[0:count, :], "send_a")
    sent_kv(pairs - 1)
    drain(stat_r, "send_stats")
    drain(rs_buf, "send_r1")
    drain(s2_buf.at[0 : n_seq - 1], "send_r2")

    @pl.when(me < n_seq - 1)
    def _():
        drain(hr1, "halo1_send")

    @pl.when(me > 0)
    def _():
        drain(tail, "halo2_send")

    drain(rs_buf, "red3")
    for c in range(chunks):
        lanes = slice(c * LANES, (c + 1) * LANES)
        kg_out[:, lanes] = fin[c, 0:taps, :]
        gg_out[:, lanes] = fin[c, taps : taps + 1, :]
        bg_out[:, lanes] = fin[c, taps + 1 : taps + 2, :]
    drain(rs_buf, "send_r3")
    drain(w_full.at[0 : 3 * pairs * rows * LANES // wide_rows, :], "out_keep")
    drain(w_full.at[0 : 3 * pairs * rows * LANES // wide_rows, :], "outs")
    drain(w_full.at[0 : 3 * pairs * rows * LANES // wide_rows, :], "send_out")
    drain(w_full.at[0 : 3 * rows * own // wide_rows, :], "send_b")


def place_outputs(*refs):
    sems = refs[20]
    copies = [pltpu.make_async_copy(refs[i], refs[10 + i], sems.at[i]) for i in range(10)]
    for copy in copies:
        copy.start()
    for copy in copies:
        copy.wait()


def fused_shards(
    queries, key_vecs, value_vecs, residual_in, point_weight, context_grad, depth_kernel,
    norm_gain, norm_bias, conv_grad,
):
    n_seq = lax.axis_size("seq")
    n_dp = lax.axis_size("dp")
    rows, channels = queries.shape[1:]
    taps = depth_kernel.shape[0]
    depth = channels // HEADS
    frames = rows * n_seq
    own = channels // n_seq
    heads = own // depth
    chunks = channels // LANES
    s = jax.ShapeDtypeStruct
    vm = pltpu.VMEM
    block = s((rows, channels), BF)
    half = channels // 2
    block_rows = 2 * rows
    heads = HEADS // 2
    all_rows = vm((frames, half), BF)
    all_cols = vm((half, frames), BF)
    some_rows = vm((block_rows, half), BF)
    scratch = (
        [all_rows] * 4 + [all_cols] * 4 + [vm((half, block_rows), BF), some_rows]
        + [vm((heads, frames, block_rows), F32), vm((heads, block_rows, block_rows), F32)]
        + [vm((heads, block_rows, frames), BF)] * 2
        + [vm((half, block_rows), F32)] + [some_rows] * 3
        + [vm((2, block_rows, block_rows), BF)]
        + [vm((4, heads, block_rows), F32)] * 2
        + [
            vm((rows, channels), BF),
            vm((rows, channels), BF),
            vm((rows, channels), BF),
            vm((channels, 2 * channels), BF),
            vm((rows, 2 * channels), F32),
            vm((rows, channels), BF),
            vm((rows, channels), BF),
            vm((rows, channels), F32),
            vm((chunks, HALO + rows, LANES), F32),
            vm((chunks, rows, LANES), F32),
            vm((chunks, rows, LANES), F32),
            vm((chunks, rows + HALO, LANES), F32),
            vm((chunks, TERM_ROWS, LANES), F32),
            vm((n_dp - 1, TERM_ROWS, LANES), F32),
            vm((n_seq, TERM_ROWS, LANES), F32),
            vm((chunks, TERM_ROWS, LANES), F32),
            vm((taps, channels), F32),
            vm((1, channels), F32),
            vm((1, channels), F32),
            vm((chunks, HALO, LANES), BF),
            vm((chunks, HALO, LANES), BF),
            pltpu.SemaphoreType.DMA((sum(SEMS.values()),)),
            pltpu.SemaphoreType.REGULAR((6,)),
        ]
    )
    spec = pl.BlockSpec(memory_space=pltpu.VMEM)
    hbm = pl.BlockSpec(memory_space=pl.ANY)
    outs = pl.pallas_call(
        functools.partial(fused_kernel, (n_seq, n_dp, rows, channels, taps, depth)),
        out_shape=(
            block, block, block, block, block, s((rows, 2 * channels), BF), block,
            s((taps, channels), F32), s((1, channels), F32), s((1, channels), F32),
        ),
        in_specs=[hbm] * 10,
        out_specs=(spec,) * 10,
        scratch_shapes=scratch,
        compiler_params=pltpu.CompilerParams(
            collective_id=0, has_side_effects=True, vmem_limit_bytes=56 * 1024 * 1024
        ),
    )(
        queries[0], key_vecs[0], value_vecs[0], residual_in[0], point_weight, context_grad[0],
        depth_kernel, norm_gain[None], norm_bias[None], conv_grad[0],
    )
    outs = pl.pallas_call(
        place_outputs,
        out_shape=tuple(s(o.shape, o.dtype) for o in outs),
        in_specs=[spec] * 10,
        out_specs=(hbm,) * 10,
        scratch_shapes=[pltpu.SemaphoreType.DMA((10,))],
    )(*outs)
    return tuple(o[None] for o in outs[:7]) + (outs[7], outs[8][0], outs[9][0])


def chosen(*args):
    n_seq = lax.axis_size("seq")
    n_dp = lax.axis_size("dp")
    recs, rows, channels = args[0].shape
    fits = (
        n_seq == 4
        and recs == 1
        and rows % 128 == 0
        and channels % (LANES * n_seq) == 0
        and 2 * channels == LANES * HEADS
        and channels // LANES == n_dp
        and rows * n_seq <= 512
        and args[4].shape[0] == channels // n_seq == 2 * LANES
        and args[6].shape[0] <= 31
    )
    return fused_shards(*args) if fits else shards(*args)


def solution(mesh):
    in_specs = (
        P("dp", "seq", None),
        P("dp", "seq", None),
        P("dp", "seq", None),
        P("dp", "seq", None),
        P("seq", None),
        P("dp", "seq", None),
        P(),
        P(),
        P(),
        P("dp", "seq", None),
    )
    out_specs = (
        P("dp", "seq", None),
        P("dp", "seq", None),
        P("dp", "seq", None),
        P("dp", "seq", None),
        P("dp", "seq", None),
        P("dp", "seq", None),
        P("dp", "seq", None),
        P(),
        P(),
        P(),
    )
    return jax.shard_map(chosen, mesh=mesh, in_specs=in_specs, out_specs=out_specs, check_vma=False)
```

```python
import functools
import jax
import jax.numpy as jnp
from jax import lax
from jax.sharding import PartitionSpec as P
from jax.experimental import pallas as pl
from jax.experimental.pallas import tpu as pltpu

HEADS = 16


def from_behind(block, axis, distance):
    devices = range(lax.axis_size(axis))
    route = [(i - distance, i) for i in devices if i - distance in devices]
    return lax.ppermute(block, axis, route)


def block_probs(query_block, key_heads, scaling):
    scores = (
        jnp.einsum("qhd,khd->hqk", query_block, key_heads, preferred_element_type=jnp.float32)
        * scaling
    )
    shifted = jnp.exp(scores - jnp.max(scores, axis=2, keepdims=True))
    return shifted / jnp.sum(shifted, axis=2, keepdims=True)


def attend_forward(query_part, key_part, value_part, head_count):
    frames, channels = query_part.shape
    head_depth = channels // head_count
    scaling = head_depth ** (-0.5)
    query_heads = query_part.reshape(frames, head_count, head_depth)
    key_heads = key_part.reshape(frames, head_count, head_depth)
    value_heads = value_part.reshape(frames, head_count, head_depth)
    block_rows = min(512, frames)

    def one_block(running, index):
        query_block = lax.dynamic_slice_in_dim(query_heads, index * block_rows, block_rows, 0)
        rounded = block_probs(query_block, key_heads, scaling).astype(jnp.bfloat16)
        context = jnp.einsum(
            "hqk,khd->qhd", rounded, value_heads, preferred_element_type=jnp.float32
        ).astype(jnp.bfloat16)
        return (running, context)

    unused, blocks = lax.scan(
        one_block, jnp.zeros((), jnp.float32), jnp.arange(frames // block_rows)
    )
    return blocks.reshape(frames, channels)


def attend_backward(query_part, key_part, value_part, grad_part, context_part, head_count):
    frames, channels = query_part.shape
    head_depth = channels // head_count
    scaling = head_depth ** (-0.5)
    query_heads = query_part.reshape(frames, head_count, head_depth)
    key_heads = key_part.reshape(frames, head_count, head_depth)
    value_heads = value_part.reshape(frames, head_count, head_depth)
    grad_heads = grad_part.reshape(frames, head_count, head_depth)
    context_heads = context_part.reshape(frames, head_count, head_depth)
    block_rows = min(512, frames)

    def one_block(running, index):
        key_total, value_total = running
        start = index * block_rows
        query_block = lax.dynamic_slice_in_dim(query_heads, start, block_rows, 0)
        grad_block = lax.dynamic_slice_in_dim(grad_heads, start, block_rows, 0)
        context_block = lax.dynamic_slice_in_dim(context_heads, start, block_rows, 0)
        probabilities = block_probs(query_block, key_heads, scaling)
        rounded = probabilities.astype(jnp.bfloat16)
        row_dots = jnp.sum(
            grad_block.astype(jnp.float32) * context_block.astype(jnp.float32), axis=2
        )
        prob_grad = jnp.einsum(
            "qhd,khd->hqk", grad_block, value_heads, preferred_element_type=jnp.float32
        )
        score_grad = (probabilities * (prob_grad - row_dots.T[:, :, None]) * scaling).astype(
            jnp.bfloat16
        )
        query_grad = jnp.einsum(
            "hqk,khd->qhd", score_grad, key_heads, preferred_element_type=jnp.float32
        ).astype(jnp.bfloat16)
        key_total = key_total + jnp.einsum(
            "hqk,qhd->khd", score_grad, query_block, preferred_element_type=jnp.float32
        )
        value_total = value_total + jnp.einsum(
            "hqk,qhd->khd", rounded, grad_block, preferred_element_type=jnp.float32
        )
        return ((key_total, value_total), query_grad)

    empty = jnp.zeros((frames, head_count, head_depth), jnp.float32)
    totals, blocks = lax.scan(one_block, (empty, empty), jnp.arange(frames // block_rows))
    query_grad = blocks.reshape(frames, channels)
    key_grad = totals[0].astype(jnp.bfloat16).reshape(frames, channels)
    value_grad = totals[1].astype(jnp.bfloat16).reshape(frames, channels)
    return (query_grad, key_grad, value_grad)


def shards(
    queries,
    key_vecs,
    value_vecs,
    residual_in,
    point_weight,
    context_grad,
    depth_kernel,
    norm_gain,
    norm_bias,
    conv_grad,
):
    head_count = HEADS // lax.axis_size("seq")
    query_heads, key_heads, value_heads = (
        lax.all_to_all(queries, "seq", split_axis=2, concat_axis=1, tiled=True),
        lax.all_to_all(key_vecs, "seq", split_axis=2, concat_axis=1, tiled=True),
        lax.all_to_all(value_vecs, "seq", split_axis=2, concat_axis=1, tiled=True),
    )
    context_local = attend_forward(query_heads[0], key_heads[0], value_heads[0], head_count)
    context_out = lax.all_to_all(
        context_local[None], "seq", split_axis=1, concat_axis=2, tiled=True
    )
    taps = depth_kernel.shape[0]
    channels = depth_kernel.shape[1]
    span = taps - 1
    frames = residual_in.shape[1]
    mixed = (residual_in[0].astype(jnp.float32) + context_out[0].astype(jnp.float32)).astype(
        jnp.bfloat16
    )
    pre_conv = jnp.dot(
        mixed,
        lax.all_gather(point_weight, "seq", axis=0, tiled=True),
        preferred_element_type=jnp.float32,
    )
    conv_input = pre_conv.astype(jnp.bfloat16)[None]
    value_half = conv_input[:, :, :channels].astype(jnp.float32)
    gate_sig = jax.nn.sigmoid(conv_input[:, :, channels:].astype(jnp.float32))
    glu = (value_half * gate_sig).astype(jnp.bfloat16)
    earlier = from_behind(glu[:, frames - span :], "seq", 1)
    glu_wide = jnp.concatenate([earlier, glu], axis=1)
    glu_view = lax.optimization_barrier(glu_wide).astype(jnp.float32)
    depthwise = jnp.zeros((1, frames, channels), jnp.float32)
    for offset in range(taps):
        depthwise = depthwise + depth_kernel[offset] * glu_view[:, offset : offset + frames]
    average = jnp.mean(depthwise, axis=2, keepdims=True)
    centered = depthwise - average
    variance = jnp.mean(centered * centered, axis=2, keepdims=True)
    inverse = lax.rsqrt(variance + 1e-05)
    normed = centered * inverse
    affine = normed * norm_gain + norm_bias
    sig_affine = jax.nn.sigmoid(affine)
    conv_output = (affine * sig_affine).astype(jnp.bfloat16)
    affine_grad = conv_grad.astype(jnp.float32) * (sig_affine * (1.0 + affine * (1.0 - sig_affine)))
    gain_term = jnp.sum(affine_grad * normed, axis=(0, 1))
    bias_term = jnp.sum(affine_grad, axis=(0, 1))
    normed_grad = affine_grad * norm_gain
    depth_grad = inverse * (
        normed_grad
        - jnp.mean(normed_grad, axis=2, keepdims=True)
        - normed * jnp.mean(normed_grad * normed, axis=2, keepdims=True)
    )
    kernel_term = jnp.stack(
        [
            jnp.sum(depth_grad * glu_view[:, offset : offset + frames], axis=(0, 1))
            for offset in range(taps)
        ]
    )
    kernel_total, gain_total, bias_total = lax.psum(
        (kernel_term, gain_term, bias_term), ("dp", "seq")
    )
    recordings = lax.axis_size("dp")
    kernel_grad = kernel_total / recordings
    gain_grad = gain_total / recordings
    bias_grad = bias_total / recordings
    later = from_behind(depth_grad[:, :span], "seq", -1)
    grad_wide = jnp.concatenate([depth_grad, later], axis=1)
    glu_grad = jnp.zeros((1, frames, channels), jnp.float32)
    for offset in range(taps):
        begin = span - offset
        glu_grad = glu_grad + depth_kernel[offset] * grad_wide[:, begin : begin + frames]
    input_grad = jnp.concatenate(
        [glu_grad * gate_sig, glu_grad * value_half * gate_sig * (1.0 - gate_sig)], axis=2
    ).astype(jnp.bfloat16)
    slope_rows = input_grad[0]
    mixed_grad = jnp.einsum(
        "fc,dc->fd",
        slope_rows,
        lax.all_gather(point_weight, "seq", axis=0, tiled=True),
        preferred_element_type=jnp.float32,
    )
    residual_grad = (context_grad.astype(jnp.float32) + mixed_grad[None]).astype(jnp.bfloat16)
    grad_heads = lax.all_to_all(residual_grad, "seq", split_axis=2, concat_axis=1, tiled=True)
    query_grad, key_grad, value_grad = attend_backward(
        query_heads[0], key_heads[0], value_heads[0], grad_heads[0], context_local, head_count
    )
    query_out, key_out, value_out = (
        lax.all_to_all(query_grad[None], "seq", split_axis=1, concat_axis=2, tiled=True),
        lax.all_to_all(key_grad[None], "seq", split_axis=1, concat_axis=2, tiled=True),
        lax.all_to_all(value_grad[None], "seq", split_axis=1, concat_axis=2, tiled=True),
    )
    return (
        context_out,
        conv_output,
        query_out,
        key_out,
        value_out,
        input_grad,
        residual_grad,
        kernel_grad,
        gain_grad,
        bias_grad,
    )


BF = jnp.bfloat16
F32 = jnp.float32
HALO = 32
LANES = 128
TERM_ROWS = 40


SEMS = dict(
    send_a=1, send_kv=4, send_b=1, send_out=1, send_stats=1, send_r1=1, send_r2=1, send_r3=1,
    w_send=2, halo1_send=1, halo2_send=1,
    near=1, kv=4, q_far=1, w_y=2, w_mate=1, w_pair=1, w_z=3, w_x=3, ctx_mate=4, halo1=1, halo2=1,
    grad_near=2, grad_far=2, stats=3, red1=1, red2=1, red3=1, outs=1, keep=1, w_self=1, loads=6,
    ctx_keep=4, out_keep=1,
)


def sem_base(name):
    names = list(SEMS)
    return sum(SEMS[n] for n in names[: names.index(name)])


def fused_kernel(
    dims,
    q_ref, k_ref, v_ref, res_ref, w_ref, cg_ref, taps_hbm, gain_hbm, bias_hbm, og_ref,
    ctx_out, conv_out, dq_out, dk_out, dv_out, ig_out, rg_out, kg_out, gg_out, bg_out,
    q_h, k_h, v_h, g_h, qt, kt, vt, gt, ctxt, ctx_h, prob, p_f, pb_s, ds_s, dqt, dq_h, dk_h, dv_h,
    ds_f, stat_s, stat_r,
    res_v, cg_v, og_v, w_full, pre, mixed, a_s, sig_s, glu_f, dw, ng_s, dg, part, rs_buf, s2_buf, fin,
    taps_ref, gain_ref, bias_ref, hs1, hr1,
    sems, token,
):
    n_seq, n_dp, rows, channels, taps, depth = dims
    own = channels // 2
    pairs = own // LANES
    frames = rows * n_seq
    block = 2 * rows
    chunks = channels // LANES
    scaling = depth ** (-0.5)
    line = n_dp // 2
    me = lax.axis_index("seq")
    dp = lax.axis_index("dp")
    core = lax.rem(me, 2)
    mate = me + 1 - 2 * core
    across = lax.rem(me + 2, n_seq)
    diag = lax.rem(mate + 2, n_seq)
    x_pos = lax.rem(dp, 2)
    z_pos = lax.div(dp, 2)
    x_dp = dp + 1 - 2 * x_pos
    peers = [across, diag, mate]
    chip = lax.div(me, 2)
    other = 2 * (1 - chip)
    dp_peers = [lax.rem(dp + d, n_dp) for d in range(1, n_dp)]
    has_up = z_pos < line - 1
    has_down = z_pos > 0

    def sem(name, index=0):
        return sems.at[sem_base(name) + index]

    def local(src, dst, name, index=0):
        copy = pltpu.make_async_copy(src, dst, sem(name, index))
        copy.start()
        return copy

    def remote(src, dst, device, send, recv):
        copy = pltpu.make_async_remote_copy(
            src_ref=src, dst_ref=dst, send_sem=sem(*send), recv_sem=sem(*recv),
            device_id=device, device_id_type=pl.DeviceIdType.MESH,
        )
        copy.start()
        return copy

    def drain(ref, name, index=0):
        pltpu.make_async_copy(ref, ref, sem(name, index)).wait()

    def at(value, size):
        return pl.ds(pl.multiple_of(value * size, size), size)

    barrier = pltpu.get_barrier_semaphore()

    def greet(device):
        pl.semaphore_signal(barrier, inc=1, device_id=device, device_id_type=pl.DeviceIdType.MESH)

    for p in peers:
        greet((dp, p))
    greet((x_dp, me))

    @pl.when(has_up)
    def _():
        greet((dp + 2, me))

    @pl.when(has_down)
    def _():
        greet((dp - 2, me))

    pl.semaphore_wait(barrier, n_seq + has_up.astype(jnp.int32) + has_down.astype(jnp.int32))

    w_rows = w_ref.shape[0]
    piece = w_rows // 8
    z_odd = lax.rem(z_pos, 2)
    z_dp = dp + 2 - 4 * z_odd

    def w_piece(owner, x, z, u):
        start = owner * w_rows + (4 * z + 2 * x + u) * piece
        return pl.ds(pl.multiple_of(start, piece), piece)

    w_sends = [
        remote(
            w_ref.at[at(4 * z_odd + 2 * x_pos + u, piece), :],
            w_full.at[w_piece(me, x_pos, z_odd, u), :],
            (dp, across), ("w_send", u), ("w_y", u),
        )
        for u in range(2)
    ]

    def tell(step):
        @pl.when(has_up)
        def _():
            pl.semaphore_signal(
                token.at[2 * step], inc=1, device_id=(dp + 2, me),
                device_id_type=pl.DeviceIdType.MESH,
            )

        @pl.when(has_down)
        def _():
            pl.semaphore_signal(
                token.at[2 * step + 1], inc=1, device_id=(dp - 2, me),
                device_id_type=pl.DeviceIdType.MESH,
            )

    def told(step):
        @pl.when(has_down)
        def _():
            pl.semaphore_wait(token.at[2 * step], 1)

        @pl.when(has_up)
        def _():
            pl.semaphore_wait(token.at[2 * step + 1], 1)

    tell(0)

    def head_cols(owner, pair):
        return pl.ds(pl.multiple_of(owner * own + pair * LANES, LANES), LANES)

    spot = at(core, rows)
    far_spot = pl.ds(pl.multiple_of(block + core * rows, rows), rows)

    def half_cols(half):
        return pl.ds(pl.multiple_of(half * own, own), own)

    for src, dst in ((q_ref, q_h), (k_ref, k_h), (v_ref, v_h)):
        remote(src.at[:, half_cols(1 - core)], dst.at[spot, :], (dp, mate), ("send_a",), ("near",))
        local(src.at[:, half_cols(core)], dst.at[spot, :], "keep")

    def send_far(src, dst, pair, send, recv):
        pc = slice(pair * LANES, (pair + 1) * LANES)
        for half in range(2):
            cols = slice(half * own + pair * LANES, half * own + (pair + 1) * LANES)
            remote(src.at[:, cols], dst.at[far_spot, pc], (dp, other + half), send, recv)

    def send_kv(pair):
        send_far(k_ref, k_h, pair, ("send_kv", pair), ("kv", pair))
        send_far(v_ref, v_h, pair, ("send_kv", pair), ("kv", pair))

    def sent_kv(pair):
        drain(w_full.at[0 : 4 * rows * LANES // (2 * channels), :], "send_kv", pair)

    def w_take(x, z, u, name, index, *onward):
        here = w_full.at[w_piece(across, x, z, u), :]
        drain(here, name, index)
        for device, to_name, to_index in onward:
            remote(here, here, (device, me), ("send_a",), (to_name, to_index))
        remote(here, here, (dp, mate), ("send_a",), ("w_pair",))

    z_other, x_other = 1 - z_odd, 1 - x_pos

    def flip(value):
        return value.astype(F32).T

    def attend(pair):
        heads = (2 * pair, 2 * pair + 1)
        for h in heads:
            hr = slice(h * depth, (h + 1) * depth)
            scores = jnp.dot(k_h[:, hr], qt[hr, 0:block], preferred_element_type=F32)
            prob[h] = scores
            stat_s[0, h : h + 1, :] = jnp.max(scores, axis=0, keepdims=True)
        for h in heads:
            shifted = jnp.exp(prob[h] - stat_s[0, h : h + 1, :])
            prob[h] = shifted
            stat_s[1, h : h + 1, :] = 1.0 / jnp.sum(shifted, axis=0, keepdims=True)
        for h in heads:
            hr = slice(h * depth, (h + 1) * depth)
            p = prob[h] * stat_s[1, h : h + 1, :]
            rounded = p.astype(BF)
            prob[h] = p
            pb_s[h, :, 0:block] = rounded[0:block]
            ctxt[hr, :] = jnp.dot(vt[hr, :], rounded, preferred_element_type=F32).astype(BF)
        pc = slice(pair * LANES, (pair + 1) * LANES)
        ctx_h[:, pc] = flip(ctxt[pc, :]).astype(BF)
        send_rows(ctx_h, ctx_out, pair, ("send_a",), ("ctx_mate", pair))
        keep_rows(ctx_h, ctx_out, pair, "ctx_keep", pair)

    def send_rows(src, dst, pair, send, recv):
        source = slice(pair * LANES, (pair + 1) * LANES)
        remote(src.at[at(1 - core, rows), source], dst.at[:, head_cols(core, pair)], (dp, mate), send, recv)

    def keep_rows(src, dst, pair, name, index=0):
        source = slice(pair * LANES, (pair + 1) * LANES)
        local(src.at[spot, source], dst.at[:, head_cols(core, pair)], name, index)

    def send_out(src, dst, pair):
        send_rows(src, dst, pair, ("send_out",), ("outs",))
        keep_rows(src, dst, pair, "out_keep")

    def values_in(pair):
        pc = slice(pair * LANES, (pair + 1) * LANES)
        drain(w_full.at[0 : 4 * rows * LANES // (2 * channels), :], "kv", pair)
        vt[pc, block:] = flip(v_h[block:, pc]).astype(BF)

    w_sends[0].wait_send()
    w_sends[1].wait_send()
    send_kv(0)
    send_kv(1)
    w_take(x_pos, z_odd, 0, "w_y", 0, (z_dp, "w_z", 0), (x_dp, "w_x", 0))
    loads = [
        local(src, dst, "loads", t)
        for t, (src, dst) in enumerate(
            ((res_ref, res_v), (cg_ref, cg_v), (og_ref, og_v), (taps_hbm, taps_ref), (gain_hbm, gain_ref), (bias_hbm, bias_ref))
        )
    ]
    w_self = local(w_ref, w_full.at[at(me, w_rows), :], "w_self")
    w_take(x_pos, z_odd, 1, "w_y", 1, (x_dp, "w_x", 1), (z_dp, "w_z", 1))
    told(0)
    tell(1)
    drain(w_full.at[0 : 3 * rows * own // (2 * channels), :], "near")
    drain(w_full.at[0 : 3 * rows * own // (2 * channels), :], "keep")
    for pair in range(pairs):
        pc = slice(pair * LANES, (pair + 1) * LANES)
        qt[pc, 0:block] = (flip(q_h[0:block, pc]) * scaling).astype(BF)
        vt[pc, 0:block] = flip(v_h[0:block, pc]).astype(BF)
    w_take(x_pos, z_other, 0, "w_z", 0, (x_dp, "w_x", 2))
    sent_kv(0)
    send_kv(2)
    remote(w_ref, w_full.at[at(me, w_rows), :], (dp, mate), ("send_a",), ("w_mate",))
    values_in(0)
    attend(0)
    w_take(x_other, z_odd, 0, "w_x", 0)
    w_take(x_other, z_odd, 1, "w_x", 1, (z_dp, "w_z", 2))
    told(1)
    tell(2)
    sent_kv(1)
    send_kv(3)
    values_in(1)
    attend(1)
    w_take(x_pos, z_other, 1, "w_z", 1)
    w_take(x_other, z_other, 0, "w_x", 2)
    sent_kv(2)
    for pair in range(pairs):
        send_far(q_ref, q_h, pair, ("send_a",), ("q_far",))
    values_in(2)
    attend(2)
    told(2)
    w_take(x_other, z_other, 1, "w_z", 2)
    values_in(3)
    attend(3)
    stats = (dp, across)
    remote(stat_s.at[0:2], stat_r.at[0:2], stats, ("send_stats",), ("stats", 0))

    for pair in range(pairs):
        pc = slice(pair * LANES, (pair + 1) * LANES)
        kt[pc, :] = flip(k_h[:, pc]).astype(BF)
    loads[0].wait()
    w_self.wait()
    drain(w_full.at[at(mate, w_rows), :], "w_mate")
    drain(w_full.at[at(diag, w_rows), :], "w_pair")
    wide = 2 * LANES
    spans = [
        [slice(o * own + pair * LANES, o * own + (pair + 1) * LANES) for o in range(2)]
        for pair in range(pairs)
    ]

    def mix(pair):
        drain(ctx_h.at[0:rows, 0:LANES], "ctx_keep", pair)
        drain(ctx_h.at[0:rows, 0:LANES], "ctx_mate", pair)
        for n, cols in enumerate(spans[pair]):
            both = res_v[:, cols].astype(F32) + ctx_out[:, cols].astype(F32)
            mixed[:, (pair * 2 + n) * LANES : (pair * 2 + n + 1) * LANES] = both.astype(BF)

    def weigh(some, cols):
        weights = jnp.concatenate([w_full[r, cols] for pair in some for r in spans[pair]], axis=0)
        lanes = slice(some[0] * 2 * LANES, (some[-1] + 1) * 2 * LANES)
        return jnp.dot(mixed[:, lanes], weights, preferred_element_type=F32)

    early, late = range(pairs - 1), range(pairs - 1, pairs)
    for pair in early:
        mix(pair)

    def conv_first(i, carry):
        cols = at(i, 2 * wide)
        pre[:, cols] = weigh(early, cols)
        return carry

    lax.fori_loop(0, channels // wide, conv_first, 0)
    mix(pairs - 1)

    for i in range(channels // wide):
        cols = slice(i * wide, (i + 1) * wide)
        gates = slice(channels + i * wide, channels + (i + 1) * wide)
        a = (weigh(late, cols) + pre[:, cols]).astype(BF)
        b = (weigh(late, gates) + pre[:, gates]).astype(BF)
        sig = jax.nn.sigmoid(b.astype(F32))
        a_s[:, cols] = a
        sig_s[:, cols] = sig
        rounded = (a.astype(F32) * sig).astype(BF)
        glu = rounded.astype(F32)
        for half in range(2):
            lanes = slice(half * LANES, (half + 1) * LANES)
            glu_f[2 * i + half, HALO : HALO + rows, :] = glu[:, lanes]
            hs1[2 * i + half] = rounded[rows - HALO :, lanes]
        two = slice(2 * i, 2 * i + 2)

        @pl.when(me < n_seq - 1)
        def _():
            remote(hs1.at[two], hr1.at[two], (dp, me + 1), ("halo1_send",), ("halo1",))

    for copy in loads[2:]:
        copy.wait()
    span = taps - 1
    base = HALO - span

    def norm_rows(first, count, unroll):
        here = slice(first, first + count)
        zero = jnp.zeros((count, LANES), F32)

        def conv(c, total):
            lanes = at(c, LANES)
            acc = zero
            for o in range(taps):
                low = base + first + o
                acc = acc + taps_ref[o : o + 1, lanes] * glu_f[c, low : low + count, :]
            dw[c, here, :] = acc
            return total + acc

        total = lax.fori_loop(0, chunks, conv, zero)
        average = jnp.sum(total, axis=1, keepdims=True) * (1.0 / channels)

        def squares(c, total):
            centered = dw[c, here, :] - average
            return total + centered * centered

        total = lax.fori_loop(0, chunks, squares, zero, unroll=unroll)
        variance = jnp.sum(total, axis=1, keepdims=True) * (1.0 / channels)
        inverse = lax.rsqrt(variance + 1e-05)

        def norm_step(c, carry):
            s1, s2 = carry
            lanes = at(c, LANES)
            normed = (dw[c, here, :] - average) * inverse
            affine = normed * gain_ref[:, lanes] + bias_ref[:, lanes]
            sig = jax.nn.sigmoid(affine)
            conv_out[here, lanes] = (affine * sig).astype(BF)
            affine_grad = og_v[here, lanes].astype(F32) * (sig * (1.0 + affine * (1.0 - sig)))
            gain_term = jnp.sum(affine_grad * normed, axis=0, keepdims=True)
            bias_term = jnp.sum(affine_grad, axis=0, keepdims=True)
            if first == 0:
                gain_term = gain_term + part[c, taps : taps + 1, :]
                bias_term = bias_term + part[c, taps + 1 : taps + 2, :]
            part[c, taps : taps + 1, :] = gain_term
            part[c, taps + 1 : taps + 2, :] = bias_term
            normed_grad = affine_grad * gain_ref[:, lanes]
            dw[c, here, :] = normed
            ng_s[c, here, :] = normed_grad
            return s1 + normed_grad, s2 + normed_grad * normed

        s1, s2 = lax.fori_loop(0, chunks, norm_step, (zero, zero), unroll=unroll)
        m1 = jnp.sum(s1, axis=1, keepdims=True) * (1.0 / channels)
        m2 = jnp.sum(s2, axis=1, keepdims=True) * (1.0 / channels)

        def depth_grad_step(c, carry):
            grad = inverse * (ng_s[c, here, :] - m1 - dw[c, here, :] * m2)
            dg[c, here, :] = grad
            return carry

        lax.fori_loop(0, chunks, depth_grad_step, 0, unroll=unroll)

    norm_rows(HALO, rows - HALO, 2)
    @pl.when(me > 0)
    def _():
        drain(hr1, "halo1")
        glu_f[:, 0:HALO, :] = hr1[...].astype(F32)

    @pl.when(me == 0)
    def _():
        glu_f[:, 0:HALO, :] = jnp.zeros((chunks, HALO, LANES), F32)

    norm_rows(0, HALO, chunks)
    tail = dg.at[:, rows : rows + HALO, :]

    @pl.when(me > 0)
    def _():
        remote(dg.at[:, 0:HALO, :], tail, (dp, me - 1), ("halo2_send",), ("halo2",))

    def glu_back(first, count):
        def body(c, carry):
            lanes = at(c, LANES)
            gates = pl.ds(pl.multiple_of(channels + c * LANES, LANES), LANES)
            here = slice(first, first + count)
            acc = jnp.zeros((count, LANES), F32)
            for o in range(taps):
                low = first + span - o
                acc = acc + taps_ref[o : o + 1, lanes] * dg[c, low : low + count, :]
            sig = sig_s[here, lanes]
            ig_out[here, lanes] = (acc * sig).astype(BF)
            slope = acc * a_s[here, lanes].astype(F32) * sig * (1.0 - sig)
            ig_out[here, gates] = slope.astype(BF)
            return carry

        lax.fori_loop(0, chunks, body, 0)

    def tap_grad(c, carry):
        grad = dg[c, 0:rows, :]
        for o in range(taps):
            part[c, o : o + 1, :] = jnp.sum(
                grad * glu_f[c, base + o : base + o + rows, :], axis=0, keepdims=True
            )
        part[c, taps + 2 : TERM_ROWS, :] = jnp.zeros((TERM_ROWS - taps - 2, LANES), F32)
        return carry

    lax.fori_loop(0, chunks, tap_grad, 0, unroll=2)
    for d, p in enumerate(dp_peers):
        remote(part.at[p], rs_buf.at[d], (p, me), ("send_r1",), ("red1",))
    glu_back(0, rows - HALO)

    @pl.when(me < n_seq - 1)
    def _():
        drain(tail, "halo2")

    @pl.when(me == n_seq - 1)
    def _():
        tail[...] = jnp.zeros((chunks, HALO, LANES), F32)

    glu_back(rows - HALO, HALO)
    loads[1].wait()
    quad = 2 * LANES
    behind = z_pos >= line // 2

    def grad_away(half, step):
        cols = pl.ds(pl.multiple_of(half * own + step * quad, quad), quad)
        within = slice(step * quad, (step + 1) * quad)
        remote(
            rg_out.at[:, cols], g_h.at[far_spot, within], (dp, other + half),
            ("send_b",), ("grad_far", step),
        )

    for step in range(pairs // 2):
        within = slice(step * quad, (step + 1) * quad)
        for half, mine in ((core, True), (1 - core, False)):
            cols = pl.ds(pl.multiple_of(half * own + step * quad, quad), quad)
            grad = lax.dot_general(
                ig_out[...], w_full[cols, :], (((1,), (1,)), ((), ())), preferred_element_type=F32
            )
            rg_out[:, cols] = (cg_v[:, cols].astype(F32) + grad).astype(BF)
            if step == 0:
                grad_away(half, step)
            if mine:
                g_h[spot, within] = rg_out[:, cols]
            else:
                remote(
                    rg_out.at[:, cols], g_h.at[spot, within], (dp, mate), ("send_b",), ("grad_near", step)
                )

    def sum_recordings():
        drain(rs_buf, "red1")
        total = part[dp]
        for d in range(n_dp - 1):
            total = total + rs_buf[d]
        s2_buf[me] = total
        for p in peers:
            remote(s2_buf.at[me], s2_buf.at[me], (dp, p), ("send_r2",), ("red2",))

    def sum_frames():
        drain(s2_buf.at[0 : n_seq - 1], "red2")
        total = s2_buf[0]
        for s in range(1, n_seq):
            total = total + s2_buf[s]
        fin[dp] = total * (1.0 / n_dp)
        for p in dp_peers:
            remote(fin.at[dp], fin.at[dp], (p, me), ("send_r3",), ("red3",))

    def row_dots(step):
        drain(g_h.at[0:rows, 0:quad], "grad_near", step)
        stat_s[2 + step] = jnp.zeros((2 * pairs, block), F32)
        for pair in (2 * step, 2 * step + 1):
            pc = slice(pair * LANES, (pair + 1) * LANES)
            gt[pc, 0:block] = flip(g_h[0:block, pc]).astype(BF)
            for h in (2 * pair, 2 * pair + 1):
                hr = slice(h * depth, (h + 1) * depth)
                both = gt[hr, 0:block].astype(F32) * ctxt[hr, :].astype(F32)
                stat_s[2 + step, h : h + 1, :] = jnp.sum(both, axis=0, keepdims=True)
        slab = slice(2 + step, 3 + step)
        remote(stat_s.at[slab], stat_r.at[slab], stats, ("send_stats",), ("stats", 1 + step))

    row_dots(0)
    pl.when(behind)(sum_recordings)
    for half in (core, 1 - core):
        grad_away(half, pairs // 2 - 1)

    drain(w_full.at[0 : 2 * pairs * rows * LANES // (2 * channels), :], "q_far")
    drain(stat_r.at[0:2], "stats", 0)
    def far_scores(pair):
        pc = slice(pair * LANES, (pair + 1) * LANES)
        qt[pc, block:] = (flip(q_h[block:, pc]) * scaling).astype(BF)
        for h in (2 * pair, 2 * pair + 1):
            hr = slice(h * depth, (h + 1) * depth)
            p_f[h] = jnp.dot(k_h[0:block, hr], qt[hr, block:], preferred_element_type=F32)

    far_scores(0)
    for pair in range(pairs):
        if pair + 1 < pairs:
            far_scores(pair + 1)
        for h in (2 * pair, 2 * pair + 1):
            p = jnp.exp(p_f[h] - stat_r[0, h : h + 1, :]) * stat_r[1, h : h + 1, :]
            p_f[h] = p
            pb_s[h, :, block:] = p.astype(BF)

    pl.when(jnp.logical_not(behind))(sum_recordings)
    row_dots(1)
    for pair in range(pairs):
        pc = slice(pair * LANES, (pair + 1) * LANES)
        heads = (2 * pair, 2 * pair + 1)
        spots = [slice(h * depth, (h + 1) * depth) for h in heads]
        prob_grads = [
            jnp.dot(v_h[:, hr], gt[hr, 0:block], preferred_element_type=F32) for hr in spots
        ]
        for h, prob_grad in zip(heads, prob_grads):
            score_grad = (prob[h] * (prob_grad - stat_s[2 + pair // 2, h : h + 1, :]) * scaling).astype(BF)
            ds_s[h, :, 0:block] = score_grad[0:block]
            ds_f[h % 2] = score_grad[block:]
        for h, hr in zip(heads, spots):
            score_grad = jnp.concatenate([ds_s[h, :, 0:block], ds_f[h % 2]], axis=0)
            dqt[hr, :] = jnp.dot(kt[hr, :], score_grad, preferred_element_type=F32)
        dq_h[:, pc] = dqt[pc, :].T.astype(BF)
        send_out(dq_h, dq_out, pair)
        if pair == 0:
            pl.when(behind)(sum_frames)

    pl.when(jnp.logical_not(behind))(sum_frames)
    first_head = lax.broadcasted_iota(jnp.int32, (block, LANES), 1) < depth
    for pair in range(pairs):
        pc = slice(pair * LANES, (pair + 1) * LANES)
        if pair % 2 == 0:
            drain(stat_r.at[2:3], "stats", 1 + pair // 2)
            drain(g_h.at[0:block, 0:quad], "grad_far", pair // 2)
        gt[pc, block:] = flip(g_h[block:, pc]).astype(BF)
        heads = (2 * pair, 2 * pair + 1)
        spots = [slice(h * depth, (h + 1) * depth) for h in heads]
        prob_grads = [
            jnp.dot(v_h[0:block, hr], gt[hr, block:], preferred_element_type=F32) for hr in spots
        ]
        for h, prob_grad in zip(heads, prob_grads):
            score_grad = p_f[h] * (prob_grad - stat_r[2 + pair // 2, h : h + 1, :]) * scaling
            ds_s[h, :, block:] = score_grad.astype(BF)
        left = jnp.dot(pb_s[2 * pair], g_h[:, pc], preferred_element_type=F32)
        right = jnp.dot(pb_s[2 * pair + 1], g_h[:, pc], preferred_element_type=F32)
        dv_h[:, pc] = jnp.where(first_head, left, right).astype(BF)
        send_out(dv_h, dv_out, pair)
        left = jnp.dot(ds_s[2 * pair], q_h[:, pc], preferred_element_type=F32)
        right = jnp.dot(ds_s[2 * pair + 1], q_h[:, pc], preferred_element_type=F32)
        dk_h[:, pc] = jnp.where(first_head, left, right).astype(BF)
        send_out(dk_h, dk_out, pair)

    wide_rows = 2 * channels
    count = 2 * w_rows + 6 * piece + 6 * pairs * rows * LANES // wide_rows
    drain(w_full.at[0:count, :], "send_a")
    sent_kv(pairs - 1)
    drain(stat_r, "send_stats")
    drain(rs_buf, "send_r1")
    drain(s2_buf.at[0 : n_seq - 1], "send_r2")

    @pl.when(me < n_seq - 1)
    def _():
        drain(hr1, "halo1_send")

    @pl.when(me > 0)
    def _():
        drain(tail, "halo2_send")

    drain(rs_buf, "red3")
    for c in range(chunks):
        lanes = slice(c * LANES, (c + 1) * LANES)
        kg_out[:, lanes] = fin[c, 0:taps, :]
        gg_out[:, lanes] = fin[c, taps : taps + 1, :]
        bg_out[:, lanes] = fin[c, taps + 1 : taps + 2, :]
    drain(rs_buf, "send_r3")
    drain(w_full.at[0 : 3 * pairs * rows * LANES // wide_rows, :], "out_keep")
    drain(w_full.at[0 : 3 * pairs * rows * LANES // wide_rows, :], "outs")
    drain(w_full.at[0 : 3 * pairs * rows * LANES // wide_rows, :], "send_out")
    drain(w_full.at[0 : 3 * rows * own // wide_rows, :], "send_b")


def place_outputs(*refs):
    sems = refs[20]
    copies = [pltpu.make_async_copy(refs[i], refs[10 + i], sems.at[i]) for i in range(10)]
    for copy in copies:
        copy.start()
    for copy in copies:
        copy.wait()


def fused_shards(
    queries, key_vecs, value_vecs, residual_in, point_weight, context_grad, depth_kernel,
    norm_gain, norm_bias, conv_grad,
):
    n_seq = lax.axis_size("seq")
    n_dp = lax.axis_size("dp")
    rows, channels = queries.shape[1:]
    taps = depth_kernel.shape[0]
    depth = channels // HEADS
    frames = rows * n_seq
    own = channels // n_seq
    heads = own // depth
    chunks = channels // LANES
    s = jax.ShapeDtypeStruct
    vm = pltpu.VMEM
    block = s((rows, channels), BF)
    half = channels // 2
    block_rows = 2 * rows
    heads = HEADS // 2
    all_rows = vm((frames, half), BF)
    all_cols = vm((half, frames), BF)
    some_rows = vm((block_rows, half), BF)
    scratch = (
        [all_rows] * 4 + [all_cols] * 4 + [vm((half, block_rows), BF), some_rows]
        + [vm((heads, frames, block_rows), F32), vm((heads, block_rows, block_rows), F32)]
        + [vm((heads, block_rows, frames), BF)] * 2
        + [vm((half, block_rows), F32)] + [some_rows] * 3
        + [vm((2, block_rows, block_rows), BF)]
        + [vm((4, heads, block_rows), F32)] * 2
        + [
            vm((rows, channels), BF),
            vm((rows, channels), BF),
            vm((rows, channels), BF),
            vm((channels, 2 * channels), BF),
            vm((rows, 2 * channels), F32),
            vm((rows, channels), BF),
            vm((rows, channels), BF),
            vm((rows, channels), F32),
            vm((chunks, HALO + rows, LANES), F32),
            vm((chunks, rows, LANES), F32),
            vm((chunks, rows, LANES), F32),
            vm((chunks, rows + HALO, LANES), F32),
            vm((chunks, TERM_ROWS, LANES), F32),
            vm((n_dp - 1, TERM_ROWS, LANES), F32),
            vm((n_seq, TERM_ROWS, LANES), F32),
            vm((chunks, TERM_ROWS, LANES), F32),
            vm((taps, channels), F32),
            vm((1, channels), F32),
            vm((1, channels), F32),
            vm((chunks, HALO, LANES), BF),
            vm((chunks, HALO, LANES), BF),
            pltpu.SemaphoreType.DMA((sum(SEMS.values()),)),
            pltpu.SemaphoreType.REGULAR((6,)),
        ]
    )
    spec = pl.BlockSpec(memory_space=pltpu.VMEM)
    hbm = pl.BlockSpec(memory_space=pl.ANY)
    outs = pl.pallas_call(
        functools.partial(fused_kernel, (n_seq, n_dp, rows, channels, taps, depth)),
        out_shape=(
            block, block, block, block, block, s((rows, 2 * channels), BF), block,
            s((taps, channels), F32), s((1, channels), F32), s((1, channels), F32),
        ),
        in_specs=[hbm] * 10,
        out_specs=(spec,) * 10,
        scratch_shapes=scratch,
        compiler_params=pltpu.CompilerParams(
            collective_id=0, has_side_effects=True, vmem_limit_bytes=56 * 1024 * 1024
        ),
    )(
        queries[0], key_vecs[0], value_vecs[0], residual_in[0], point_weight, context_grad[0],
        depth_kernel, norm_gain[None], norm_bias[None], conv_grad[0],
    )
    outs = pl.pallas_call(
        place_outputs,
        out_shape=tuple(s(o.shape, o.dtype) for o in outs),
        in_specs=[spec] * 10,
        out_specs=(hbm,) * 10,
        scratch_shapes=[pltpu.SemaphoreType.DMA((10,))],
    )(*outs)
    return tuple(o[None] for o in outs[:7]) + (outs[7], outs[8][0], outs[9][0])


def chosen(*args):
    n_seq = lax.axis_size("seq")
    n_dp = lax.axis_size("dp")
    recs, rows, channels = args[0].shape
    fits = (
        n_seq == 4
        and recs == 1
        and rows % 128 == 0
        and channels % (LANES * n_seq) == 0
        and 2 * channels == LANES * HEADS
        and channels // LANES == n_dp
        and rows * n_seq <= 512
        and args[4].shape[0] == channels // n_seq == 2 * LANES
        and args[6].shape[0] <= 31
    )
    return fused_shards(*args) if fits else shards(*args)


def solution(mesh):
    in_specs = (
        P("dp", "seq", None),
        P("dp", "seq", None),
        P("dp", "seq", None),
        P("dp", "seq", None),
        P("seq", None),
        P("dp", "seq", None),
        P(),
        P(),
        P(),
        P("dp", "seq", None),
    )
    out_specs = (
        P("dp", "seq", None),
        P("dp", "seq", None),
        P("dp", "seq", None),
        P("dp", "seq", None),
        P("dp", "seq", None),
        P("dp", "seq", None),
        P("dp", "seq", None),
        P(),
        P(),
        P(),
    )
    return jax.shard_map(chosen, mesh=mesh, in_specs=in_specs, out_specs=out_specs, check_vma=False)
```
